32 devices in a mesh: rep: 4 (over x, core), shard: 8 (over z, y).
Axes of the slice: x: 2, y: 2, z: 4, core: 2. Of those that a mesh axis runs over, the one named last changes fastest.
Arguments:
- tokens: bfloat16 [8192, 768], P(('rep', 'shard')), may hold values from -6 to 6
- letters: bfloat16 [8192, 8, 768], P(('rep', 'shard')), may hold values from -6 to 6
- lengths: int32 [32], P(('rep', 'shard')), may hold values from 64 to 256, as said below
- counts: int32 [8192], P(('rep', 'shard')), may hold values from 1 to 8, as said below
- cot_token: bfloat16 [8192, 768], P(('rep', 'shard')), may hold values from -6 to 6
- cot_letter: bfloat16 [8192, 768], P(('rep', 'shard')), may hold values from -6 to 6
- project_weight: bfloat16 [768, 2304], P('shard'), may hold values from -0.21875 to 0.21875
- project_bias: bfloat16 [1536], P('shard'), may hold values from -1.75 to 1.75
- output_weight: bfloat16 [768, 768], P('shard'), may hold values from -1.5 to 1.5
- output_bias: bfloat16 [768], P('shard'), may hold values from -1.75 to 1.75
- first_gain: bfloat16 [768], P('shard'), may hold values from 0.5 to 1.5
- first_shift: bfloat16 [768], P('shard'), may hold values from -1.75 to 1.75
- up_weight: bfloat16 [768, 3072], P('shard'), may hold values from -0.21875 to 0.21875
- up_bias: bfloat16 [3072], P('shard'), may hold values from -1.75 to 1.75
- down_weight: bfloat16 [3072, 768], P('shard'), may hold values from -0.109375 to 0.109375
- down_bias: bfloat16 [768], P('shard'), may hold values from -1.75 to 1.75
- second_gain: bfloat16 [768], P('shard'), may hold values from 0.5 to 1.5
- second_shift: bfloat16 [768], P('shard'), may hold values from -1.75 to 1.75
- gates_input: bfloat16 [2, 768, 1152], P(None, 'shard'), may hold values from -0.21875 to 0.21875
- gates_hidden: bfloat16 [2, 384, 1152], P(None, 'shard'), may hold values from -0.3125 to 0.3125
- shift_input: bfloat16 [2, 1152], P(None, 'shard'), may hold values from -1.75 to 1.75
- shift_hidden: bfloat16 [2, 1152], P(None, 'shard'), may hold values from -1.75 to 1.75
- token_mixer: bfloat16 [768, 768], P('shard'), may hold values from -0.21875 to 0.21875
- token_offset: bfloat16 [768], P('shard'), may hold values from -1.75 to 1.75
- letter_mixer: bfloat16 [768, 768], P('shard'), may hold values from -0.21875 to 0.21875
- letter_offset: bfloat16 [768], P('shard'), may hold values from -1.75 to 1.75
- window_kernel: bfloat16 [3, 1536, 1536], P(None, 'shard'), may hold values from -0.09375 to 0.09375
- window_offset: bfloat16 [1536], P('shard'), may hold values from -1.75 to 1.75
- third_gain: bfloat16 [768], P('shard'), may hold values from 0.5 to 1.5
- third_shift: bfloat16 [768], P('shard'), may hold values from -1.75 to 1.75
- fourth_gain: bfloat16 [768], P('shard'), may hold values from 0.5 to 1.5
- fourth_shift: bfloat16 [768], P('shard'), may hold values from -1.75 to 1.75
Outputs:
- token_out: bfloat16 [8192, 768], P(('rep', 'shard'))
- letter_out: bfloat16 [8192, 768], P(('rep', 'shard'))
- tokens_grad: bfloat16 [8192, 768], P(('rep', 'shard'))
- letters_grad: bfloat16 [8192, 8, 768], P(('rep', 'shard'))
- project_weight_grad: float32 [768, 2304], P('shard')
- project_bias_grad: float32 [1536], P('shard')
- output_weight_grad: float32 [768, 768], P('shard')
- output_bias_grad: float32 [768], P('shard')
- first_gain_grad: float32 [768], P('shard')
- first_shift_grad: float32 [768], P('shard')
- up_weight_grad: float32 [768, 3072], P('shard')
- up_bias_grad: float32 [3072], P('shard')
- down_weight_grad: float32 [3072, 768], P('shard')
- down_bias_grad: float32 [768], P('shard')
- second_gain_grad: float32 [768], P('shard')
- second_shift_grad: float32 [768], P('shard')
- gates_input_grad: float32 [2, 768, 1152], P(None, 'shard')
- gates_hidden_grad: float32 [2, 384, 1152], P(None, 'shard')
- shift_input_grad: float32 [2, 1152], P(None, 'shard')
- shift_hidden_grad: float32 [2, 1152], P(None, 'shard')
- token_mixer_grad: float32 [768, 768], P('shard')
- token_offset_grad: float32 [768], P('shard')
- letter_mixer_grad: float32 [768, 768], P('shard')
- letter_offset_grad: float32 [768], P('shard')
- window_kernel_grad: float32 [3, 1536, 1536], P(None, 'shard')
- window_offset_grad: float32 [1536], P('shard')
- third_gain_grad: float32 [768], P('shard')
- third_shift_grad: float32 [768], P('shard')
- fourth_gain_grad: float32 [768], P('shard')
- fourth_shift_grad: float32 [768], P('shard')
The draws below stay inside these ranges and needn't reach their ends.
Inputs may be any that keep to these rules, and one draw needn't show every extreme that they name: `lengths`: each sequence has at least 64 valid tokens, the first ones of its slots; the first sequence is full. `counts`: A token's characters fill its first slots; the first token of all has 8. Counts are given for padded tokens too.
All inputs are finite; a program needn't handle non-finite values.
Results may differ from the reference program's by a relative error of at most 0.023.
Values may be sent and summed in bfloat16 or wider, within the bound.
No kernel may reach another device: no remote copies, remote signals or barrier semaphores. Data moves between devices by JAX's collectives and lax.ppermute only.
A program may use at most 256 MiB of HBM per device.

```python
import jax
import jax.numpy as jnp
from jax import lax

D = 768
HEADS = 12
FF = 3072
HID = 384
CHARS = 8
TOK_DEV = 256
SEQS = 32
TOKENS = 8192


def draw_lengths(key, part):
    drawn = jax.random.randint(key, (SEQS,), TOK_DEV // 4, TOK_DEV + 1)
    return jnp.where(jnp.arange(SEQS) == 0, TOK_DEV, drawn).astype(jnp.int32)


def draw_counts(key, part):
    drawn = jax.random.randint(key, (TOKENS,), 1, CHARS + 1)
    return jnp.where(jnp.arange(TOKENS) == 0, CHARS, drawn).astype(jnp.int32)


def level_of(own_key, shape, pieces, smallest, high):
    def one(axis_at, shards_of):
        heights = jax.random.uniform(jax.random.fold_in(jax.random.fold_in(own_key, 6), axis_at), (shards_of,), jnp.float32, smallest / len(pieces), high / len(pieces))
        return jnp.repeat(jnp.exp(heights), shape[axis_at] // shards_of).reshape((-1,) + (1,) * (len(shape) - axis_at - 1))

    loudness = one(*pieces[0])
    for cut in pieces[1:]:
        loudness = loudness * one(*cut)
    return loudness


def gaussian(rng, dims, scale, limit, shards=(), kind=jnp.bfloat16):
    values = scale * jax.random.normal(rng, dims, jnp.float32)
    if shards:
        values = values * level_of(rng, dims, shards, -0.22, 0.18)
    return jnp.clip(values, -limit, limit).astype(kind)


def setup_inputs(seed: int = 0) -> dict:
    seeds = jax.random.split(jax.random.key(seed), 33)
    return {
        "tokens": gaussian(seeds[0], (TOKENS, D), 1.0, 6.0, ((0, 32),)),
        "letters": gaussian(seeds[1], (TOKENS, CHARS, D), 1.0, 6.0, ((0, 32),)),
        "lengths": draw_lengths(jax.random.fold_in(seeds[32], 71), 0),
        "counts": draw_counts(jax.random.fold_in(seeds[32], 71), 0),
        "cot_token": gaussian(seeds[4], (TOKENS, D), 1.0, 6.0, ((0, 32),)),
        "cot_letter": gaussian(seeds[5], (TOKENS, D), 1.0, 6.0, ((0, 32),)),
        "project_weight": gaussian(seeds[6], (D, 3 * D), D ** -0.5, 0.21875, ((0, 8),)),
        "project_bias": gaussian(seeds[7], (2 * D,), 0.3, 1.75, ((0, 8),)),
        "output_weight": gaussian(seeds[8], (D, D), (max(D // 48, 1)) ** -0.5, 1.5, ((0, 8),)),
        "output_bias": gaussian(seeds[9], (D,), 0.3, 1.75, ((0, 8),)),
        "first_gain": jnp.clip(1.0 + 0.1 * jax.random.normal(seeds[10], (D,), jnp.float32), 0.5, 1.5).astype(jnp.bfloat16),
        "first_shift": gaussian(seeds[11], (D,), 0.3, 1.75, ((0, 8),)),
        "up_weight": gaussian(seeds[12], (D, FF), D ** -0.5, 0.21875, ((0, 8),)),
        "up_bias": gaussian(seeds[13], (FF,), 0.3, 1.75, ((0, 8),)),
        "down_weight": gaussian(seeds[14], (FF, D), FF ** -0.5, 0.109375, ((0, 8),)),
        "down_bias": gaussian(seeds[15], (D,), 0.3, 1.75, ((0, 8),)),
        "second_gain": jnp.clip(1.0 + 0.1 * jax.random.normal(seeds[16], (D,), jnp.float32), 0.5, 1.5).astype(jnp.bfloat16),
        "second_shift": gaussian(seeds[17], (D,), 0.3, 1.75, ((0, 8),)),
        "gates_input": gaussian(seeds[18], (2, D, 3 * HID), D ** -0.5, 0.21875, ((1, 8),)),
        "gates_hidden": gaussian(seeds[19], (2, HID, 3 * HID), HID ** -0.5, 0.3125, ((1, 8),)),
        "shift_input": gaussian(seeds[20], (2, 3 * HID), 0.3, 1.75, ((1, 8),)),
        "shift_hidden": gaussian(seeds[21], (2, 3 * HID), 0.3, 1.75, ((1, 8),)),
        "token_mixer": gaussian(seeds[22], (D, D), D ** -0.5, 0.21875, ((0, 8),)),
        "token_offset": gaussian(seeds[23], (D,), 0.3, 1.75, ((0, 8),)),
        "letter_mixer": gaussian(seeds[24], (D, D), D ** -0.5, 0.21875, ((0, 8),)),
        "letter_offset": gaussian(seeds[25], (D,), 0.3, 1.75, ((0, 8),)),
        "window_kernel": gaussian(seeds[26], (3, 2 * D, 2 * D), (6 * D) ** -0.5, 0.09375, ((1, 8),)),
        "window_offset": gaussian(seeds[27], (2 * D,), 0.3, 1.75, ((0, 8),)),
        "third_gain": jnp.clip(1.0 + 0.1 * jax.random.normal(seeds[28], (D,), jnp.float32), 0.5, 1.5).astype(jnp.bfloat16),
        "third_shift": gaussian(seeds[29], (D,), 0.3, 1.75, ((0, 8),)),
        "fourth_gain": jnp.clip(1.0 + 0.1 * jax.random.normal(seeds[30], (D,), jnp.float32), 0.5, 1.5).astype(jnp.bfloat16),
        "fourth_shift": gaussian(seeds[31], (D,), 0.3, 1.75, ((0, 8),)),
    }


EPS = 1e-05
PRECISE = lax.Precision.HIGHEST

@jax.custom_vjp
def low(v):
    return lax.optimization_barrier(v.astype(jnp.bfloat16)).astype(jnp.float32)

@jax.custom_vjp
def low_back(v):
    return v

def low_keep(v):
    return (low(v), None)

def low_pass(kept, grad):
    return (grad,)

def back_keep(v):
    return (v, None)

def back_low(kept, grad):
    return (low(grad),)
low.defvjp(low_keep, low_pass)
low_back.defvjp(back_keep, back_low)

def product(left, right):
    return jnp.dot(left, right, precision=PRECISE)

def normalize(values, gain, shift):
    center = lax.optimization_barrier(jnp.mean(values, axis=-1, keepdims=True))
    centered = values - center
    spread = lax.optimization_barrier(jnp.mean(centered * centered, axis=-1, keepdims=True))
    return centered * lax.rsqrt(spread + EPS) * gain + shift

def recurrent_cell(inputs, hidden_gates, carried):
    hidden_width = carried.shape[-1]
    reset = jax.nn.sigmoid(inputs[:, :hidden_width] + hidden_gates[:, :hidden_width])
    update = jax.nn.sigmoid(inputs[:, hidden_width:2 * hidden_width] + hidden_gates[:, hidden_width:2 * hidden_width])
    candidate = jnp.tanh(inputs[:, 2 * hidden_width:] + reset * hidden_gates[:, 2 * hidden_width:])
    return (1.0 - update) * candidate + update * carried

def recurrent(gate_inputs, hidden_weight, hidden_shift, letter_counts, step_order):
    carried = jnp.zeros((gate_inputs.shape[0], hidden_weight.shape[0]), jnp.float32)
    for position in step_order:
        hidden_gates = low_back(product(low(carried), hidden_weight) + hidden_shift)
        fresh = recurrent_cell(gate_inputs[:, position], hidden_gates, carried)
        carried = jnp.where((position < letter_counts)[:, None], fresh, carried)
    return carried

def forward(tokens, letters, weights, length, letter_counts):
    project_weight, project_bias, output_weight, output_bias, first_gain, first_shift, up_weight, up_bias, down_weight, down_bias, second_gain, second_shift, gates_input, gates_hidden, shift_input, shift_hidden, token_mixer, token_offset, letter_mixer, letter_offset, window_kernel, window_offset, third_gain, third_shift, fourth_gain, fourth_shift = weights
    seq_rows, model_width = tokens.shape
    head_width = model_width // HEADS
    score_scale = float(head_width) ** (-0.5)
    row_mask = (jnp.arange(seq_rows) < length).astype(jnp.float32)[:, None]
    bias_full = jnp.concatenate([project_bias[:model_width], jnp.zeros((model_width,), jnp.float32), project_bias[model_width:]])
    mixed = low(low_back(product(tokens, project_weight) + bias_full))
    queries = mixed[:, :model_width].reshape(seq_rows, HEADS, head_width)
    key_rows = mixed[:, model_width:2 * model_width].reshape(seq_rows, HEADS, head_width)
    value_rows = mixed[:, 2 * model_width:].reshape(seq_rows, HEADS, head_width)
    raw_scores = low_back(jnp.einsum('qhd,khd->hqk', queries, key_rows, precision=PRECISE) * score_scale)
    masked_scores = jnp.where(row_mask[:, 0][None, None, :] > 0.5, raw_scores, -1e+30)
    probabilities = low(jax.nn.softmax(masked_scores, axis=-1))
    context = low(low_back(jnp.einsum('hqk,khd->qhd', probabilities, value_rows, precision=PRECISE))).reshape(seq_rows, model_width)
    attended = low_back(product(context, output_weight) + output_bias)
    first = normalize(tokens + attended, first_gain, first_shift)
    upper = low_back(product(low(first), up_weight) + up_bias)
    activated = low(jax.nn.gelu(upper, approximate=False))
    lowered = low_back(product(activated, down_weight) + down_bias)
    second = normalize(first + lowered, second_gain, second_shift)
    letter_slots = letters.shape[1]
    gate_inputs = low_back(jnp.einsum('lcd,zde->zlce', letters, gates_input, precision=PRECISE) + shift_input[:, None, None, :])
    forth = recurrent(gate_inputs[0], gates_hidden[0], shift_hidden[0], letter_counts, list(range(letter_slots)))
    backward_state = recurrent(gate_inputs[1], gates_hidden[1], shift_hidden[1], letter_counts, list(range(letter_slots - 1, -1, -1)))
    pooled = jnp.concatenate([forth, backward_state], axis=-1)
    token_side = low_back(product(low(second), token_mixer) + token_offset)
    letter_side = low_back(product(low(pooled), letter_mixer) + letter_offset)
    joined = low(jnp.concatenate([token_side, letter_side], axis=-1) * row_mask)
    padded = jnp.pad(joined, ((1, 1), (0, 0)))
    convolved = low_back(product(padded[:-2], window_kernel[0]) + product(padded[1:-1], window_kernel[1]) + product(padded[2:], window_kernel[2]) + window_offset)
    widened = jax.nn.gelu(convolved, approximate=False)
    token_out = normalize(second + widened[:, :model_width], third_gain, third_shift) * row_mask
    letter_out = normalize(pooled + widened[:, model_width:], fourth_gain, fourth_shift) * row_mask
    return (token_out, letter_out)

def reference(tokens, letters, lengths, counts, cot_token, cot_letter, project_weight, project_bias, output_weight, output_bias, first_gain, first_shift, up_weight, up_bias, down_weight, down_bias, second_gain, second_shift, gates_input, gates_hidden, shift_input, shift_hidden, token_mixer, token_offset, letter_mixer, letter_offset, window_kernel, window_offset, third_gain, third_shift, fourth_gain, fourth_shift):
    weight_list = tuple((item.astype(jnp.float32) for item in (project_weight, project_bias, output_weight, output_bias, first_gain, first_shift, up_weight, up_bias, down_weight, down_bias, second_gain, second_shift, gates_input, gates_hidden, shift_input, shift_hidden, token_mixer, token_offset, letter_mixer, letter_offset, window_kernel, window_offset, third_gain, third_shift, fourth_gain, fourth_shift)))
    sequences = lengths.shape[0]
    seq_rows = tokens.shape[0] // sequences
    model_width = tokens.shape[1]
    letter_slots = letters.shape[1]
    token_blocks = tokens.astype(jnp.float32).reshape(sequences, seq_rows, model_width)
    letter_blocks = letters.astype(jnp.float32).reshape(sequences, seq_rows, letter_slots, model_width)
    count_blocks = counts.reshape(sequences, seq_rows)
    cot_tokens = cot_token.astype(jnp.float32).reshape(sequences, seq_rows, model_width)
    cot_letters = cot_letter.astype(jnp.float32).reshape(sequences, seq_rows, model_width)

    def one_sequence(summed, inputs):
        token_rows, letter_rows, length, letter_counts, cot_rows, cot_letter_rows = inputs

        def local(token_in, letter_in, weight_in):
            return forward(token_in, letter_in, weight_in, length, letter_counts)
        outputs, pullback = jax.vjp(local, token_rows, letter_rows, weight_list)
        delta_tokens, delta_letters, delta_weights = pullback((cot_rows, cot_letter_rows))
        summed = jax.tree.map(lambda left, right: left + right, summed, delta_weights)
        return (summed, (outputs[0].astype(jnp.bfloat16), outputs[1].astype(jnp.bfloat16), delta_tokens.astype(jnp.bfloat16), delta_letters.astype(jnp.bfloat16)))
    initial = jax.tree.map(jnp.zeros_like, weight_list)
    summed, emitted = lax.scan(one_sequence, initial, (token_blocks, letter_blocks, lengths, count_blocks, cot_tokens, cot_letters))
    token_out = emitted[0].reshape(sequences * seq_rows, model_width)
    letter_out = emitted[1].reshape(sequences * seq_rows, model_width)
    tokens_grad = emitted[2].reshape(sequences * seq_rows, model_width)
    letters_grad = emitted[3].reshape(sequences * seq_rows, letter_slots, model_width)
    return (token_out, letter_out, tokens_grad, letters_grad, summed[0], summed[1], summed[2], summed[3], summed[4], summed[5], summed[6], summed[7], summed[8], summed[9], summed[10], summed[11], summed[12], summed[13], summed[14], summed[15], summed[16], summed[17], summed[18], summed[19], summed[20], summed[21], summed[22], summed[23], summed[24], summed[25])
```

```python
import jax
import jax.numpy as jnp
from jax import lax
from jax.experimental import pallas as pl
from jax.experimental.pallas import tpu as pltpu
from jax.sharding import PartitionSpec as P

HEADS = 12


EPS = 1e-05


def shortened(value):
    return jax.tree.map(lambda a: a.astype(jnp.bfloat16) if a.dtype == jnp.float32 else a, value)


def product(left, right):
    return jnp.dot(left, right, preferred_element_type=jnp.float32)


def left_product(left, right):
    return lax.dot_general(
        left, right, (((0,), (0,)), ((), ())), preferred_element_type=jnp.float32
    )


def right_product(left, right):
    return lax.dot_general(
        left, right, (((1,), (1,)), ((), ())), preferred_element_type=jnp.float32
    )


def column_sum(values):
    return jnp.sum(values.astype(jnp.float32), axis=0)


def normalize(values, gain, shift):
    center = jnp.mean(values, axis=-1, keepdims=True)
    centered = values - center
    spread = jnp.mean(centered * centered, axis=-1, keepdims=True)
    return centered * lax.rsqrt(spread + EPS) * gain + shift


def exact_gelu(values):
    return jax.nn.gelu(values, approximate=False)


def recurrent_cell(inputs, hidden_gates, carried):
    hidden_width = carried.shape[-1]
    reset = jax.nn.sigmoid(inputs[:, :hidden_width] + hidden_gates[:, :hidden_width])
    update = jax.nn.sigmoid(
        inputs[:, hidden_width : 2 * hidden_width]
        + hidden_gates[:, hidden_width : 2 * hidden_width]
    )
    candidate = jnp.tanh(
        inputs[:, 2 * hidden_width :] + reset * hidden_gates[:, 2 * hidden_width :]
    )
    return (1.0 - update) * candidate + update * carried


DEPTH_SIZE = 4


class Place:
    def __init__(self):
        self.rep_size = lax.axis_size("rep")
        self.shard_size = lax.axis_size("shard")
        self.depth = DEPTH_SIZE
        self.height = self.shard_size // DEPTH_SIZE
        rep_at = lax.axis_index("rep")
        shard_at = lax.axis_index("shard")
        self.shard_at = shard_at
        self.core = rep_at % 2
        self.side = (rep_at // 2) % 2
        self.row = shard_at % self.height
        self.layer = shard_at // self.height
        self.coords = jnp.stack([self.layer, self.row, self.side, self.core]).astype(jnp.int32)

    def over_core(self, value):
        return lax.ppermute(value, "rep", [(i, i ^ 1) for i in range(self.rep_size)])

    def over_side(self, value):
        return lax.ppermute(value, "rep", [(i, i ^ 2) for i in range(self.rep_size)])

    def over_far(self, value, step):
        return lax.ppermute(
            value, "rep", [(i, (i + 4 * step) % self.rep_size) for i in range(self.rep_size)]
        )

    def over_row(self, value, step):
        return lax.ppermute(value, "shard", [(i, i ^ step) for i in range(self.shard_size)])

    def over_layer(self, value, step):
        return lax.ppermute(
            value, "shard", [(i, i ^ (step * self.height)) for i in range(self.shard_size)]
        )


def put_together(place, parts, rows, columns, split):
    depth, part_rows, half = parts[0][0][0].shape
    flat = [part for group in parts for inner in group for part in inner]
    slots = [
        (core_slot, side_slot, row_slot)
        for core_slot in range(2)
        for side_slot in range(len(parts[0]))
        for row_slot in range(len(parts[0][0]))
    ]
    height = place.height
    pieces = 2 if split else 1

    def body(coords_ref, *refs):
        ins, out_ref, sems = refs[: len(flat)], refs[len(flat)], refs[len(flat) + 1]
        layer, row, side, core = (coords_ref[i] for i in range(4))
        copies = []
        for at, (core_slot, side_slot, row_slot) in enumerate(slots):
            for layer_slot in range(depth):
                block = (layer ^ layer_slot) * height + (row ^ row_slot)
                if split:
                    block = block * 2 + (side ^ side_slot)
                column = pl.multiple_of((core ^ core_slot) * half, 128)
                copies.append(
                    pltpu.make_async_copy(
                        ins[at].at[layer_slot],
                        out_ref.at[block, :, pl.ds(column, half)],
                        sems.at[at * depth + layer_slot],
                    )
                )
        for copy in copies:
            copy.start()
        for copy in copies:
            copy.wait()

    blocks = depth * height * pieces
    whole = pl.pallas_call(
        body,
        out_shape=jax.ShapeDtypeStruct((blocks, part_rows, columns), flat[0].dtype),
        in_specs=[pl.BlockSpec(memory_space=pltpu.SMEM)]
        + [pl.BlockSpec(memory_space=pl.ANY)] * len(flat),
        out_specs=pl.BlockSpec(memory_space=pl.ANY),
        scratch_shapes=[pltpu.SemaphoreType.DMA((len(flat) * depth,))],
        name="put_together",
    )(place.coords, *flat)
    return whole.reshape(rows * place.shard_size, columns)


def gathered(place, shard, split):
    rows, columns = shard.shape
    half = columns // 2
    part_rows = rows // 2 if split else rows
    top = place.side * part_rows if split else 0
    piece = lax.dynamic_slice(shard, (top, place.core * half), (part_rows, half))
    layers = jnp.stack(
        [piece] + [place.over_layer(piece, step) for step in range(1, place.depth)]
    )
    column = [layers] + [place.over_row(layers, step) for step in range(1, place.height)]
    sides = [column]
    if split:
        sides.append([place.over_side(part) for part in column])
    cores = [sides, [[place.over_core(part) for part in group] for group in sides]]
    return put_together(place, cores, rows, columns, split)


def pick(value, at, axis):
    return lax.dynamic_index_in_dim(value, at, axis, keepdims=False)


def widen(value):
    return value.astype(jnp.float32)


def narrow(value):
    return value.astype(jnp.bfloat16)


def owned_gradient(place, inputs, delta, split):
    half = delta.shape[1] // 2

    def half_of(at):
        return left_product(inputs, lax.dynamic_slice_in_dim(delta, at * half, half, axis=1))

    return owned_sum(place, half_of, split)


def owned_hidden(place, states, deltas):
    def half_of(at):
        state = jnp.where(at == 0, states[0], states[1])
        return left_product(state, jnp.where(at == 0, deltas[0], deltas[1]))

    both = owned_sum(place, half_of, False)
    half = both.shape[1] // 2
    return jnp.stack([both[:, :half], both[:, half:]])


def owned_sum(place, half_of, split):
    sent = narrow(half_of(1 - place.core))
    other = place.over_core(sent)
    held = narrow(half_of(place.core) + widen(other))
    full_rows, half = held.shape
    rows = full_rows // place.shard_size
    part_rows = rows // 2 if split else rows
    if split:
        held = held.reshape(place.shard_size, 2, part_rows, half)
        other = place.over_side(pick(held, 1 - place.side, 1))
        held = narrow(widen(pick(held, place.side, 1)) + widen(other))
    held = held.reshape(place.depth, place.height, part_rows, half)
    total = widen(pick(held, place.row, 1))
    for step in range(1, place.height):
        total = total + widen(place.over_row(pick(held, place.row ^ step, 1), step))
    held = narrow(total)
    total = widen(pick(held, place.layer, 0))
    for step in range(1, place.depth):
        total = total + widen(place.over_layer(pick(held, place.layer ^ step, 0), step))
    held = narrow(total)
    for step in range(1, place.rep_size // 4):
        total = total + widen(place.over_far(held, step))
    held = narrow(total)
    other = place.over_side(held)
    if split:
        first = jnp.where(place.side == 0, held, other)
        last = jnp.where(place.side == 0, other, held)
        held = jnp.concatenate([first, last], axis=0)
    else:
        held = narrow(widen(held) + widen(other))
    other = place.over_core(held)
    first = jnp.where(place.core == 0, held, other)
    last = jnp.where(place.core == 0, other, held)
    return widen(jnp.concatenate([first, last], axis=1))


def gathered_vectors(place, vectors):
    flat = [v.reshape(-1) for v in vectors]
    packed = jnp.concatenate(flat)[None, :]
    layers = jnp.concatenate(
        [packed] + [place.over_layer(packed, step) for step in range(1, place.depth)], axis=0
    )
    slots = jnp.stack(
        [layers] + [place.over_row(layers, step) for step in range(1, place.height)], axis=1
    ).reshape(place.shard_size, -1)
    order = jnp.arange(place.shard_size)
    slot_of = ((order // place.height) ^ place.layer) * place.height + (
        (order % place.height) ^ place.row
    )
    ordered = jnp.take(slots, slot_of, axis=0, mode="clip").astype(jnp.float32)
    whole, start = [], 0
    for v in vectors:
        width = v.size
        part = ordered[:, start : start + width]
        if v.ndim == 1:
            whole.append(part.reshape(-1))
        else:
            lead, inner = v.shape
            whole.append(
                part.reshape(place.shard_size, lead, inner).transpose(1, 0, 2).reshape(lead, -1)
            )
        start += width
    return whole


def owned_vectors(place, vectors):
    count = place.shard_size
    rows = []
    for v in vectors:
        if v.ndim == 1:
            rows.append(v.reshape(count, -1))
        else:
            lead = v.shape[0]
            rows.append(v.reshape(lead, count, -1).transpose(1, 0, 2).reshape(count, -1))
    total = jnp.concatenate(rows, axis=1)
    total = total + place.over_core(total)
    total = total + place.over_side(total)
    base = total
    for step in range(1, place.rep_size // 4):
        total = total + place.over_far(base, step)
    span = 1
    while span < place.height:
        total = total + place.over_row(total, span)
        span *= 2
    span = 1
    while span < place.depth:
        total = total + place.over_layer(total, span)
        span *= 2
    own = lax.dynamic_index_in_dim(total, place.shard_at, 0, keepdims=False)
    parts, start = [], 0
    for v in vectors:
        width = v.size // count
        part = own[start : start + width]
        parts.append(part if v.ndim == 1 else part.reshape(v.shape[0], -1))
        start += width
    return parts


def shards(
    tokens,
    letters,
    lengths,
    counts,
    cot_token,
    cot_letter,
    project_weight,
    project_bias,
    output_weight,
    output_bias,
    first_gain,
    first_shift,
    up_weight,
    up_bias,
    down_weight,
    down_bias,
    second_gain,
    second_shift,
    gates_input,
    gates_hidden,
    shift_input,
    shift_hidden,
    token_mixer,
    token_offset,
    letter_mixer,
    letter_offset,
    window_kernel,
    window_offset,
    third_gain,
    third_shift,
    fourth_gain,
    fourth_shift,
):
    place = Place()
    seq_rows, model_width = tokens.shape
    letter_slots = letters.shape[1]
    head_width = model_width // HEADS
    score_scale = float(head_width) ** (-0.5)
    row_valid = jnp.arange(seq_rows) < lengths[0]
    row_mask = row_valid.astype(jnp.float32)[:, None]
    key_valid = row_valid[None, None, :]
    letter_flat = letters.transpose(1, 0, 2).reshape(letter_slots * seq_rows, model_width)

    (
        full_pbias,
        full_obias,
        gain_one,
        shift_one,
        full_ubias,
        full_dbias,
        gain_two,
        shift_two,
        full_sin,
        full_shid,
        full_toff,
        full_loff,
        full_koff,
        gain_three,
        shift_three,
        gain_four,
        shift_four,
    ) = gathered_vectors(
        place,
        (
            project_bias,
            output_bias,
            first_gain,
            first_shift,
            up_bias,
            down_bias,
            second_gain,
            second_shift,
            shift_input,
            shift_hidden,
            token_offset,
            letter_offset,
            window_offset,
            third_gain,
            third_shift,
            fourth_gain,
            fourth_shift,
        ),
    )
    side_by_side = lambda w: jnp.concatenate([w[i] for i in range(w.shape[0])], axis=1)
    full_project = gathered(place, project_weight, True)
    full_gin = gathered(place, side_by_side(gates_input), True)
    full_ghid = gathered(place, side_by_side(gates_hidden), False)
    full_output = gathered(place, output_weight, False)
    full_up = gathered(place, up_weight, False)
    full_down = gathered(place, down_weight, False)
    full_tmix = gathered(place, token_mixer, False)
    full_lmix = gathered(place, letter_mixer, False)
    full_kernel = gathered(place, side_by_side(window_kernel), True)

    bias_full = jnp.concatenate(
        [full_pbias[:model_width], jnp.zeros((model_width,), jnp.float32), full_pbias[model_width:]]
    )
    mixed = (product(tokens, full_project) + bias_full).astype(jnp.bfloat16)
    queries = mixed[:, :model_width].reshape(seq_rows, HEADS, head_width)
    key_rows = mixed[:, model_width : 2 * model_width].reshape(seq_rows, HEADS, head_width)
    value_rows = mixed[:, 2 * model_width :].reshape(seq_rows, HEADS, head_width)

    def masked_scores_of(query_part, key_part):
        raw_scores = (
            jnp.einsum("qhd,khd->hqk", query_part, key_part, preferred_element_type=jnp.float32)
            * score_scale
        )
        return jnp.where(key_valid, raw_scores, -1e30)

    masked_scores = masked_scores_of(queries, key_rows)
    row_peak = jnp.max(masked_scores, axis=-1, keepdims=True)
    log_total = row_peak + jnp.log(
        jnp.sum(jnp.exp(masked_scores - row_peak), axis=-1, keepdims=True)
    )
    probs_low = jnp.exp(masked_scores - log_total).astype(jnp.bfloat16)
    context = (
        jnp.einsum("hqk,khd->qhd", probs_low, value_rows, preferred_element_type=jnp.float32)
        .astype(jnp.bfloat16)
        .reshape(seq_rows, model_width)
    )
    attended = product(context, full_output) + full_obias
    residual_one = tokens.astype(jnp.float32) + attended
    first = normalize(residual_one, gain_one, shift_one)
    first_low = first.astype(jnp.bfloat16)
    upper = product(first_low, full_up) + full_ubias
    activated = exact_gelu(upper).astype(jnp.bfloat16)
    residual_two = first + product(activated, full_down) + full_dbias
    second = normalize(residual_two, gain_two, shift_two)
    hidden_width = full_ghid.shape[0]
    gates_width = 3 * hidden_width
    forward_order = list(range(letter_slots))
    reverse_order = list(range(letter_slots - 1, -1, -1))
    ghid_of = [full_ghid[:, d * gates_width : (d + 1) * gates_width] for d in range(2)]
    gin_of = [full_gin[:, d * gates_width : (d + 1) * gates_width] for d in range(2)]

    def run_direction(direction, step_order):
        gate_inputs = (product(letter_flat, gin_of[direction]) + full_sin[direction]).reshape(
            letter_slots, seq_rows, gates_width
        )
        carried = jnp.zeros((seq_rows, hidden_width), jnp.float32)
        saved_states = []
        for position in step_order:
            saved_states.append(carried)
            hidden_gates = product(carried.astype(jnp.bfloat16), ghid_of[direction]) + full_shid[
                direction
            ]
            fresh = recurrent_cell(gate_inputs[position], hidden_gates, carried)
            carried = jnp.where((position < counts)[:, None], fresh, carried)
        return (carried, gate_inputs, saved_states)

    forth_state, forth_inputs, forth_saved = run_direction(0, forward_order)
    back_state, back_inputs, back_saved = run_direction(1, reverse_order)
    pooled = jnp.concatenate([forth_state, back_state], axis=-1)
    second_low = second.astype(jnp.bfloat16)
    pooled_low = pooled.astype(jnp.bfloat16)
    token_side = product(second_low, full_tmix) + full_toff
    letter_side = product(pooled_low, full_lmix) + full_loff
    joined = (jnp.concatenate([token_side, letter_side], axis=-1) * row_mask).astype(jnp.bfloat16)
    joined_width = joined.shape[1]
    taps = product(joined, full_kernel)
    convolved = (
        jnp.pad(taps[:-1, :joined_width], ((1, 0), (0, 0)))
        + taps[:, joined_width : 2 * joined_width]
        + jnp.pad(taps[1:, 2 * joined_width :], ((0, 1), (0, 0)))
        + full_koff
    )
    widened = exact_gelu(convolved)
    residual_three = second + widened[:, :model_width]
    residual_four = pooled + widened[:, model_width:]
    token_out = normalize(residual_three, gain_three, shift_three) * row_mask
    letter_out = normalize(residual_four, gain_four, shift_four) * row_mask

    out_token_delta = cot_token.astype(jnp.float32) * row_mask
    out_letter_delta = cot_letter.astype(jnp.float32) * row_mask
    unused_three, pull_three = jax.vjp(normalize, residual_three, gain_three, shift_three)
    delta_three, delta_gain_three, delta_shift_three = pull_three(out_token_delta)
    unused_four, pull_four = jax.vjp(normalize, residual_four, gain_four, shift_four)
    delta_four, delta_gain_four, delta_shift_four = pull_four(out_letter_delta)
    unused_gelu, pull_gelu = jax.vjp(exact_gelu, convolved)
    delta_conv = pull_gelu(jnp.concatenate([delta_three, delta_four], axis=-1))[0].astype(
        jnp.bfloat16
    )
    delta_koff = column_sum(delta_conv)
    delta_taps = jnp.concatenate(
        [
            jnp.pad(delta_conv[1:], ((0, 1), (0, 0))),
            delta_conv,
            jnp.pad(delta_conv[:-1], ((1, 0), (0, 0))),
        ],
        axis=1,
    )
    kernel_grad = owned_gradient(place, joined, delta_taps, True)
    delta_joined = right_product(delta_taps, full_kernel) * row_mask
    delta_tside = delta_joined[:, :model_width].astype(jnp.bfloat16)
    delta_lside = delta_joined[:, model_width:].astype(jnp.bfloat16)
    tmix_grad = owned_gradient(place, second_low, delta_tside, False)
    delta_toff = column_sum(delta_tside)
    lmix_grad = owned_gradient(place, pooled_low, delta_lside, False)
    delta_loff = column_sum(delta_lside)
    delta_second = delta_three + right_product(delta_tside, full_tmix)
    delta_pooled = delta_four + right_product(delta_lside, full_lmix)

    def back_direction(direction, step_order, gate_inputs, saved_states, delta_carried):
        delta_inputs = [None] * letter_slots
        delta_gate_list = [None] * letter_slots
        state_list = [None] * letter_slots
        delta_hshift = jnp.zeros((gates_width,), jnp.float32)
        for turn in range(letter_slots - 1, -1, -1):
            position = step_order[turn]
            carried = saved_states[turn]
            active = (position < counts)[:, None]
            carried_low = carried.astype(jnp.bfloat16)
            hidden_gates = product(carried_low, ghid_of[direction]) + full_shid[direction]
            unused_cell, pullback = jax.vjp(
                recurrent_cell, gate_inputs[position], hidden_gates, carried
            )
            delta_in, delta_gates, delta_direct = pullback(jnp.where(active, delta_carried, 0.0))
            gates_low = delta_gates.astype(jnp.bfloat16)
            delta_hshift = delta_hshift + column_sum(gates_low)
            delta_carried = (
                jnp.where(active, 0.0, delta_carried)
                + delta_direct
                + right_product(gates_low, ghid_of[direction])
            )
            delta_inputs[position] = delta_in.astype(jnp.bfloat16)
            delta_gate_list[turn] = gates_low
            state_list[turn] = carried_low
        inputs_low = jnp.concatenate(delta_inputs, axis=0)
        return (
            inputs_low,
            column_sum(inputs_low),
            jnp.concatenate(state_list, axis=0),
            jnp.concatenate(delta_gate_list, axis=0),
            delta_hshift,
        )

    forth_back = back_direction(
        0, forward_order, forth_inputs, forth_saved, delta_pooled[:, :hidden_width]
    )
    back_back = back_direction(
        1, reverse_order, back_inputs, back_saved, delta_pooled[:, hidden_width:]
    )
    gates_low = jnp.concatenate([forth_back[0], back_back[0]], axis=1)
    letters_grad = (
        right_product(gates_low, full_gin)
        .astype(jnp.bfloat16)
        .reshape(letter_slots, seq_rows, model_width)
        .transpose(1, 0, 2)
    )
    gin_grad = owned_gradient(place, letter_flat, gates_low, True)
    gin_grad = jnp.stack([gin_grad[:, :gates_width], gin_grad[:, gates_width:]])
    sin_delta = jnp.stack([forth_back[1], back_back[1]])
    shid_delta = jnp.stack([forth_back[4], back_back[4]])
    ghid_grad = owned_hidden(
        place, (forth_back[2], back_back[2]), (forth_back[3], back_back[3])
    )

    unused_two, pull_two = jax.vjp(normalize, residual_two, gain_two, shift_two)
    delta_two, delta_gain_two, delta_shift_two = pull_two(delta_second)
    delta_lowered = delta_two.astype(jnp.bfloat16)
    down_grad = owned_gradient(place, activated, delta_lowered, False)
    delta_dbias = column_sum(delta_lowered)
    unused_act, pull_act = jax.vjp(exact_gelu, upper)
    delta_upper = pull_act(right_product(delta_lowered, full_down))[0].astype(jnp.bfloat16)
    up_grad = owned_gradient(place, first_low, delta_upper, False)
    delta_ubias = column_sum(delta_upper)
    delta_first = delta_two + right_product(delta_upper, full_up)
    unused_one, pull_one = jax.vjp(normalize, residual_one, gain_one, shift_one)
    delta_one, delta_gain_one, delta_shift_one = pull_one(delta_first)
    delta_attended = delta_one.astype(jnp.bfloat16)
    output_grad = owned_gradient(place, context, delta_attended, False)
    delta_obias = column_sum(delta_attended)
    delta_context = (
        right_product(delta_attended, full_output)
        .astype(jnp.bfloat16)
        .reshape(seq_rows, HEADS, head_width)
    )
    probabilities = jnp.exp(masked_scores_of(queries, key_rows) - log_total)
    delta_values = jnp.einsum(
        "hqk,qhd->khd",
        probabilities.astype(jnp.bfloat16),
        delta_context,
        preferred_element_type=jnp.float32,
    )
    delta_probs = jnp.einsum(
        "qhd,khd->hqk", delta_context, value_rows, preferred_element_type=jnp.float32
    )
    delta_scores = (
        probabilities * (delta_probs - jnp.sum(probabilities * delta_probs, axis=-1, keepdims=True))
    ).astype(jnp.bfloat16)
    delta_queries = (
        jnp.einsum("hqk,khd->qhd", delta_scores, key_rows, preferred_element_type=jnp.float32)
        * score_scale
    )
    delta_keys = (
        jnp.einsum("hqk,qhd->khd", delta_scores, queries, preferred_element_type=jnp.float32)
        * score_scale
    )
    delta_mixed = jnp.concatenate(
        [
            delta_queries.reshape(seq_rows, model_width),
            delta_keys.reshape(seq_rows, model_width),
            delta_values.reshape(seq_rows, model_width),
        ],
        axis=-1,
    ).astype(jnp.bfloat16)
    project_grad = owned_gradient(place, tokens, delta_mixed, True)
    delta_mixed_sum = column_sum(delta_mixed)
    delta_pbias = jnp.concatenate(
        [delta_mixed_sum[:model_width], delta_mixed_sum[2 * model_width :]]
    )
    tokens_grad = (delta_one + right_product(delta_mixed, full_project)).astype(jnp.bfloat16)
    (
        pbias_grad,
        obias_grad,
        gain_one_grad,
        shift_one_grad,
        ubias_grad,
        dbias_grad,
        gain_two_grad,
        shift_two_grad,
        sin_grad,
        shid_grad,
        toff_grad,
        loff_grad,
        koff_grad,
        gain_three_grad,
        shift_three_grad,
        gain_four_grad,
        shift_four_grad,
    ) = owned_vectors(
        place,
        (
            delta_pbias,
            delta_obias,
            delta_gain_one,
            delta_shift_one,
            delta_ubias,
            delta_dbias,
            delta_gain_two,
            delta_shift_two,
            sin_delta,
            shid_delta,
            delta_toff,
            delta_loff,
            delta_koff,
            delta_gain_three,
            delta_shift_three,
            delta_gain_four,
            delta_shift_four,
        ),
    )
    taps_grad = jnp.stack(
        [kernel_grad[:, t * joined_width : (t + 1) * joined_width] for t in range(3)]
    )
    return (
        token_out.astype(jnp.bfloat16),
        letter_out.astype(jnp.bfloat16),
        tokens_grad,
        letters_grad,
        project_grad,
        pbias_grad,
        output_grad,
        obias_grad,
        gain_one_grad,
        shift_one_grad,
        up_grad,
        ubias_grad,
        down_grad,
        dbias_grad,
        gain_two_grad,
        shift_two_grad,
        gin_grad,
        ghid_grad,
        sin_grad,
        shid_grad,
        tmix_grad,
        toff_grad,
        lmix_grad,
        loff_grad,
        taps_grad,
        koff_grad,
        gain_three_grad,
        shift_three_grad,
        gain_four_grad,
        shift_four_grad,
    )


def solution(mesh):
    placed = (
        P(("rep", "shard"), None),
        P(("rep", "shard"), None, None),
        P(("rep", "shard")),
        P(("rep", "shard")),
        P(("rep", "shard"), None),
        P(("rep", "shard"), None),
        P("shard", None),
        P("shard"),
        P("shard", None),
        P("shard"),
        P("shard"),
        P("shard"),
        P("shard", None),
        P("shard"),
        P("shard", None),
        P("shard"),
        P("shard"),
        P("shard"),
        P(None, "shard", None),
        P(None, "shard", None),
        P(None, "shard"),
        P(None, "shard"),
        P("shard", None),
        P("shard"),
        P("shard", None),
        P("shard"),
        P(None, "shard", None),
        P("shard"),
        P("shard"),
        P("shard"),
        P("shard"),
        P("shard"),
    )
    return jax.shard_map(
        shards,
        mesh=mesh,
        in_specs=placed,
        out_specs=(
            P(("rep", "shard"), None),
            P(("rep", "shard"), None),
            P(("rep", "shard"), None),
            P(("rep", "shard"), None, None),
            P("shard", None),
            P("shard"),
            P("shard", None),
            P("shard"),
            P("shard"),
            P("shard"),
            P("shard", None),
            P("shard"),
            P("shard", None),
            P("shard"),
            P("shard"),
            P("shard"),
            P(None, "shard", None),
            P(None, "shard", None),
            P(None, "shard"),
            P(None, "shard"),
            P("shard", None),
            P("shard"),
            P("shard", None),
            P("shard"),
            P(None, "shard", None),
            P("shard"),
            P("shard"),
            P("shard"),
            P("shard"),
            P("shard"),
        ),
        check_vma=False,
    )
```

```python
import jax
import jax.numpy as jnp
from jax import lax
from jax.experimental import pallas as pl
from jax.experimental.pallas import tpu as pltpu
from jax.sharding import PartitionSpec as P

HEADS = 12


EPS = 1e-05


def shortened(value):
    return jax.tree.map(lambda a: a.astype(jnp.bfloat16) if a.dtype == jnp.float32 else a, value)


def product(left, right):
    return jnp.dot(left, right, preferred_element_type=jnp.float32)


def left_product(left, right):
    return lax.dot_general(
        left, right, (((0,), (0,)), ((), ())), preferred_element_type=jnp.float32
    )


def right_product(left, right):
    return lax.dot_general(
        left, right, (((1,), (1,)), ((), ())), preferred_element_type=jnp.float32
    )


def column_sum(values):
    return jnp.sum(values.astype(jnp.float32), axis=0)


def normalize(values, gain, shift):
    center = jnp.mean(values, axis=-1, keepdims=True)
    centered = values - center
    spread = jnp.mean(centered * centered, axis=-1, keepdims=True)
    return centered * lax.rsqrt(spread + EPS) * gain + shift


def exact_gelu(values):
    return jax.nn.gelu(values, approximate=False)


def recurrent_cell(inputs, hidden_gates, carried):
    hidden_width = carried.shape[-1]
    reset = jax.nn.sigmoid(inputs[:, :hidden_width] + hidden_gates[:, :hidden_width])
    update = jax.nn.sigmoid(
        inputs[:, hidden_width : 2 * hidden_width]
        + hidden_gates[:, hidden_width : 2 * hidden_width]
    )
    candidate = jnp.tanh(
        inputs[:, 2 * hidden_width :] + reset * hidden_gates[:, 2 * hidden_width :]
    )
    return (1.0 - update) * candidate + update * carried


DEPTH_SIZE = 4


class Place:
    def __init__(self):
        self.rep_size = lax.axis_size("rep")
        self.shard_size = lax.axis_size("shard")
        self.depth = DEPTH_SIZE
        self.height = self.shard_size // DEPTH_SIZE
        rep_at = lax.axis_index("rep")
        shard_at = lax.axis_index("shard")
        self.shard_at = shard_at
        self.core = rep_at % 2
        self.side = (rep_at // 2) % 2
        self.row = shard_at % self.height
        self.layer = shard_at // self.height
        self.coords = jnp.stack([self.layer, self.row, self.side, self.core]).astype(jnp.int32)

    def over_core(self, value):
        return lax.ppermute(value, "rep", [(i, i ^ 1) for i in range(self.rep_size)])

    def over_side(self, value):
        return lax.ppermute(value, "rep", [(i, i ^ 2) for i in range(self.rep_size)])

    def over_far(self, value, step):
        return lax.ppermute(
            value, "rep", [(i, (i + 4 * step) % self.rep_size) for i in range(self.rep_size)]
        )

    def over_row(self, value, step):
        return lax.ppermute(value, "shard", [(i, i ^ step) for i in range(self.shard_size)])

    def over_layer(self, value, step):
        return lax.ppermute(
            value, "shard", [(i, i ^ (step * self.height)) for i in range(self.shard_size)]
        )


def put_together(place, parts, rows, columns, split):
    depth, part_rows, half = parts[0][0][0].shape
    flat = [part for group in parts for inner in group for part in inner]
    slots = [
        (core_slot, side_slot, row_slot)
        for core_slot in range(2)
        for side_slot in range(len(parts[0]))
        for row_slot in range(len(parts[0][0]))
    ]
    height = place.height
    pieces = 2 if split else 1

    def body(coords_ref, *refs):
        ins, out_ref, sems = refs[: len(flat)], refs[len(flat)], refs[len(flat) + 1]
        layer, row, side, core = (coords_ref[i] for i in range(4))
        copies = []
        for at, (core_slot, side_slot, row_slot) in enumerate(slots):
            for layer_slot in range(depth):
                block = (layer ^ layer_slot) * height + (row ^ row_slot)
                if split:
                    block = block * 2 + (side ^ side_slot)
                column = pl.multiple_of((core ^ core_slot) * half, 128)
                copies.append(
                    pltpu.make_async_copy(
                        ins[at].at[layer_slot],
                        out_ref.at[block, :, pl.ds(column, half)],
                        sems.at[at * depth + layer_slot],
                    )
                )
        for copy in copies:
            copy.start()
        for copy in copies:
            copy.wait()

    blocks = depth * height * pieces
    whole = pl.pallas_call(
        body,
        out_shape=jax.ShapeDtypeStruct((blocks, part_rows, columns), flat[0].dtype),
        in_specs=[pl.BlockSpec(memory_space=pltpu.SMEM)]
        + [pl.BlockSpec(memory_space=pl.ANY)] * len(flat),
        out_specs=pl.BlockSpec(memory_space=pltpu.VMEM),
        scratch_shapes=[pltpu.SemaphoreType.DMA((len(flat) * depth,))],
        name="put_together",
    )(place.coords, *flat)
    return whole.reshape(rows * place.shard_size, columns)


def gathered(place, shard, split):
    rows, columns = shard.shape
    half = columns // 2
    part_rows = rows // 2 if split else rows
    top = place.side * part_rows if split else 0
    piece = lax.dynamic_slice(shard, (top, place.core * half), (part_rows, half))
    layers = jnp.stack(
        [piece] + [place.over_layer(piece, step) for step in range(1, place.depth)]
    )
    column = [layers] + [place.over_row(layers, step) for step in range(1, place.height)]
    sides = [column]
    if split:
        sides.append([place.over_side(part) for part in column])
    cores = [sides, [[place.over_core(part) for part in group] for group in sides]]
    return put_together(place, cores, rows, columns, split)


def pick(value, at, axis):
    return lax.dynamic_index_in_dim(value, at, axis, keepdims=False)


def widen(value):
    return value.astype(jnp.float32)


def narrow(value):
    return value.astype(jnp.bfloat16)


def owned_gradient(place, inputs, delta, split):
    half = delta.shape[1] // 2

    def half_of(at):
        return left_product(inputs, lax.dynamic_slice_in_dim(delta, at * half, half, axis=1))

    return owned_sum(place, half_of, split)


def owned_hidden(place, states, deltas):
    def half_of(at):
        state = jnp.where(at == 0, states[0], states[1])
        return left_product(state, jnp.where(at == 0, deltas[0], deltas[1]))

    both = owned_sum(place, half_of, False)
    half = both.shape[1] // 2
    return jnp.stack([both[:, :half], both[:, half:]])


def owned_sum(place, half_of, split):
    sent = narrow(half_of(1 - place.core))
    other = place.over_core(sent)
    held = narrow(half_of(place.core) + widen(other))
    full_rows, half = held.shape
    rows = full_rows // place.shard_size
    part_rows = rows // 2 if split else rows
    if split:
        held = held.reshape(place.shard_size, 2, part_rows, half)
        other = place.over_side(pick(held, 1 - place.side, 1))
        held = narrow(widen(pick(held, place.side, 1)) + widen(other))
    held = held.reshape(place.depth, place.height, part_rows, half)
    total = widen(pick(held, place.row, 1))
    for step in range(1, place.height):
        total = total + widen(place.over_row(pick(held, place.row ^ step, 1), step))
    held = narrow(total)
    total = widen(pick(held, place.layer, 0))
    for step in range(1, place.depth):
        total = total + widen(place.over_layer(pick(held, place.layer ^ step, 0), step))
    held = narrow(total)
    for step in range(1, place.rep_size // 4):
        total = total + widen(place.over_far(held, step))
    held = narrow(total)
    other = place.over_side(held)
    if split:
        first = jnp.where(place.side == 0, held, other)
        last = jnp.where(place.side == 0, other, held)
        held = jnp.concatenate([first, last], axis=0)
    else:
        held = narrow(widen(held) + widen(other))
    other = place.over_core(held)
    first = jnp.where(place.core == 0, held, other)
    last = jnp.where(place.core == 0, other, held)
    return widen(jnp.concatenate([first, last], axis=1))


def gathered_vectors(place, vectors):
    flat = [v.reshape(-1) for v in vectors]
    packed = jnp.concatenate(flat)[None, :]
    layers = jnp.concatenate(
        [packed] + [place.over_layer(packed, step) for step in range(1, place.depth)], axis=0
    )
    slots = jnp.stack(
        [layers] + [place.over_row(layers, step) for step in range(1, place.height)], axis=1
    ).reshape(place.shard_size, -1)
    order = jnp.arange(place.shard_size)
    slot_of = ((order // place.height) ^ place.layer) * place.height + (
        (order % place.height) ^ place.row
    )
    ordered = jnp.take(slots, slot_of, axis=0, mode="clip").astype(jnp.float32)
    whole, start = [], 0
    for v in vectors:
        width = v.size
        part = ordered[:, start : start + width]
        if v.ndim == 1:
            whole.append(part.reshape(-1))
        else:
            lead, inner = v.shape
            whole.append(
                part.reshape(place.shard_size, lead, inner).transpose(1, 0, 2).reshape(lead, -1)
            )
        start += width
    return whole


def owned_vectors(place, vectors):
    count = place.shard_size
    rows = []
    for v in vectors:
        if v.ndim == 1:
            rows.append(v.reshape(count, -1))
        else:
            lead = v.shape[0]
            rows.append(v.reshape(lead, count, -1).transpose(1, 0, 2).reshape(count, -1))
    total = jnp.concatenate(rows, axis=1)
    total = total + place.over_core(total)
    total = total + place.over_side(total)
    base = total
    for step in range(1, place.rep_size // 4):
        total = total + place.over_far(base, step)
    span = 1
    while span < place.height:
        total = total + place.over_row(total, span)
        span *= 2
    span = 1
    while span < place.depth:
        total = total + place.over_layer(total, span)
        span *= 2
    own = lax.dynamic_index_in_dim(total, place.shard_at, 0, keepdims=False)
    parts, start = [], 0
    for v in vectors:
        width = v.size // count
        part = own[start : start + width]
        parts.append(part if v.ndim == 1 else part.reshape(v.shape[0], -1))
        start += width
    return parts


def shards(
    tokens,
    letters,
    lengths,
    counts,
    cot_token,
    cot_letter,
    project_weight,
    project_bias,
    output_weight,
    output_bias,
    first_gain,
    first_shift,
    up_weight,
    up_bias,
    down_weight,
    down_bias,
    second_gain,
    second_shift,
    gates_input,
    gates_hidden,
    shift_input,
    shift_hidden,
    token_mixer,
    token_offset,
    letter_mixer,
    letter_offset,
    window_kernel,
    window_offset,
    third_gain,
    third_shift,
    fourth_gain,
    fourth_shift,
):
    place = Place()
    seq_rows, model_width = tokens.shape
    letter_slots = letters.shape[1]
    head_width = model_width // HEADS
    score_scale = float(head_width) ** (-0.5)
    row_valid = jnp.arange(seq_rows) < lengths[0]
    row_mask = row_valid.astype(jnp.float32)[:, None]
    key_valid = row_valid[None, None, :]
    letter_flat = letters.transpose(1, 0, 2).reshape(letter_slots * seq_rows, model_width)

    (
        full_pbias,
        full_obias,
        gain_one,
        shift_one,
        full_ubias,
        full_dbias,
        gain_two,
        shift_two,
        full_sin,
        full_shid,
        full_toff,
        full_loff,
        full_koff,
        gain_three,
        shift_three,
        gain_four,
        shift_four,
    ) = gathered_vectors(
        place,
        (
            project_bias,
            output_bias,
            first_gain,
            first_shift,
            up_bias,
            down_bias,
            second_gain,
            second_shift,
            shift_input,
            shift_hidden,
            token_offset,
            letter_offset,
            window_offset,
            third_gain,
            third_shift,
            fourth_gain,
            fourth_shift,
        ),
    )
    side_by_side = lambda w: jnp.concatenate([w[i] for i in range(w.shape[0])], axis=1)
    full_project = gathered(place, project_weight, True)
    full_gin = gathered(place, side_by_side(gates_input), True)
    full_ghid = gathered(place, side_by_side(gates_hidden), False)
    full_output = gathered(place, output_weight, False)
    full_up = gathered(place, up_weight, False)
    full_down = gathered(place, down_weight, False)
    full_tmix = gathered(place, token_mixer, False)
    full_lmix = gathered(place, letter_mixer, False)
    full_kernel = gathered(place, side_by_side(window_kernel), True)

    bias_full = jnp.concatenate(
        [full_pbias[:model_width], jnp.zeros((model_width,), jnp.float32), full_pbias[model_width:]]
    )
    mixed = (product(tokens, full_project) + bias_full).astype(jnp.bfloat16)
    queries = mixed[:, :model_width].reshape(seq_rows, HEADS, head_width)
    key_rows = mixed[:, model_width : 2 * model_width].reshape(seq_rows, HEADS, head_width)
    value_rows = mixed[:, 2 * model_width :].reshape(seq_rows, HEADS, head_width)

    def masked_scores_of(query_part, key_part):
        raw_scores = (
            jnp.einsum("qhd,khd->hqk", query_part, key_part, preferred_element_type=jnp.float32)
            * score_scale
        )
        return jnp.where(key_valid, raw_scores, -1e30)

    masked_scores = masked_scores_of(queries, key_rows)
    row_peak = jnp.max(masked_scores, axis=-1, keepdims=True)
    log_total = row_peak + jnp.log(
        jnp.sum(jnp.exp(masked_scores - row_peak), axis=-1, keepdims=True)
    )
    probs_low = jnp.exp(masked_scores - log_total).astype(jnp.bfloat16)
    context = (
        jnp.einsum("hqk,khd->qhd", probs_low, value_rows, preferred_element_type=jnp.float32)
        .astype(jnp.bfloat16)
        .reshape(seq_rows, model_width)
    )
    attended = product(context, full_output) + full_obias
    residual_one = tokens.astype(jnp.float32) + attended
    first = normalize(residual_one, gain_one, shift_one)
    first_low = first.astype(jnp.bfloat16)
    upper = product(first_low, full_up) + full_ubias
    activated = exact_gelu(upper).astype(jnp.bfloat16)
    residual_two = first + product(activated, full_down) + full_dbias
    second = normalize(residual_two, gain_two, shift_two)
    hidden_width = full_ghid.shape[0]
    gates_width = 3 * hidden_width
    forward_order = list(range(letter_slots))
    reverse_order = list(range(letter_slots - 1, -1, -1))
    ghid_of = [full_ghid[:, d * gates_width : (d + 1) * gates_width] for d in range(2)]
    gin_of = [full_gin[:, d * gates_width : (d + 1) * gates_width] for d in range(2)]

    def run_direction(direction, step_order):
        gate_inputs = (product(letter_flat, gin_of[direction]) + full_sin[direction]).reshape(
            letter_slots, seq_rows, gates_width
        )
        carried = jnp.zeros((seq_rows, hidden_width), jnp.float32)
        saved_states = []
        for position in step_order:
            saved_states.append(carried)
            hidden_gates = product(carried.astype(jnp.bfloat16), ghid_of[direction]) + full_shid[
                direction
            ]
            fresh = recurrent_cell(gate_inputs[position], hidden_gates, carried)
            carried = jnp.where((position < counts)[:, None], fresh, carried)
        return (carried, gate_inputs, saved_states)

    forth_state, forth_inputs, forth_saved = run_direction(0, forward_order)
    back_state, back_inputs, back_saved = run_direction(1, reverse_order)
    pooled = jnp.concatenate([forth_state, back_state], axis=-1)
    second_low = second.astype(jnp.bfloat16)
    pooled_low = pooled.astype(jnp.bfloat16)
    token_side = product(second_low, full_tmix) + full_toff
    letter_side = product(pooled_low, full_lmix) + full_loff
    joined = (jnp.concatenate([token_side, letter_side], axis=-1) * row_mask).astype(jnp.bfloat16)
    joined_width = joined.shape[1]
    taps = product(joined, full_kernel)
    convolved = (
        jnp.pad(taps[:-1, :joined_width], ((1, 0), (0, 0)))
        + taps[:, joined_width : 2 * joined_width]
        + jnp.pad(taps[1:, 2 * joined_width :], ((0, 1), (0, 0)))
        + full_koff
    )
    widened = exact_gelu(convolved)
    residual_three = second + widened[:, :model_width]
    residual_four = pooled + widened[:, model_width:]
    token_out = normalize(residual_three, gain_three, shift_three) * row_mask
    letter_out = normalize(residual_four, gain_four, shift_four) * row_mask

    out_token_delta = cot_token.astype(jnp.float32) * row_mask
    out_letter_delta = cot_letter.astype(jnp.float32) * row_mask
    unused_three, pull_three = jax.vjp(normalize, residual_three, gain_three, shift_three)
    delta_three, delta_gain_three, delta_shift_three = pull_three(out_token_delta)
    unused_four, pull_four = jax.vjp(normalize, residual_four, gain_four, shift_four)
    delta_four, delta_gain_four, delta_shift_four = pull_four(out_letter_delta)
    unused_gelu, pull_gelu = jax.vjp(exact_gelu, convolved)
    delta_conv = pull_gelu(jnp.concatenate([delta_three, delta_four], axis=-1))[0].astype(
        jnp.bfloat16
    )
    delta_koff = column_sum(delta_conv)
    delta_taps = jnp.concatenate(
        [
            jnp.pad(delta_conv[1:], ((0, 1), (0, 0))),
            delta_conv,
            jnp.pad(delta_conv[:-1], ((1, 0), (0, 0))),
        ],
        axis=1,
    )
    kernel_grad = owned_gradient(place, joined, delta_taps, True)
    delta_joined = right_product(delta_taps, full_kernel) * row_mask
    delta_tside = delta_joined[:, :model_width].astype(jnp.bfloat16)
    delta_lside = delta_joined[:, model_width:].astype(jnp.bfloat16)
    tmix_grad = owned_gradient(place, second_low, delta_tside, False)
    delta_toff = column_sum(delta_tside)
    lmix_grad = owned_gradient(place, pooled_low, delta_lside, False)
    delta_loff = column_sum(delta_lside)
    delta_second = delta_three + right_product(delta_tside, full_tmix)
    delta_pooled = delta_four + right_product(delta_lside, full_lmix)

    def back_direction(direction, step_order, gate_inputs, saved_states, delta_carried):
        delta_inputs = [None] * letter_slots
        delta_gate_list = [None] * letter_slots
        state_list = [None] * letter_slots
        delta_hshift = jnp.zeros((gates_width,), jnp.float32)
        for turn in range(letter_slots - 1, -1, -1):
            position = step_order[turn]
            carried = saved_states[turn]
            active = (position < counts)[:, None]
            carried_low = carried.astype(jnp.bfloat16)
            hidden_gates = product(carried_low, ghid_of[direction]) + full_shid[direction]
            unused_cell, pullback = jax.vjp(
                recurrent_cell, gate_inputs[position], hidden_gates, carried
            )
            delta_in, delta_gates, delta_direct = pullback(jnp.where(active, delta_carried, 0.0))
            gates_low = delta_gates.astype(jnp.bfloat16)
            delta_hshift = delta_hshift + column_sum(gates_low)
            delta_carried = (
                jnp.where(active, 0.0, delta_carried)
                + delta_direct
                + right_product(gates_low, ghid_of[direction])
            )
            delta_inputs[position] = delta_in.astype(jnp.bfloat16)
            delta_gate_list[turn] = gates_low
            state_list[turn] = carried_low
        inputs_low = jnp.concatenate(delta_inputs, axis=0)
        return (
            inputs_low,
            column_sum(inputs_low),
            jnp.concatenate(state_list, axis=0),
            jnp.concatenate(delta_gate_list, axis=0),
            delta_hshift,
        )

    forth_back = back_direction(
        0, forward_order, forth_inputs, forth_saved, delta_pooled[:, :hidden_width]
    )
    back_back = back_direction(
        1, reverse_order, back_inputs, back_saved, delta_pooled[:, hidden_width:]
    )
    gates_low = jnp.concatenate([forth_back[0], back_back[0]], axis=1)
    letters_grad = (
        right_product(gates_low, full_gin)
        .astype(jnp.bfloat16)
        .reshape(letter_slots, seq_rows, model_width)
        .transpose(1, 0, 2)
    )
    gin_grad = owned_gradient(place, letter_flat, gates_low, True)
    gin_grad = jnp.stack([gin_grad[:, :gates_width], gin_grad[:, gates_width:]])
    sin_delta = jnp.stack([forth_back[1], back_back[1]])
    shid_delta = jnp.stack([forth_back[4], back_back[4]])
    ghid_grad = owned_hidden(
        place, (forth_back[2], back_back[2]), (forth_back[3], back_back[3])
    )

    unused_two, pull_two = jax.vjp(normalize, residual_two, gain_two, shift_two)
    delta_two, delta_gain_two, delta_shift_two = pull_two(delta_second)
    delta_lowered = delta_two.astype(jnp.bfloat16)
    down_grad = owned_gradient(place, activated, delta_lowered, False)
    delta_dbias = column_sum(delta_lowered)
    unused_act, pull_act = jax.vjp(exact_gelu, upper)
    delta_upper = pull_act(right_product(delta_lowered, full_down))[0].astype(jnp.bfloat16)
    up_grad = owned_gradient(place, first_low, delta_upper, False)
    delta_ubias = column_sum(delta_upper)
    delta_first = delta_two + right_product(delta_upper, full_up)
    unused_one, pull_one = jax.vjp(normalize, residual_one, gain_one, shift_one)
    delta_one, delta_gain_one, delta_shift_one = pull_one(delta_first)
    delta_attended = delta_one.astype(jnp.bfloat16)
    output_grad = owned_gradient(place, context, delta_attended, False)
    delta_obias = column_sum(delta_attended)
    delta_context = (
        right_product(delta_attended, full_output)
        .astype(jnp.bfloat16)
        .reshape(seq_rows, HEADS, head_width)
    )
    probabilities = jnp.exp(masked_scores_of(queries, key_rows) - log_total)
    delta_values = jnp.einsum(
        "hqk,qhd->khd",
        probabilities.astype(jnp.bfloat16),
        delta_context,
        preferred_element_type=jnp.float32,
    )
    delta_probs = jnp.einsum(
        "qhd,khd->hqk", delta_context, value_rows, preferred_element_type=jnp.float32
    )
    delta_scores = (
        probabilities * (delta_probs - jnp.sum(probabilities * delta_probs, axis=-1, keepdims=True))
    ).astype(jnp.bfloat16)
    delta_queries = (
        jnp.einsum("hqk,khd->qhd", delta_scores, key_rows, preferred_element_type=jnp.float32)
        * score_scale
    )
    delta_keys = (
        jnp.einsum("hqk,qhd->khd", delta_scores, queries, preferred_element_type=jnp.float32)
        * score_scale
    )
    delta_mixed = jnp.concatenate(
        [
            delta_queries.reshape(seq_rows, model_width),
            delta_keys.reshape(seq_rows, model_width),
            delta_values.reshape(seq_rows, model_width),
        ],
        axis=-1,
    ).astype(jnp.bfloat16)
    project_grad = owned_gradient(place, tokens, delta_mixed, True)
    delta_mixed_sum = column_sum(delta_mixed)
    delta_pbias = jnp.concatenate(
        [delta_mixed_sum[:model_width], delta_mixed_sum[2 * model_width :]]
    )
    tokens_grad = (delta_one + right_product(delta_mixed, full_project)).astype(jnp.bfloat16)
    (
        pbias_grad,
        obias_grad,
        gain_one_grad,
        shift_one_grad,
        ubias_grad,
        dbias_grad,
        gain_two_grad,
        shift_two_grad,
        sin_grad,
        shid_grad,
        toff_grad,
        loff_grad,
        koff_grad,
        gain_three_grad,
        shift_three_grad,
        gain_four_grad,
        shift_four_grad,
    ) = owned_vectors(
        place,
        (
            delta_pbias,
            delta_obias,
            delta_gain_one,
            delta_shift_one,
            delta_ubias,
            delta_dbias,
            delta_gain_two,
            delta_shift_two,
            sin_delta,
            shid_delta,
            delta_toff,
            delta_loff,
            delta_koff,
            delta_gain_three,
            delta_shift_three,
            delta_gain_four,
            delta_shift_four,
        ),
    )
    taps_grad = jnp.stack(
        [kernel_grad[:, t * joined_width : (t + 1) * joined_width] for t in range(3)]
    )
    return (
        token_out.astype(jnp.bfloat16),
        letter_out.astype(jnp.bfloat16),
        tokens_grad,
        letters_grad,
        project_grad,
        pbias_grad,
        output_grad,
        obias_grad,
        gain_one_grad,
        shift_one_grad,
        up_grad,
        ubias_grad,
        down_grad,
        dbias_grad,
        gain_two_grad,
        shift_two_grad,
        gin_grad,
        ghid_grad,
        sin_grad,
        shid_grad,
        tmix_grad,
        toff_grad,
        lmix_grad,
        loff_grad,
        taps_grad,
        koff_grad,
        gain_three_grad,
        shift_three_grad,
        gain_four_grad,
        shift_four_grad,
    )


def solution(mesh):
    placed = (
        P(("rep", "shard"), None),
        P(("rep", "shard"), None, None),
        P(("rep", "shard")),
        P(("rep", "shard")),
        P(("rep", "shard"), None),
        P(("rep", "shard"), None),
        P("shard", None),
        P("shard"),
        P("shard", None),
        P("shard"),
        P("shard"),
        P("shard"),
        P("shard", None),
        P("shard"),
        P("shard", None),
        P("shard"),
        P("shard"),
        P("shard"),
        P(None, "shard", None),
        P(None, "shard", None),
        P(None, "shard"),
        P(None, "shard"),
        P("shard", None),
        P("shard"),
        P("shard", None),
        P("shard"),
        P(None, "shard", None),
        P("shard"),
        P("shard"),
        P("shard"),
        P("shard"),
        P("shard"),
    )
    return jax.shard_map(
        shards,
        mesh=mesh,
        in_specs=placed,
        out_specs=(
            P(("rep", "shard"), None),
            P(("rep", "shard"), None),
            P(("rep", "shard"), None),
            P(("rep", "shard"), None, None),
            P("shard", None),
            P("shard"),
            P("shard", None),
            P("shard"),
            P("shard"),
            P("shard"),
            P("shard", None),
            P("shard"),
            P("shard", None),
            P("shard"),
            P("shard"),
            P("shard"),
            P(None, "shard", None),
            P(None, "shard", None),
            P(None, "shard"),
            P(None, "shard"),
            P("shard", None),
            P("shard"),
            P("shard", None),
            P("shard"),
            P(None, "shard", None),
            P("shard"),
            P("shard"),
            P("shard"),
            P("shard"),
            P("shard"),
        ),
        check_vma=False,
    )
```

```python
import jax
import jax.numpy as jnp
from jax import lax
from jax.experimental import pallas as pl
from jax.experimental.pallas import tpu as pltpu
from jax.sharding import PartitionSpec as P

HEADS = 12


EPS = 1e-05


def shortened(value):
    return jax.tree.map(lambda a: a.astype(jnp.bfloat16) if a.dtype == jnp.float32 else a, value)


def product(left, right):
    return jnp.dot(left, right, preferred_element_type=jnp.float32)


def left_product(left, right):
    return lax.dot_general(
        left, right, (((0,), (0,)), ((), ())), preferred_element_type=jnp.float32
    )


def right_product(left, right):
    return lax.dot_general(
        left, right, (((1,), (1,)), ((), ())), preferred_element_type=jnp.float32
    )


def column_sum(values):
    return jnp.sum(values.astype(jnp.float32), axis=0)


def normalize(values, gain, shift):
    center = jnp.mean(values, axis=-1, keepdims=True)
    centered = values - center
    spread = jnp.mean(centered * centered, axis=-1, keepdims=True)
    return centered * lax.rsqrt(spread + EPS) * gain + shift


def gelu_and_slope(values):
    below = 0.5 + 0.5 * lax.erf(values * (0.5**0.5))
    density = jnp.exp(-0.5 * values * values) * ((2.0 * jnp.pi) ** -0.5)
    return values * below, below + values * density


def logistic(values):
    return 0.5 + 0.5 * jnp.tanh(0.5 * values)


def recurrent_forward(slots, gin, ghid, sin, shid, counts):
    letter_slots, rows, width = slots.shape
    hidden = ghid.shape[0]
    gates = 3 * hidden
    last_slot = letter_slots - 1

    def body(
        ahead_ref,
        behind_ref,
        gin_ref,
        ghid_ref,
        sin_ref,
        shid_ref,
        counts_ref,
        gates_ahead,
        gates_behind,
        prev_ahead,
        prev_behind,
        last_ref,
        state_ref,
    ):
        step = pl.program_id(0)

        @pl.when(step == 0)
        def _():
            state_ref[...] = jnp.zeros_like(state_ref)

        counts_in = counts_ref[...]
        work = (
            (0, ahead_ref, step, gates_ahead, prev_ahead),
            (1, behind_ref, last_slot - step, gates_behind, prev_behind),
        )
        for at, slot_ref, slot, gates_ref, prev_ref in work:
            columns = slice(at * gates, (at + 1) * gates)
            own = slice(at * hidden, (at + 1) * hidden)
            state = state_ref[:, own]
            state_low = state.astype(jnp.bfloat16)
            prev_ref[0] = state_low
            inputs = product(slot_ref[0], gin_ref[:, columns]) + sin_ref[:, columns]
            turned = product(state_low, ghid_ref[:, columns]) + shid_ref[:, columns]
            reset = logistic(inputs[:, :hidden] + turned[:, :hidden])
            update = logistic(
                inputs[:, hidden : 2 * hidden] + turned[:, hidden : 2 * hidden]
            )
            turned_new = turned[:, 2 * hidden :]
            fresh = jnp.tanh(inputs[:, 2 * hidden :] + reset * turned_new)
            gates_ref[0, :, :hidden] = reset.astype(jnp.bfloat16)
            gates_ref[0, :, hidden : 2 * hidden] = update.astype(jnp.bfloat16)
            gates_ref[0, :, 2 * hidden : 3 * hidden] = fresh.astype(jnp.bfloat16)
            gates_ref[0, :, 3 * hidden :] = turned_new.astype(jnp.bfloat16)
            moved = (1.0 - update) * fresh + update * state
            state_ref[:, own] = jnp.where(slot < counts_in, moved, state)

        @pl.when(step == last_slot)
        def _():
            last_ref[...] = state_ref[...]

    ahead = lambda i: (i, 0, 0)
    behind = lambda i: (last_slot - i, 0, 0)
    fixed = lambda i: (0, 0)
    low = jnp.bfloat16
    return pl.pallas_call(
        body,
        grid=(letter_slots,),
        in_specs=[
            pl.BlockSpec((1, rows, width), ahead),
            pl.BlockSpec((1, rows, width), behind),
            pl.BlockSpec(gin.shape, fixed),
            pl.BlockSpec(ghid.shape, fixed),
            pl.BlockSpec((1, 2 * gates), fixed),
            pl.BlockSpec((1, 2 * gates), fixed),
            pl.BlockSpec((rows, 1), fixed),
        ],
        out_specs=[
            pl.BlockSpec((1, rows, 4 * hidden), ahead),
            pl.BlockSpec((1, rows, 4 * hidden), behind),
            pl.BlockSpec((1, rows, hidden), ahead),
            pl.BlockSpec((1, rows, hidden), behind),
            pl.BlockSpec((rows, 2 * hidden), fixed),
        ],
        out_shape=[
            jax.ShapeDtypeStruct((letter_slots, rows, 4 * hidden), low),
            jax.ShapeDtypeStruct((letter_slots, rows, 4 * hidden), low),
            jax.ShapeDtypeStruct((letter_slots, rows, hidden), low),
            jax.ShapeDtypeStruct((letter_slots, rows, hidden), low),
            jax.ShapeDtypeStruct((rows, 2 * hidden), jnp.float32),
        ],
        scratch_shapes=[pltpu.VMEM((rows, 2 * hidden), jnp.float32)],
        name="recurrent_forward",
    )(slots, slots, gin, ghid, sin, shid, counts)


def recurrent_backward(saved_gates, saved_states, ghid, counts, delta):
    letter_slots, rows, _ = saved_gates[0].shape
    hidden = ghid.shape[0]
    gates = 3 * hidden
    last_slot = letter_slots - 1

    def body(
        gates_ahead,
        gates_behind,
        prev_ahead,
        prev_behind,
        ghid_ref,
        counts_ref,
        delta_ref,
        inputs_ahead,
        inputs_behind,
        turned_ahead,
        turned_behind,
        inputs_sum,
        turned_sum,
        carry_ref,
    ):
        step = pl.program_id(0)

        @pl.when(step == 0)
        def _():
            carry_ref[...] = delta_ref[...]
            inputs_sum[...] = jnp.zeros_like(inputs_sum)
            turned_sum[...] = jnp.zeros_like(turned_sum)

        counts_in = counts_ref[...]
        work = (
            (0, last_slot - step, gates_ahead, prev_ahead, inputs_ahead, turned_ahead),
            (1, step, gates_behind, prev_behind, inputs_behind, turned_behind),
        )
        for at, slot, gates_ref, prev_ref, inputs_ref, turned_ref in work:
            start = at * gates
            own = slice(at * hidden, (at + 1) * hidden)
            reset = gates_ref[0, :, :hidden].astype(jnp.float32)
            update = gates_ref[0, :, hidden : 2 * hidden].astype(jnp.float32)
            fresh = gates_ref[0, :, 2 * hidden : 3 * hidden].astype(jnp.float32)
            turned_new = gates_ref[0, :, 3 * hidden :].astype(jnp.float32)
            state = prev_ref[0].astype(jnp.float32)
            carry = carry_ref[:, own]
            active = slot < counts_in
            moved = jnp.where(active, carry, 0.0)
            delta_fresh = moved * (1.0 - update) * (1.0 - fresh * fresh)
            delta_update = moved * (state - fresh) * update * (1.0 - update)
            delta_reset = delta_fresh * turned_new * reset * (1.0 - reset)
            low_reset = delta_reset.astype(jnp.bfloat16)
            low_update = delta_update.astype(jnp.bfloat16)
            low_fresh = delta_fresh.astype(jnp.bfloat16)
            low_turned = (delta_fresh * reset).astype(jnp.bfloat16)
            inputs_ref[0, :, :hidden] = low_reset
            inputs_ref[0, :, hidden : 2 * hidden] = low_update
            inputs_ref[0, :, 2 * hidden :] = low_fresh
            turned_ref[0, :, :hidden] = low_reset
            turned_ref[0, :, hidden : 2 * hidden] = low_update
            turned_ref[0, :, 2 * hidden :] = low_turned
            through = right_product(turned_ref[0], ghid_ref[:, start : start + gates])
            carry_ref[:, own] = jnp.where(active, moved * update, carry) + through
            sums = [
                jnp.sum(part.astype(jnp.float32), axis=0, keepdims=True)
                for part in (low_reset, low_update, low_fresh, low_turned)
            ]
            for place_at, (first, second) in enumerate(
                ((sums[0], sums[0]), (sums[1], sums[1]), (sums[2], sums[3]))
            ):
                columns = slice(start + place_at * hidden, start + (place_at + 1) * hidden)
                inputs_sum[:, columns] += first
                turned_sum[:, columns] += second

    ahead = lambda i: (last_slot - i, 0, 0)
    behind = lambda i: (i, 0, 0)
    fixed = lambda i: (0, 0)
    low = jnp.bfloat16
    return pl.pallas_call(
        body,
        grid=(letter_slots,),
        in_specs=[
            pl.BlockSpec((1, rows, 4 * hidden), ahead),
            pl.BlockSpec((1, rows, 4 * hidden), behind),
            pl.BlockSpec((1, rows, hidden), ahead),
            pl.BlockSpec((1, rows, hidden), behind),
            pl.BlockSpec(ghid.shape, fixed),
            pl.BlockSpec((rows, 1), fixed),
            pl.BlockSpec((rows, 2 * hidden), fixed),
        ],
        out_specs=[
            pl.BlockSpec((1, rows, gates), ahead),
            pl.BlockSpec((1, rows, gates), behind),
            pl.BlockSpec((1, rows, gates), ahead),
            pl.BlockSpec((1, rows, gates), behind),
            pl.BlockSpec((1, 2 * gates), fixed),
            pl.BlockSpec((1, 2 * gates), fixed),
        ],
        out_shape=[
            jax.ShapeDtypeStruct((letter_slots, rows, gates), low),
            jax.ShapeDtypeStruct((letter_slots, rows, gates), low),
            jax.ShapeDtypeStruct((letter_slots, rows, gates), low),
            jax.ShapeDtypeStruct((letter_slots, rows, gates), low),
            jax.ShapeDtypeStruct((1, 2 * gates), jnp.float32),
            jax.ShapeDtypeStruct((1, 2 * gates), jnp.float32),
        ],
        scratch_shapes=[pltpu.VMEM((rows, 2 * hidden), jnp.float32)],
        name="recurrent_backward",
    )(*saved_gates, *saved_states, ghid, counts, delta)


DEPTH_SIZE = 4


class Place:
    def __init__(self):
        self.rep_size = lax.axis_size("rep")
        self.shard_size = lax.axis_size("shard")
        self.depth = DEPTH_SIZE
        self.height = self.shard_size // DEPTH_SIZE
        rep_at = lax.axis_index("rep")
        shard_at = lax.axis_index("shard")
        self.shard_at = shard_at
        self.core = rep_at % 2
        self.side = (rep_at // 2) % 2
        self.row = shard_at % self.height
        self.layer = shard_at // self.height
        self.coords = jnp.stack([self.layer, self.row, self.side, self.core]).astype(jnp.int32)

    def over_core(self, value):
        return lax.ppermute(value, "rep", [(i, i ^ 1) for i in range(self.rep_size)])

    def over_side(self, value):
        return lax.ppermute(value, "rep", [(i, i ^ 2) for i in range(self.rep_size)])

    def over_far(self, value, step):
        return lax.ppermute(
            value, "rep", [(i, (i + 4 * step) % self.rep_size) for i in range(self.rep_size)]
        )

    def over_row(self, value, step):
        return lax.ppermute(value, "shard", [(i, i ^ step) for i in range(self.shard_size)])

    def over_layer(self, value, step):
        return lax.ppermute(
            value, "shard", [(i, i ^ (step * self.height)) for i in range(self.shard_size)]
        )


def put_together(place, parts, rows, half, split):
    depth = place.depth
    flat = [part for group in parts for inner in group for part in inner]
    slots = [
        (core_slot, side_slot, row_slot)
        for core_slot in range(2)
        for side_slot in range(len(parts[0]))
        for row_slot in range(len(parts[0][0]))
    ]
    height = place.height
    pieces = 2 if split else 1
    part_rows = [r // pieces for r in rows]
    starts = [sum(part_rows[:i]) for i in range(len(rows))]

    def body(coords_ref, *refs):
        ins = refs[: len(flat)]
        outs = refs[len(flat) : len(flat) + len(rows)]
        sems = refs[-1]
        layer, row, side, core = (coords_ref[i] for i in range(4))
        copies = []
        for at, (core_slot, side_slot, row_slot) in enumerate(slots):
            for layer_slot in range(depth):
                block = (layer ^ layer_slot) * height + (row ^ row_slot)
                if split:
                    block = block * 2 + (side ^ side_slot)
                column = pl.multiple_of((core ^ core_slot) * half, 128)
                for out_ref, start, count in zip(outs, starts, part_rows):
                    copies.append(
                        pltpu.make_async_copy(
                            ins[at].at[layer_slot, pl.ds(start, count), :],
                            out_ref.at[block, :, pl.ds(column, half)],
                            sems.at[len(copies)],
                        )
                    )
        for copy in copies:
            copy.start()
        for copy in copies:
            copy.wait()

    blocks = depth * height * pieces
    whole = pl.pallas_call(
        body,
        out_shape=[
            jax.ShapeDtypeStruct((blocks, count, 2 * half), flat[0].dtype) for count in part_rows
        ],
        in_specs=[pl.BlockSpec(memory_space=pltpu.SMEM)]
        + [pl.BlockSpec(memory_space=pl.ANY)] * len(flat),
        out_specs=[pl.BlockSpec(memory_space=pltpu.VMEM)] * len(rows),
        scratch_shapes=[pltpu.SemaphoreType.DMA((len(flat) * depth * len(rows),))],
        name="put_together",
    )(place.coords, *flat)
    return [w.reshape(r * place.shard_size, 2 * half) for w, r in zip(whole, rows)]


def gathered(place, shards_in, split):
    half = shards_in[0].shape[1] // 2
    pieces = []
    for shard in shards_in:
        part_rows = shard.shape[0] // 2 if split else shard.shape[0]
        top = place.side * part_rows if split else 0
        pieces.append(lax.dynamic_slice(shard, (top, place.core * half), (part_rows, half)))
    piece = pieces[0] if len(pieces) == 1 else jnp.concatenate(pieces, axis=0)
    layers = jnp.stack(
        [piece] + [place.over_layer(piece, step) for step in range(1, place.depth)]
    )
    column = [layers] + [place.over_row(layers, step) for step in range(1, place.height)]
    sides = [column]
    if split:
        sides.append([place.over_side(part) for part in column])
    cores = [sides, [[place.over_core(part) for part in group] for group in sides]]
    return put_together(place, cores, [shard.shape[0] for shard in shards_in], half, split)


def pick(value, at, axis):
    return lax.dynamic_index_in_dim(value, at, axis, keepdims=False)


def widen(value):
    return value.astype(jnp.float32)


def narrow(value):
    return value.astype(jnp.bfloat16)


def core_sum(place, inputs, delta):
    half = delta.shape[1] // 2

    def half_of(at):
        return left_product(inputs, lax.dynamic_slice_in_dim(delta, at * half, half, axis=1))

    other = place.over_core(narrow(half_of(1 - place.core)))
    return narrow(half_of(place.core) + widen(other))


def core_sum_of_pair(place, first, second):
    first, second = narrow(first), narrow(second)
    other = place.over_core(jnp.where(place.core == 0, second, first))
    return narrow(widen(jnp.where(place.core == 0, first, second)) + widen(other))


def owned_sums(place, helds, split):
    half = helds[0].shape[1]
    pieces = 2 if split else 1
    parts = [h.shape[0] // place.shard_size // pieces for h in helds]
    blocks = [h.reshape(place.shard_size, pieces, p, half) for h, p in zip(helds, parts)]
    if split:
        kept = []
        for block in blocks:
            other = place.over_side(pick(block, 1 - place.side, 1))
            kept.append(narrow(widen(pick(block, place.side, 1)) + widen(other)))
    else:
        kept = [block[:, 0] for block in blocks]
    shape = (place.depth, place.height)
    kept = [k.reshape(shape + k.shape[1:]) for k in kept]

    def stacked(values):
        return values[0] if len(values) == 1 else jnp.concatenate(values, axis=-2)

    total = widen(stacked([pick(k, place.row, 1) for k in kept]))
    for step in range(1, place.height):
        sent = stacked([pick(k, place.row ^ step, 1) for k in kept])
        total = total + widen(place.over_row(sent, step))
    held = narrow(total)
    total = widen(pick(held, place.layer, 0))
    for step in range(1, place.depth):
        total = total + widen(place.over_layer(pick(held, place.layer ^ step, 0), step))
    held = narrow(total)
    for step in range(1, place.rep_size // 4):
        total = total + widen(place.over_far(held, step))
    held = narrow(total)
    other = place.over_side(held)
    if split:
        low_side = jnp.where(place.side == 0, held, other)
        high_side = jnp.where(place.side == 0, other, held)
        rows, start = [], 0
        for p in parts:
            rows += [low_side[start : start + p], high_side[start : start + p]]
            start += p
        held = jnp.concatenate(rows, axis=0)
    else:
        held = narrow(widen(held) + widen(other))
    other = place.over_core(held)
    first = jnp.where(place.core == 0, held, other)
    last = jnp.where(place.core == 0, other, held)
    results, start = [], 0
    for p in parts:
        own = slice(start, start + p * pieces)
        results.append(widen(jnp.concatenate([first[own], last[own]], axis=1)))
        start += p * pieces
    return results


def gathered_vectors(place, vectors):
    flat = [v.reshape(-1) for v in vectors]
    packed = jnp.concatenate(flat)[None, :]
    layers = jnp.concatenate(
        [packed] + [place.over_layer(packed, step) for step in range(1, place.depth)], axis=0
    )
    slots = jnp.stack(
        [layers] + [place.over_row(layers, step) for step in range(1, place.height)], axis=1
    ).reshape(place.shard_size, -1)
    order = jnp.arange(place.shard_size)
    slot_of = ((order // place.height) ^ place.layer) * place.height + (
        (order % place.height) ^ place.row
    )
    ordered = jnp.take(slots, slot_of, axis=0, mode="clip").astype(jnp.float32)
    whole, start = [], 0
    for v in vectors:
        width = v.size
        part = ordered[:, start : start + width]
        if v.ndim == 1:
            whole.append(part.reshape(-1))
        else:
            lead, inner = v.shape
            whole.append(
                part.reshape(place.shard_size, lead, inner).transpose(1, 0, 2).reshape(lead, -1)
            )
        start += width
    return whole


def owned_vectors(place, vectors):
    count = place.shard_size
    rows = []
    for v in vectors:
        if v.ndim == 1:
            rows.append(v.reshape(count, -1))
        else:
            lead = v.shape[0]
            rows.append(v.reshape(lead, count, -1).transpose(1, 0, 2).reshape(count, -1))
    total = jnp.concatenate(rows, axis=1)
    total = total + place.over_core(total)
    total = total + place.over_side(total)
    base = total
    for step in range(1, place.rep_size // 4):
        total = total + place.over_far(base, step)
    span = 1
    while span < place.height:
        total = total + place.over_row(total, span)
        span *= 2
    span = 1
    while span < place.depth:
        total = total + place.over_layer(total, span)
        span *= 2
    own = lax.dynamic_index_in_dim(total, place.shard_at, 0, keepdims=False)
    parts, start = [], 0
    for v in vectors:
        width = v.size // count
        part = own[start : start + width]
        parts.append(part if v.ndim == 1 else part.reshape(v.shape[0], -1))
        start += width
    return parts


def shards(
    tokens,
    letters,
    lengths,
    counts,
    cot_token,
    cot_letter,
    project_weight,
    project_bias,
    output_weight,
    output_bias,
    first_gain,
    first_shift,
    up_weight,
    up_bias,
    down_weight,
    down_bias,
    second_gain,
    second_shift,
    gates_input,
    gates_hidden,
    shift_input,
    shift_hidden,
    token_mixer,
    token_offset,
    letter_mixer,
    letter_offset,
    window_kernel,
    window_offset,
    third_gain,
    third_shift,
    fourth_gain,
    fourth_shift,
):
    place = Place()
    seq_rows, model_width = tokens.shape
    letter_slots = letters.shape[1]
    head_width = model_width // HEADS
    score_scale = float(head_width) ** (-0.5)
    row_valid = jnp.arange(seq_rows) < lengths[0]
    row_mask = row_valid.astype(jnp.float32)[:, None]
    key_valid = row_valid[None, None, :]
    letter_flat = letters.transpose(1, 0, 2).reshape(letter_slots * seq_rows, model_width)

    (
        full_pbias,
        full_obias,
        gain_one,
        shift_one,
        full_ubias,
        full_dbias,
        gain_two,
        shift_two,
        full_sin,
        full_shid,
        full_toff,
        full_loff,
        full_koff,
        gain_three,
        shift_three,
        gain_four,
        shift_four,
    ) = gathered_vectors(
        place,
        (
            project_bias,
            output_bias,
            first_gain,
            first_shift,
            up_bias,
            down_bias,
            second_gain,
            second_shift,
            shift_input,
            shift_hidden,
            token_offset,
            letter_offset,
            window_offset,
            third_gain,
            third_shift,
            fourth_gain,
            fourth_shift,
        ),
    )
    side_by_side = lambda w: jnp.concatenate([w[i] for i in range(w.shape[0])], axis=1)
    full_gin, full_project = gathered(place, (side_by_side(gates_input), project_weight), True)
    (full_ghid,) = gathered(place, (side_by_side(gates_hidden),), False)
    full_output, full_down, full_tmix, full_lmix = gathered(
        place, (output_weight, down_weight, token_mixer, letter_mixer), False
    )
    (full_up,) = gathered(place, (up_weight,), False)
    (full_kernel,) = gathered(place, (side_by_side(window_kernel),), True)

    bias_full = jnp.concatenate(
        [full_pbias[:model_width], jnp.zeros((model_width,), jnp.float32), full_pbias[model_width:]]
    )
    mixed = (product(tokens, full_project) + bias_full).astype(jnp.bfloat16)
    queries = mixed[:, :model_width].reshape(seq_rows, HEADS, head_width)
    key_rows = mixed[:, model_width : 2 * model_width].reshape(seq_rows, HEADS, head_width)
    value_rows = mixed[:, 2 * model_width :].reshape(seq_rows, HEADS, head_width)

    def masked_scores_of(query_part, key_part):
        raw_scores = (
            jnp.einsum("qhd,khd->hqk", query_part, key_part, preferred_element_type=jnp.float32)
            * score_scale
        )
        return jnp.where(key_valid, raw_scores, -1e30)

    masked_scores = masked_scores_of(queries, key_rows)
    row_peak = jnp.max(masked_scores, axis=-1, keepdims=True)
    log_total = row_peak + jnp.log(
        jnp.sum(jnp.exp(masked_scores - row_peak), axis=-1, keepdims=True)
    )
    probabilities = jnp.exp(masked_scores - log_total)
    probs_low = probabilities.astype(jnp.bfloat16)
    context = (
        jnp.einsum("hqk,khd->qhd", probs_low, value_rows, preferred_element_type=jnp.float32)
        .astype(jnp.bfloat16)
        .reshape(seq_rows, model_width)
    )
    attended = product(context, full_output) + full_obias
    residual_one = tokens.astype(jnp.float32) + attended
    first = normalize(residual_one, gain_one, shift_one)
    first_low = first.astype(jnp.bfloat16)
    upper = product(first_low, full_up) + full_ubias
    activated, slope_upper = gelu_and_slope(upper)
    activated = activated.astype(jnp.bfloat16)
    residual_two = first + product(activated, full_down) + full_dbias
    second = normalize(residual_two, gain_two, shift_two)
    hidden_width = full_ghid.shape[0]
    gates_width = 3 * hidden_width
    counts_column = counts.reshape(-1, 1)
    gates_ahead, gates_behind, prev_ahead, prev_behind, pooled = recurrent_forward(
        letter_flat.reshape(letter_slots, seq_rows, model_width),
        full_gin,
        full_ghid,
        full_sin.reshape(1, -1),
        full_shid.reshape(1, -1),
        counts_column,
    )
    second_low = second.astype(jnp.bfloat16)
    pooled_low = pooled.astype(jnp.bfloat16)
    token_side = product(second_low, full_tmix) + full_toff
    letter_side = product(pooled_low, full_lmix) + full_loff
    joined = (jnp.concatenate([token_side, letter_side], axis=-1) * row_mask).astype(jnp.bfloat16)
    joined_width = joined.shape[1]
    taps = product(joined, full_kernel)
    convolved = (
        jnp.pad(taps[:-1, :joined_width], ((1, 0), (0, 0)))
        + taps[:, joined_width : 2 * joined_width]
        + jnp.pad(taps[1:, 2 * joined_width :], ((0, 1), (0, 0)))
        + full_koff
    )
    widened, slope_conv = gelu_and_slope(convolved)
    residual_three = second + widened[:, :model_width]
    residual_four = pooled + widened[:, model_width:]
    token_out = normalize(residual_three, gain_three, shift_three) * row_mask
    letter_out = normalize(residual_four, gain_four, shift_four) * row_mask

    out_token_delta = cot_token.astype(jnp.float32) * row_mask
    out_letter_delta = cot_letter.astype(jnp.float32) * row_mask
    unused_three, pull_three = jax.vjp(normalize, residual_three, gain_three, shift_three)
    delta_three, delta_gain_three, delta_shift_three = pull_three(out_token_delta)
    unused_four, pull_four = jax.vjp(normalize, residual_four, gain_four, shift_four)
    delta_four, delta_gain_four, delta_shift_four = pull_four(out_letter_delta)
    delta_conv = (jnp.concatenate([delta_three, delta_four], axis=-1) * slope_conv).astype(
        jnp.bfloat16
    )
    delta_koff = column_sum(delta_conv)
    delta_taps = jnp.concatenate(
        [
            jnp.pad(delta_conv[1:], ((0, 1), (0, 0))),
            delta_conv,
            jnp.pad(delta_conv[:-1], ((1, 0), (0, 0))),
        ],
        axis=1,
    )
    (kernel_grad,) = owned_sums(place, (core_sum(place, joined, delta_taps),), True)
    delta_joined = right_product(delta_taps, full_kernel) * row_mask
    delta_tside = delta_joined[:, :model_width].astype(jnp.bfloat16)
    delta_lside = delta_joined[:, model_width:].astype(jnp.bfloat16)
    tmix_sum = core_sum(place, second_low, delta_tside)
    delta_toff = column_sum(delta_tside)
    lmix_sum = core_sum(place, pooled_low, delta_lside)
    delta_loff = column_sum(delta_lside)
    delta_second = delta_three + right_product(delta_tside, full_tmix)
    delta_pooled = delta_four + right_product(delta_lside, full_lmix)

    inputs_ahead, inputs_behind, turned_ahead, turned_behind, sin_delta, shid_delta = (
        recurrent_backward(
            (gates_ahead, gates_behind),
            (prev_ahead, prev_behind),
            full_ghid,
            counts_column,
            delta_pooled,
        )
    )
    flat_rows = lambda v: v.reshape(letter_slots * seq_rows, -1)
    inputs_ahead, inputs_behind = flat_rows(inputs_ahead), flat_rows(inputs_behind)
    gin_sum = core_sum_of_pair(
        place,
        left_product(letter_flat, inputs_ahead),
        left_product(letter_flat, inputs_behind),
    )
    ghid_sum = core_sum_of_pair(
        place,
        left_product(flat_rows(prev_ahead), flat_rows(turned_ahead)),
        left_product(flat_rows(prev_behind), flat_rows(turned_behind)),
    )
    letters_grad = (
        (
            right_product(inputs_ahead, full_gin[:, :gates_width])
            + right_product(inputs_behind, full_gin[:, gates_width:])
        )
        .astype(jnp.bfloat16)
        .reshape(letter_slots, seq_rows, model_width)
        .transpose(1, 0, 2)
    )
    sin_delta = sin_delta.reshape(2, -1)
    shid_delta = shid_delta.reshape(2, -1)
    in_pair = lambda v: jnp.stack([v[:, :gates_width], v[:, gates_width:]])
    (ghid_grad,) = owned_sums(place, (ghid_sum,), False)
    (gin_grad,) = owned_sums(place, (gin_sum,), True)
    ghid_grad, gin_grad = in_pair(ghid_grad), in_pair(gin_grad)

    unused_two, pull_two = jax.vjp(normalize, residual_two, gain_two, shift_two)
    delta_two, delta_gain_two, delta_shift_two = pull_two(delta_second)
    delta_lowered = delta_two.astype(jnp.bfloat16)
    down_sum = core_sum(place, activated, delta_lowered)
    tmix_grad, lmix_grad, down_grad = owned_sums(place, (tmix_sum, lmix_sum, down_sum), False)
    delta_dbias = column_sum(delta_lowered)
    delta_upper = (right_product(delta_lowered, full_down) * slope_upper).astype(jnp.bfloat16)
    (up_grad,) = owned_sums(place, (core_sum(place, first_low, delta_upper),), False)
    delta_ubias = column_sum(delta_upper)
    delta_first = delta_two + right_product(delta_upper, full_up)
    unused_one, pull_one = jax.vjp(normalize, residual_one, gain_one, shift_one)
    delta_one, delta_gain_one, delta_shift_one = pull_one(delta_first)
    delta_attended = delta_one.astype(jnp.bfloat16)
    (output_grad,) = owned_sums(place, (core_sum(place, context, delta_attended),), False)
    delta_obias = column_sum(delta_attended)
    delta_context = (
        right_product(delta_attended, full_output)
        .astype(jnp.bfloat16)
        .reshape(seq_rows, HEADS, head_width)
    )
    delta_values = jnp.einsum(
        "hqk,qhd->khd",
        probs_low,
        delta_context,
        preferred_element_type=jnp.float32,
    )
    delta_probs = jnp.einsum(
        "qhd,khd->hqk", delta_context, value_rows, preferred_element_type=jnp.float32
    )
    delta_scores = (
        probabilities * (delta_probs - jnp.sum(probabilities * delta_probs, axis=-1, keepdims=True))
    ).astype(jnp.bfloat16)
    delta_queries = (
        jnp.einsum("hqk,khd->qhd", delta_scores, key_rows, preferred_element_type=jnp.float32)
        * score_scale
    )
    delta_keys = (
        jnp.einsum("hqk,qhd->khd", delta_scores, queries, preferred_element_type=jnp.float32)
        * score_scale
    )
    delta_mixed = jnp.concatenate(
        [
            delta_queries.reshape(seq_rows, model_width),
            delta_keys.reshape(seq_rows, model_width),
            delta_values.reshape(seq_rows, model_width),
        ],
        axis=-1,
    ).astype(jnp.bfloat16)
    (project_grad,) = owned_sums(place, (core_sum(place, tokens, delta_mixed),), True)
    delta_mixed_sum = column_sum(delta_mixed)
    delta_pbias = jnp.concatenate(
        [delta_mixed_sum[:model_width], delta_mixed_sum[2 * model_width :]]
    )
    tokens_grad = (delta_one + right_product(delta_mixed, full_project)).astype(jnp.bfloat16)
    (
        pbias_grad,
        obias_grad,
        gain_one_grad,
        shift_one_grad,
        ubias_grad,
        dbias_grad,
        gain_two_grad,
        shift_two_grad,
        sin_grad,
        shid_grad,
        toff_grad,
        loff_grad,
        koff_grad,
        gain_three_grad,
        shift_three_grad,
        gain_four_grad,
        shift_four_grad,
    ) = owned_vectors(
        place,
        (
            delta_pbias,
            delta_obias,
            delta_gain_one,
            delta_shift_one,
            delta_ubias,
            delta_dbias,
            delta_gain_two,
            delta_shift_two,
            sin_delta,
            shid_delta,
            delta_toff,
            delta_loff,
            delta_koff,
            delta_gain_three,
            delta_shift_three,
            delta_gain_four,
            delta_shift_four,
        ),
    )
    taps_grad = jnp.stack(
        [kernel_grad[:, t * joined_width : (t + 1) * joined_width] for t in range(3)]
    )
    return (
        token_out.astype(jnp.bfloat16),
        letter_out.astype(jnp.bfloat16),
        tokens_grad,
        letters_grad,
        project_grad,
        pbias_grad,
        output_grad,
        obias_grad,
        gain_one_grad,
        shift_one_grad,
        up_grad,
        ubias_grad,
        down_grad,
        dbias_grad,
        gain_two_grad,
        shift_two_grad,
        gin_grad,
        ghid_grad,
        sin_grad,
        shid_grad,
        tmix_grad,
        toff_grad,
        lmix_grad,
        loff_grad,
        taps_grad,
        koff_grad,
        gain_three_grad,
        shift_three_grad,
        gain_four_grad,
        shift_four_grad,
    )


def solution(mesh):
    placed = (
        P(("rep", "shard"), None),
        P(("rep", "shard"), None, None),
        P(("rep", "shard")),
        P(("rep", "shard")),
        P(("rep", "shard"), None),
        P(("rep", "shard"), None),
        P("shard", None),
        P("shard"),
        P("shard", None),
        P("shard"),
        P("shard"),
        P("shard"),
        P("shard", None),
        P("shard"),
        P("shard", None),
        P("shard"),
        P("shard"),
        P("shard"),
        P(None, "shard", None),
        P(None, "shard", None),
        P(None, "shard"),
        P(None, "shard"),
        P("shard", None),
        P("shard"),
        P("shard", None),
        P("shard"),
        P(None, "shard", None),
        P("shard"),
        P("shard"),
        P("shard"),
        P("shard"),
        P("shard"),
    )
    return jax.shard_map(
        shards,
        mesh=mesh,
        in_specs=placed,
        out_specs=(
            P(("rep", "shard"), None),
            P(("rep", "shard"), None),
            P(("rep", "shard"), None),
            P(("rep", "shard"), None, None),
            P("shard", None),
            P("shard"),
            P("shard", None),
            P("shard"),
            P("shard"),
            P("shard"),
            P("shard", None),
            P("shard"),
            P("shard", None),
            P("shard"),
            P("shard"),
            P("shard"),
            P(None, "shard", None),
            P(None, "shard", None),
            P(None, "shard"),
            P(None, "shard"),
            P("shard", None),
            P("shard"),
            P("shard", None),
            P("shard"),
            P(None, "shard", None),
            P("shard"),
            P("shard"),
            P("shard"),
            P("shard"),
            P("shard"),
        ),
        check_vma=False,
    )
```

```python
import jax
import jax.numpy as jnp
from jax import lax
from jax.experimental import pallas as pl
from jax.experimental.pallas import tpu as pltpu
from jax.sharding import PartitionSpec as P

HEADS = 12


EPS = 1e-05


def shortened(value):
    return jax.tree.map(lambda a: a.astype(jnp.bfloat16) if a.dtype == jnp.float32 else a, value)


def product(left, right):
    return jnp.dot(left, right, preferred_element_type=jnp.float32)


def left_product(left, right):
    return lax.dot_general(
        left, right, (((0,), (0,)), ((), ())), preferred_element_type=jnp.float32
    )


def right_product(left, right):
    return lax.dot_general(
        left, right, (((1,), (1,)), ((), ())), preferred_element_type=jnp.float32
    )


def column_sum(values):
    return jnp.sum(values.astype(jnp.float32), axis=0)


def normalize(values, gain, shift):
    center = jnp.mean(values, axis=-1, keepdims=True)
    centered = values - center
    spread = jnp.mean(centered * centered, axis=-1, keepdims=True)
    return centered * lax.rsqrt(spread + EPS) * gain + shift


def gelu_and_slope(values):
    below = 0.5 + 0.5 * lax.erf(values * (0.5**0.5))
    density = jnp.exp(-0.5 * values * values) * ((2.0 * jnp.pi) ** -0.5)
    return values * below, below + values * density


def logistic(values):
    return 0.5 + 0.5 * jnp.tanh(0.5 * values)


def recurrent_forward(slots, gin, ghid, sin, shid, counts):
    letter_slots, rows, width = slots.shape
    hidden = ghid.shape[0]
    gates = 3 * hidden
    last_slot = letter_slots - 1

    def body(
        ahead_ref,
        behind_ref,
        gin_ref,
        ghid_ref,
        sin_ref,
        shid_ref,
        counts_ref,
        gates_ahead,
        gates_behind,
        prev_ahead,
        prev_behind,
        last_ref,
        state_ref,
    ):
        step = pl.program_id(0)

        @pl.when(step == 0)
        def _():
            state_ref[...] = jnp.zeros_like(state_ref)

        counts_in = counts_ref[...]
        work = (
            (0, ahead_ref, step, gates_ahead, prev_ahead),
            (1, behind_ref, last_slot - step, gates_behind, prev_behind),
        )
        for at, slot_ref, slot, gates_ref, prev_ref in work:
            columns = slice(at * gates, (at + 1) * gates)
            own = slice(at * hidden, (at + 1) * hidden)
            state = state_ref[:, own]
            state_low = state.astype(jnp.bfloat16)
            prev_ref[0] = state_low
            inputs = product(slot_ref[0], gin_ref[:, columns]) + sin_ref[:, columns]
            turned = product(state_low, ghid_ref[:, columns]) + shid_ref[:, columns]
            reset = logistic(inputs[:, :hidden] + turned[:, :hidden])
            update = logistic(
                inputs[:, hidden : 2 * hidden] + turned[:, hidden : 2 * hidden]
            )
            turned_new = turned[:, 2 * hidden :]
            fresh = jnp.tanh(inputs[:, 2 * hidden :] + reset * turned_new)
            gates_ref[0, :, :hidden] = reset.astype(jnp.bfloat16)
            gates_ref[0, :, hidden : 2 * hidden] = update.astype(jnp.bfloat16)
            gates_ref[0, :, 2 * hidden : 3 * hidden] = fresh.astype(jnp.bfloat16)
            gates_ref[0, :, 3 * hidden :] = turned_new.astype(jnp.bfloat16)
            moved = (1.0 - update) * fresh + update * state
            state_ref[:, own] = jnp.where(slot < counts_in, moved, state)

        @pl.when(step == last_slot)
        def _():
            last_ref[...] = state_ref[...]

    ahead = lambda i: (i, 0, 0)
    behind = lambda i: (last_slot - i, 0, 0)
    fixed = lambda i: (0, 0)
    low = jnp.bfloat16
    return pl.pallas_call(
        body,
        grid=(letter_slots,),
        in_specs=[
            pl.BlockSpec((1, rows, width), ahead),
            pl.BlockSpec((1, rows, width), behind),
            pl.BlockSpec(gin.shape, fixed),
            pl.BlockSpec(ghid.shape, fixed),
            pl.BlockSpec((1, 2 * gates), fixed),
            pl.BlockSpec((1, 2 * gates), fixed),
            pl.BlockSpec((rows, 1), fixed),
        ],
        out_specs=[
            pl.BlockSpec((1, rows, 4 * hidden), ahead),
            pl.BlockSpec((1, rows, 4 * hidden), behind),
            pl.BlockSpec((1, rows, hidden), ahead),
            pl.BlockSpec((1, rows, hidden), behind),
            pl.BlockSpec((rows, 2 * hidden), fixed),
        ],
        out_shape=[
            jax.ShapeDtypeStruct((letter_slots, rows, 4 * hidden), low),
            jax.ShapeDtypeStruct((letter_slots, rows, 4 * hidden), low),
            jax.ShapeDtypeStruct((letter_slots, rows, hidden), low),
            jax.ShapeDtypeStruct((letter_slots, rows, hidden), low),
            jax.ShapeDtypeStruct((rows, 2 * hidden), jnp.float32),
        ],
        scratch_shapes=[pltpu.VMEM((rows, 2 * hidden), jnp.float32)],
        name="recurrent_forward",
    )(slots, slots, gin, ghid, sin, shid, counts)


def recurrent_backward(saved_gates, saved_states, ghid, counts, delta):
    letter_slots, rows, _ = saved_gates[0].shape
    hidden = ghid.shape[0]
    gates = 3 * hidden
    last_slot = letter_slots - 1

    def body(
        gates_ahead,
        gates_behind,
        prev_ahead,
        prev_behind,
        ghid_ref,
        counts_ref,
        delta_ref,
        inputs_ahead,
        inputs_behind,
        turned_ahead,
        turned_behind,
        inputs_sum,
        turned_sum,
        carry_ref,
    ):
        step = pl.program_id(0)

        @pl.when(step == 0)
        def _():
            carry_ref[...] = delta_ref[...]
            inputs_sum[...] = jnp.zeros_like(inputs_sum)
            turned_sum[...] = jnp.zeros_like(turned_sum)

        counts_in = counts_ref[...]
        work = (
            (0, last_slot - step, gates_ahead, prev_ahead, inputs_ahead, turned_ahead),
            (1, step, gates_behind, prev_behind, inputs_behind, turned_behind),
        )
        for at, slot, gates_ref, prev_ref, inputs_ref, turned_ref in work:
            start = at * gates
            own = slice(at * hidden, (at + 1) * hidden)
            reset = gates_ref[0, :, :hidden].astype(jnp.float32)
            update = gates_ref[0, :, hidden : 2 * hidden].astype(jnp.float32)
            fresh = gates_ref[0, :, 2 * hidden : 3 * hidden].astype(jnp.float32)
            turned_new = gates_ref[0, :, 3 * hidden :].astype(jnp.float32)
            state = prev_ref[0].astype(jnp.float32)
            carry = carry_ref[:, own]
            active = slot < counts_in
            moved = jnp.where(active, carry, 0.0)
            delta_fresh = moved * (1.0 - update) * (1.0 - fresh * fresh)
            delta_update = moved * (state - fresh) * update * (1.0 - update)
            delta_reset = delta_fresh * turned_new * reset * (1.0 - reset)
            low_reset = delta_reset.astype(jnp.bfloat16)
            low_update = delta_update.astype(jnp.bfloat16)
            low_fresh = delta_fresh.astype(jnp.bfloat16)
            low_turned = (delta_fresh * reset).astype(jnp.bfloat16)
            inputs_ref[0, :, :hidden] = low_reset
            inputs_ref[0, :, hidden : 2 * hidden] = low_update
            inputs_ref[0, :, 2 * hidden :] = low_fresh
            turned_ref[0, :, :hidden] = low_reset
            turned_ref[0, :, hidden : 2 * hidden] = low_update
            turned_ref[0, :, 2 * hidden :] = low_turned
            through = right_product(turned_ref[0], ghid_ref[:, start : start + gates])
            carry_ref[:, own] = jnp.where(active, moved * update, carry) + through
            sums = [
                jnp.sum(part.astype(jnp.float32), axis=0, keepdims=True)
                for part in (low_reset, low_update, low_fresh, low_turned)
            ]
            for place_at, (first, second) in enumerate(
                ((sums[0], sums[0]), (sums[1], sums[1]), (sums[2], sums[3]))
            ):
                columns = slice(start + place_at * hidden, start + (place_at + 1) * hidden)
                inputs_sum[:, columns] += first
                turned_sum[:, columns] += second

    ahead = lambda i: (last_slot - i, 0, 0)
    behind = lambda i: (i, 0, 0)
    fixed = lambda i: (0, 0)
    low = jnp.bfloat16
    return pl.pallas_call(
        body,
        grid=(letter_slots,),
        in_specs=[
            pl.BlockSpec((1, rows, 4 * hidden), ahead),
            pl.BlockSpec((1, rows, 4 * hidden), behind),
            pl.BlockSpec((1, rows, hidden), ahead),
            pl.BlockSpec((1, rows, hidden), behind),
            pl.BlockSpec(ghid.shape, fixed),
            pl.BlockSpec((rows, 1), fixed),
            pl.BlockSpec((rows, 2 * hidden), fixed),
        ],
        out_specs=[
            pl.BlockSpec((1, rows, gates), ahead),
            pl.BlockSpec((1, rows, gates), behind),
            pl.BlockSpec((1, rows, gates), ahead),
            pl.BlockSpec((1, rows, gates), behind),
            pl.BlockSpec((1, 2 * gates), fixed),
            pl.BlockSpec((1, 2 * gates), fixed),
        ],
        out_shape=[
            jax.ShapeDtypeStruct((letter_slots, rows, gates), low),
            jax.ShapeDtypeStruct((letter_slots, rows, gates), low),
            jax.ShapeDtypeStruct((letter_slots, rows, gates), low),
            jax.ShapeDtypeStruct((letter_slots, rows, gates), low),
            jax.ShapeDtypeStruct((1, 2 * gates), jnp.float32),
            jax.ShapeDtypeStruct((1, 2 * gates), jnp.float32),
        ],
        scratch_shapes=[pltpu.VMEM((rows, 2 * hidden), jnp.float32)],
        name="recurrent_backward",
    )(*saved_gates, *saved_states, ghid, counts, delta)


DEPTH_SIZE = 4


class Place:
    def __init__(self):
        self.rep_size = lax.axis_size("rep")
        self.shard_size = lax.axis_size("shard")
        self.depth = DEPTH_SIZE
        self.height = self.shard_size // DEPTH_SIZE
        rep_at = lax.axis_index("rep")
        shard_at = lax.axis_index("shard")
        self.shard_at = shard_at
        self.core = rep_at % 2
        self.side = (rep_at // 2) % 2
        self.row = shard_at % self.height
        self.layer = shard_at // self.height
        self.coords = jnp.stack([self.layer, self.row, self.side, self.core]).astype(jnp.int32)

    def over_core(self, value):
        return lax.ppermute(value, "rep", [(i, i ^ 1) for i in range(self.rep_size)])

    def over_side(self, value):
        return lax.ppermute(value, "rep", [(i, i ^ 2) for i in range(self.rep_size)])

    def over_far(self, value, step):
        return lax.ppermute(
            value, "rep", [(i, (i + 4 * step) % self.rep_size) for i in range(self.rep_size)]
        )

    def over_row(self, value, step):
        return lax.ppermute(value, "shard", [(i, i ^ step) for i in range(self.shard_size)])

    def over_layer(self, value, step):
        return lax.ppermute(
            value, "shard", [(i, i ^ (step * self.height)) for i in range(self.shard_size)]
        )


def put_together(place, parts, rows, half, split):
    depth = place.depth
    flat = [part for group in parts for inner in group for part in inner]
    slots = [
        (core_slot, side_slot, row_slot)
        for core_slot in range(2)
        for side_slot in range(len(parts[0]))
        for row_slot in range(len(parts[0][0]))
    ]
    height = place.height
    pieces = 2 if split else 1
    part_rows = [r // pieces for r in rows]
    starts = [sum(part_rows[:i]) for i in range(len(rows))]

    def body(coords_ref, *refs):
        ins = refs[: len(flat)]
        outs = refs[len(flat) : len(flat) + len(rows)]
        sems = refs[-1]
        layer, row, side, core = (coords_ref[i] for i in range(4))
        copies = []
        for at, (core_slot, side_slot, row_slot) in enumerate(slots):
            for layer_slot in range(depth):
                block = (layer ^ layer_slot) * height + (row ^ row_slot)
                if split:
                    block = block * 2 + (side ^ side_slot)
                column = pl.multiple_of((core ^ core_slot) * half, 128)
                for out_ref, start, count in zip(outs, starts, part_rows):
                    copies.append(
                        pltpu.make_async_copy(
                            ins[at].at[layer_slot, pl.ds(start, count), :],
                            out_ref.at[block, :, pl.ds(column, half)],
                            sems.at[len(copies)],
                        )
                    )
        for copy in copies:
            copy.start()
        for copy in copies:
            copy.wait()

    blocks = depth * height * pieces
    whole = pl.pallas_call(
        body,
        out_shape=[
            jax.ShapeDtypeStruct((blocks, count, 2 * half), flat[0].dtype) for count in part_rows
        ],
        in_specs=[pl.BlockSpec(memory_space=pltpu.SMEM)]
        + [pl.BlockSpec(memory_space=pl.ANY)] * len(flat),
        out_specs=[pl.BlockSpec(memory_space=pltpu.VMEM)] * len(rows),
        scratch_shapes=[pltpu.SemaphoreType.DMA((len(flat) * depth * len(rows),))],
        name="put_together",
    )(place.coords, *flat)
    return [w.reshape(r * place.shard_size, 2 * half) for w, r in zip(whole, rows)]


def gathered(place, shards_in, split, after=None):
    half = shards_in[0].shape[1] // 2
    pieces = []
    for shard in shards_in:
        part_rows = shard.shape[0] // 2 if split else shard.shape[0]
        top = place.side * part_rows if split else 0
        pieces.append(lax.dynamic_slice(shard, (top, place.core * half), (part_rows, half)))
    piece = pieces[0] if len(pieces) == 1 else jnp.concatenate(pieces, axis=0)
    if after is not None:
        piece = hold(piece, after)
    layers = jnp.stack(
        [piece] + [place.over_layer(piece, step) for step in range(1, place.depth)]
    )
    column = [layers] + [place.over_row(layers, step) for step in range(1, place.height)]
    sides = [column]
    if split:
        sides.append([place.over_side(part) for part in column])
    cores = [sides, [[place.over_core(part) for part in group] for group in sides]]
    return put_together(place, cores, [shard.shape[0] for shard in shards_in], half, split), layers


def hold(value, *others):
    return lax.optimization_barrier((value, *others))[0]


def pick(value, at, axis):
    return lax.dynamic_index_in_dim(value, at, axis, keepdims=False)


def widen(value):
    return value.astype(jnp.float32)


def narrow(value):
    return value.astype(jnp.bfloat16)


def core_sum(place, inputs, delta):
    half = delta.shape[1] // 2

    def half_of(at):
        return left_product(inputs, lax.dynamic_slice_in_dim(delta, at * half, half, axis=1))

    sent = narrow(half_of(1 - place.core))
    return narrow(half_of(place.core) + widen(place.over_core(sent))), sent


def core_sum_of_pair(place, first, second):
    first, second = narrow(first), narrow(second)
    sent = jnp.where(place.core == 0, second, first)
    other = place.over_core(sent)
    return narrow(widen(jnp.where(place.core == 0, first, second)) + widen(other)), sent


def owned_sums(place, helds, split):
    stages = [[], [], []]
    half = helds[0].shape[1]
    pieces = 2 if split else 1
    parts = [h.shape[0] // place.shard_size // pieces for h in helds]
    blocks = [h.reshape(place.shard_size, pieces, p, half) for h, p in zip(helds, parts)]
    if split:
        kept = []
        for block in blocks:
            sent = pick(block, 1 - place.side, 1)
            stages[0].append(sent)
            other = place.over_side(sent)
            kept.append(narrow(widen(pick(block, place.side, 1)) + widen(other)))
    else:
        kept = [block[:, 0] for block in blocks]
    shape = (place.depth, place.height)
    kept = [k.reshape(shape + k.shape[1:]) for k in kept]

    def stacked(values):
        return values[0] if len(values) == 1 else jnp.concatenate(values, axis=-2)

    total = widen(stacked([pick(k, place.row, 1) for k in kept]))
    for step in range(1, place.height):
        sent = stacked([pick(k, place.row ^ step, 1) for k in kept])
        stages[1].append(sent)
        total = total + widen(place.over_row(sent, step))
    held = narrow(total)
    total = widen(pick(held, place.layer, 0))
    for step in range(1, place.depth):
        sent = pick(held, place.layer ^ step, 0)
        stages[2].append(sent)
        total = total + widen(place.over_layer(sent, step))
    held = narrow(total)
    for step in range(1, place.rep_size // 4):
        total = total + widen(place.over_far(held, step))
    held = narrow(total)
    other = place.over_side(held)
    if split:
        low_side = jnp.where(place.side == 0, held, other)
        high_side = jnp.where(place.side == 0, other, held)
        rows, start = [], 0
        for p in parts:
            rows += [low_side[start : start + p], high_side[start : start + p]]
            start += p
        held = jnp.concatenate(rows, axis=0)
    else:
        held = narrow(widen(held) + widen(other))
    other = place.over_core(held)
    first = jnp.where(place.core == 0, held, other)
    last = jnp.where(place.core == 0, other, held)
    results, start = [], 0
    for p in parts:
        own = slice(start, start + p * pieces)
        results.append(widen(jnp.concatenate([first[own], last[own]], axis=1)))
        start += p * pieces
    return results, stages


def gathered_vectors(place, vectors, after):
    flat = [v.reshape(-1) for v in vectors]
    flat[0] = hold(flat[0], after)
    packed = jnp.concatenate(flat)[None, :]
    layers = jnp.concatenate(
        [packed] + [place.over_layer(packed, step) for step in range(1, place.depth)], axis=0
    )
    slots = jnp.stack(
        [layers] + [place.over_row(layers, step) for step in range(1, place.height)], axis=1
    ).reshape(place.shard_size, -1)
    order = jnp.arange(place.shard_size)
    slot_of = ((order // place.height) ^ place.layer) * place.height + (
        (order % place.height) ^ place.row
    )
    ordered = jnp.take(slots, slot_of, axis=0, mode="clip").astype(jnp.float32)
    whole, start = [], 0
    for v in vectors:
        width = v.size
        part = ordered[:, start : start + width]
        if v.ndim == 1:
            whole.append(part.reshape(-1))
        else:
            lead, inner = v.shape
            whole.append(
                part.reshape(place.shard_size, lead, inner).transpose(1, 0, 2).reshape(lead, -1)
            )
        start += width
    return whole


def owned_vectors(place, vectors):
    count = place.shard_size
    rows = []
    for v in vectors:
        if v.ndim == 1:
            rows.append(v.reshape(count, -1))
        else:
            lead = v.shape[0]
            rows.append(v.reshape(lead, count, -1).transpose(1, 0, 2).reshape(count, -1))
    total = jnp.concatenate(rows, axis=1)
    total = total + place.over_core(total)
    total = total + place.over_side(total)
    base = total
    for step in range(1, place.rep_size // 4):
        total = total + place.over_far(base, step)
    span = 1
    while span < place.height:
        total = total + place.over_row(total, span)
        span *= 2
    span = 1
    while span < place.depth:
        total = total + place.over_layer(total, span)
        span *= 2
    own = lax.dynamic_index_in_dim(total, place.shard_at, 0, keepdims=False)
    parts, start = [], 0
    for v in vectors:
        width = v.size // count
        part = own[start : start + width]
        parts.append(part if v.ndim == 1 else part.reshape(v.shape[0], -1))
        start += width
    return parts


def shards(
    tokens,
    letters,
    lengths,
    counts,
    cot_token,
    cot_letter,
    project_weight,
    project_bias,
    output_weight,
    output_bias,
    first_gain,
    first_shift,
    up_weight,
    up_bias,
    down_weight,
    down_bias,
    second_gain,
    second_shift,
    gates_input,
    gates_hidden,
    shift_input,
    shift_hidden,
    token_mixer,
    token_offset,
    letter_mixer,
    letter_offset,
    window_kernel,
    window_offset,
    third_gain,
    third_shift,
    fourth_gain,
    fourth_shift,
):
    place = Place()
    seq_rows, model_width = tokens.shape
    letter_slots = letters.shape[1]
    head_width = model_width // HEADS
    score_scale = float(head_width) ** (-0.5)
    row_valid = jnp.arange(seq_rows) < lengths[0]
    row_mask = row_valid.astype(jnp.float32)[:, None]
    key_valid = row_valid[None, None, :]
    letter_flat = letters.transpose(1, 0, 2).reshape(letter_slots * seq_rows, model_width)

    side_by_side = lambda w: jnp.concatenate([w[i] for i in range(w.shape[0])], axis=1)
    (full_gin, full_project), first_layers = gathered(
        place, (side_by_side(gates_input), project_weight), True
    )
    (full_ghid,), second_layers = gathered(place, (side_by_side(gates_hidden),), False)
    window = side_by_side(window_kernel)
    window_half = window.shape[1] // 2
    (kernel_one,), third_layers = gathered(place, (window[:, :window_half],), True, first_layers)
    (full_output, full_down), fourth_layers = gathered(
        place, (output_weight, down_weight), False, second_layers
    )
    (full_up,), fifth_layers = gathered(place, (up_weight,), False, third_layers)
    (kernel_two,), sixth_layers = gathered(
        place, (window[:, window_half:],), True, fourth_layers
    )
    (full_tmix, full_lmix), _ = gathered(
        place, (token_mixer, letter_mixer), False, fifth_layers
    )
    (
        full_pbias,
        full_obias,
        gain_one,
        shift_one,
        full_ubias,
        full_dbias,
        gain_two,
        shift_two,
        full_sin,
        full_shid,
        full_toff,
        full_loff,
        full_koff,
        gain_three,
        shift_three,
        gain_four,
        shift_four,
    ) = gathered_vectors(
        place,
        (
            project_bias,
            output_bias,
            first_gain,
            first_shift,
            up_bias,
            down_bias,
            second_gain,
            second_shift,
            shift_input,
            shift_hidden,
            token_offset,
            letter_offset,
            window_offset,
            third_gain,
            third_shift,
            fourth_gain,
            fourth_shift,
        ),
        first_layers,
    )

    bias_full = jnp.concatenate(
        [full_pbias[:model_width], jnp.zeros((model_width,), jnp.float32), full_pbias[model_width:]]
    )
    mixed = (product(tokens, full_project) + bias_full).astype(jnp.bfloat16)
    queries = mixed[:, :model_width].reshape(seq_rows, HEADS, head_width)
    key_rows = mixed[:, model_width : 2 * model_width].reshape(seq_rows, HEADS, head_width)
    value_rows = mixed[:, 2 * model_width :].reshape(seq_rows, HEADS, head_width)

    def masked_scores_of(query_part, key_part):
        raw_scores = (
            jnp.einsum("qhd,khd->hqk", query_part, key_part, preferred_element_type=jnp.float32)
            * score_scale
        )
        return jnp.where(key_valid, raw_scores, -1e30)

    masked_scores = masked_scores_of(queries, key_rows)
    row_peak = jnp.max(masked_scores, axis=-1, keepdims=True)
    log_total = row_peak + jnp.log(
        jnp.sum(jnp.exp(masked_scores - row_peak), axis=-1, keepdims=True)
    )
    probabilities = jnp.exp(masked_scores - log_total)
    probs_low = probabilities.astype(jnp.bfloat16)
    context = (
        jnp.einsum("hqk,khd->qhd", probs_low, value_rows, preferred_element_type=jnp.float32)
        .astype(jnp.bfloat16)
        .reshape(seq_rows, model_width)
    )
    attended = product(context, full_output) + full_obias
    residual_one = tokens.astype(jnp.float32) + attended
    first = normalize(residual_one, gain_one, shift_one)
    first_low = first.astype(jnp.bfloat16)
    upper = product(first_low, full_up) + full_ubias
    activated, slope_upper = gelu_and_slope(upper)
    activated = activated.astype(jnp.bfloat16)
    residual_two = first + product(activated, full_down) + full_dbias
    second = normalize(residual_two, gain_two, shift_two)
    hidden_width = full_ghid.shape[0]
    gates_width = 3 * hidden_width
    counts_column = counts.reshape(-1, 1)
    gates_ahead, gates_behind, prev_ahead, prev_behind, pooled = recurrent_forward(
        letter_flat.reshape(letter_slots, seq_rows, model_width),
        full_gin,
        full_ghid,
        full_sin.reshape(1, -1),
        full_shid.reshape(1, -1),
        counts_column,
    )
    second_low = second.astype(jnp.bfloat16)
    pooled_low = pooled.astype(jnp.bfloat16)
    token_side = product(second_low, full_tmix) + full_toff
    letter_side = product(pooled_low, full_lmix) + full_loff
    joined = (jnp.concatenate([token_side, letter_side], axis=-1) * row_mask).astype(jnp.bfloat16)
    joined_width = joined.shape[1]
    taps_one = product(joined, kernel_one)
    taps_two = product(joined, kernel_two)
    rest = window_half - joined_width
    convolved = (
        jnp.pad(taps_one[:-1, :joined_width], ((1, 0), (0, 0)))
        + jnp.concatenate([taps_one[:, joined_width:], taps_two[:, :rest]], axis=1)
        + jnp.pad(taps_two[1:, rest:], ((0, 1), (0, 0)))
        + full_koff
    )
    widened, slope_conv = gelu_and_slope(convolved)
    residual_three = second + widened[:, :model_width]
    residual_four = pooled + widened[:, model_width:]
    token_out = normalize(residual_three, gain_three, shift_three) * row_mask
    letter_out = normalize(residual_four, gain_four, shift_four) * row_mask

    out_token_delta = cot_token.astype(jnp.float32) * row_mask
    out_letter_delta = cot_letter.astype(jnp.float32) * row_mask
    unused_three, pull_three = jax.vjp(normalize, residual_three, gain_three, shift_three)
    delta_three, delta_gain_three, delta_shift_three = pull_three(out_token_delta)
    unused_four, pull_four = jax.vjp(normalize, residual_four, gain_four, shift_four)
    delta_four, delta_gain_four, delta_shift_four = pull_four(out_letter_delta)
    delta_conv = (jnp.concatenate([delta_three, delta_four], axis=-1) * slope_conv).astype(
        jnp.bfloat16
    )
    delta_koff = column_sum(delta_conv)
    delta_taps = jnp.concatenate(
        [
            jnp.pad(delta_conv[1:], ((0, 1), (0, 0))),
            delta_conv,
            jnp.pad(delta_conv[:-1], ((1, 0), (0, 0))),
        ],
        axis=1,
    )
    taps_low, taps_high = delta_taps[:, :window_half], delta_taps[:, window_half:]
    one_sum, one_sent = core_sum(place, joined, taps_low)
    two_sum, two_sent = core_sum(place, joined, taps_high)
    (kernel_one_grad,), one_stages = owned_sums(place, (one_sum,), True)
    (kernel_two_grad,), two_stages = owned_sums(place, (two_sum,), True)
    kernel_grad = jnp.concatenate([kernel_one_grad, kernel_two_grad], axis=1)
    taps_low = hold(taps_low, one_sent, two_sent)
    delta_joined = (
        right_product(taps_low, kernel_one) + right_product(taps_high, kernel_two)
    ) * row_mask
    delta_tside = delta_joined[:, :model_width].astype(jnp.bfloat16)
    delta_lside = delta_joined[:, model_width:].astype(jnp.bfloat16)
    tmix_sum, tmix_sent = core_sum(place, second_low, delta_tside)
    delta_toff = column_sum(delta_tside)
    lmix_sum, lmix_sent = core_sum(place, pooled_low, delta_lside)
    delta_loff = column_sum(delta_lside)
    delta_second = delta_three + right_product(delta_tside, full_tmix)
    delta_pooled = delta_four + right_product(delta_lside, full_lmix)

    delta_pooled = hold(delta_pooled, *one_stages[0], *two_stages[0], tmix_sent, lmix_sent)
    inputs_ahead, inputs_behind, turned_ahead, turned_behind, sin_delta, shid_delta = (
        recurrent_backward(
            (gates_ahead, gates_behind),
            (prev_ahead, prev_behind),
            full_ghid,
            counts_column,
            delta_pooled,
        )
    )
    flat_rows = lambda v: v.reshape(letter_slots * seq_rows, -1)
    inputs_ahead, inputs_behind = flat_rows(inputs_ahead), flat_rows(inputs_behind)
    gin_sum, gin_sent = core_sum_of_pair(
        place,
        left_product(letter_flat, inputs_ahead),
        left_product(letter_flat, inputs_behind),
    )
    ghid_sum, ghid_sent = core_sum_of_pair(
        place,
        left_product(flat_rows(prev_ahead), flat_rows(turned_ahead)),
        left_product(flat_rows(prev_behind), flat_rows(turned_behind)),
    )
    inputs_ahead = hold(inputs_ahead, gin_sent, ghid_sent)
    letters_grad = (
        (
            right_product(inputs_ahead, full_gin[:, :gates_width])
            + right_product(inputs_behind, full_gin[:, gates_width:])
        )
        .astype(jnp.bfloat16)
        .reshape(letter_slots, seq_rows, model_width)
        .transpose(1, 0, 2)
    )
    sin_delta = sin_delta.reshape(2, -1)
    shid_delta = shid_delta.reshape(2, -1)
    in_pair = lambda v: jnp.stack([v[:, :gates_width], v[:, gates_width:]])
    (ghid_grad,), ghid_stages = owned_sums(place, (ghid_sum,), False)
    (gin_grad,), gin_stages = owned_sums(place, (gin_sum,), True)
    delta_second = hold(delta_second, *gin_stages[0], *one_stages[1], *ghid_stages[1], letters_grad)
    ghid_grad, gin_grad = in_pair(ghid_grad), in_pair(gin_grad)

    unused_two, pull_two = jax.vjp(normalize, residual_two, gain_two, shift_two)
    delta_two, delta_gain_two, delta_shift_two = pull_two(delta_second)
    delta_lowered = delta_two.astype(jnp.bfloat16)
    down_sum, down_sent = core_sum(place, activated, delta_lowered)
    (tmix_grad, lmix_grad, down_grad), down_stages = owned_sums(
        place, (tmix_sum, lmix_sum, down_sum), False
    )
    delta_lowered = hold(delta_lowered, down_sent)
    delta_dbias = column_sum(delta_lowered)
    delta_upper = (right_product(delta_lowered, full_down) * slope_upper).astype(jnp.bfloat16)
    up_sum, up_sent = core_sum(place, first_low, delta_upper)
    (up_grad,), up_stages = owned_sums(place, (up_sum,), False)
    delta_upper = hold(delta_upper, up_sent, *two_stages[1], *down_stages[1])
    delta_ubias = column_sum(delta_upper)
    delta_first = delta_two + right_product(delta_upper, full_up)
    unused_one, pull_one = jax.vjp(normalize, residual_one, gain_one, shift_one)
    delta_one, delta_gain_one, delta_shift_one = pull_one(delta_first)
    delta_attended = delta_one.astype(jnp.bfloat16)
    output_sum, output_sent = core_sum(place, context, delta_attended)
    (output_grad,), output_stages = owned_sums(place, (output_sum,), False)
    delta_attended = hold(delta_attended, output_sent, *up_stages[1], *one_stages[2], *gin_stages[1])
    delta_obias = column_sum(delta_attended)
    delta_context = (
        right_product(delta_attended, full_output)
        .astype(jnp.bfloat16)
        .reshape(seq_rows, HEADS, head_width)
    )
    delta_values = jnp.einsum(
        "hqk,qhd->khd",
        probs_low,
        delta_context,
        preferred_element_type=jnp.float32,
    )
    delta_probs = jnp.einsum(
        "qhd,khd->hqk", delta_context, value_rows, preferred_element_type=jnp.float32
    )
    delta_scores = (
        probabilities * (delta_probs - jnp.sum(probabilities * delta_probs, axis=-1, keepdims=True))
    ).astype(jnp.bfloat16)
    delta_queries = (
        jnp.einsum("hqk,khd->qhd", delta_scores, key_rows, preferred_element_type=jnp.float32)
        * score_scale
    )
    delta_keys = (
        jnp.einsum("hqk,qhd->khd", delta_scores, queries, preferred_element_type=jnp.float32)
        * score_scale
    )
    delta_mixed = jnp.concatenate(
        [
            delta_queries.reshape(seq_rows, model_width),
            delta_keys.reshape(seq_rows, model_width),
            delta_values.reshape(seq_rows, model_width),
        ],
        axis=-1,
    ).astype(jnp.bfloat16)
    project_sum, project_sent = core_sum(place, tokens, delta_mixed)
    (project_grad,), _ = owned_sums(place, (project_sum,), True)
    delta_mixed_sum = column_sum(delta_mixed)
    delta_pbias = jnp.concatenate(
        [delta_mixed_sum[:model_width], delta_mixed_sum[2 * model_width :]]
    )
    tokens_grad = (delta_one + right_product(delta_mixed, full_project)).astype(jnp.bfloat16)
    (
        pbias_grad,
        obias_grad,
        gain_one_grad,
        shift_one_grad,
        ubias_grad,
        dbias_grad,
        gain_two_grad,
        shift_two_grad,
        sin_grad,
        shid_grad,
        toff_grad,
        loff_grad,
        koff_grad,
        gain_three_grad,
        shift_three_grad,
        gain_four_grad,
        shift_four_grad,
    ) = owned_vectors(
        place,
        (
            delta_pbias,
            delta_obias,
            delta_gain_one,
            delta_shift_one,
            delta_ubias,
            delta_dbias,
            delta_gain_two,
            delta_shift_two,
            sin_delta,
            shid_delta,
            delta_toff,
            delta_loff,
            delta_koff,
            delta_gain_three,
            delta_shift_three,
            delta_gain_four,
            delta_shift_four,
        ),
    )
    taps_grad = jnp.stack(
        [kernel_grad[:, t * joined_width : (t + 1) * joined_width] for t in range(3)]
    )
    return (
        token_out.astype(jnp.bfloat16),
        letter_out.astype(jnp.bfloat16),
        tokens_grad,
        letters_grad,
        project_grad,
        pbias_grad,
        output_grad,
        obias_grad,
        gain_one_grad,
        shift_one_grad,
        up_grad,
        ubias_grad,
        down_grad,
        dbias_grad,
        gain_two_grad,
        shift_two_grad,
        gin_grad,
        ghid_grad,
        sin_grad,
        shid_grad,
        tmix_grad,
        toff_grad,
        lmix_grad,
        loff_grad,
        taps_grad,
        koff_grad,
        gain_three_grad,
        shift_three_grad,
        gain_four_grad,
        shift_four_grad,
    )


def solution(mesh):
    placed = (
        P(("rep", "shard"), None),
        P(("rep", "shard"), None, None),
        P(("rep", "shard")),
        P(("rep", "shard")),
        P(("rep", "shard"), None),
        P(("rep", "shard"), None),
        P("shard", None),
        P("shard"),
        P("shard", None),
        P("shard"),
        P("shard"),
        P("shard"),
        P("shard", None),
        P("shard"),
        P("shard", None),
        P("shard"),
        P("shard"),
        P("shard"),
        P(None, "shard", None),
        P(None, "shard", None),
        P(None, "shard"),
        P(None, "shard"),
        P("shard", None),
        P("shard"),
        P("shard", None),
        P("shard"),
        P(None, "shard", None),
        P("shard"),
        P("shard"),
        P("shard"),
        P("shard"),
        P("shard"),
    )
    return jax.shard_map(
        shards,
        mesh=mesh,
        in_specs=placed,
        out_specs=(
            P(("rep", "shard"), None),
            P(("rep", "shard"), None),
            P(("rep", "shard"), None),
            P(("rep", "shard"), None, None),
            P("shard", None),
            P("shard"),
            P("shard", None),
            P("shard"),
            P("shard"),
            P("shard"),
            P("shard", None),
            P("shard"),
            P("shard", None),
            P("shard"),
            P("shard"),
            P("shard"),
            P(None, "shard", None),
            P(None, "shard", None),
            P(None, "shard"),
            P(None, "shard"),
            P("shard", None),
            P("shard"),
            P("shard", None),
            P("shard"),
            P(None, "shard", None),
            P("shard"),
            P("shard"),
            P("shard"),
            P("shard"),
            P("shard"),
        ),
        check_vma=False,
    )
```

```python
import jax
import jax.numpy as jnp
from jax import lax
from jax.experimental import pallas as pl
from jax.experimental.pallas import tpu as pltpu
from jax.sharding import PartitionSpec as P


HEADS = 12


EPS = 1e-05


def product(left, right):
    return jnp.dot(left, right, preferred_element_type=jnp.float32)


def left_product(left, right):
    return lax.dot_general(
        left, right, (((0,), (0,)), ((), ())), preferred_element_type=jnp.float32
    )


def right_product(left, right):
    return lax.dot_general(
        left, right, (((1,), (1,)), ((), ())), preferred_element_type=jnp.float32
    )


def column_sum(values):
    return jnp.sum(values.astype(jnp.float32), axis=0)


def normalize(values, gain, shift):
    center = jnp.mean(values, axis=-1, keepdims=True)
    centered = values - center
    spread = jnp.mean(centered * centered, axis=-1, keepdims=True)
    return centered * lax.rsqrt(spread + EPS) * gain + shift


def gelu_and_slope(values):
    below = 0.5 + 0.5 * lax.erf(values * (0.5**0.5))
    density = jnp.exp(-0.5 * values * values) * ((2.0 * jnp.pi) ** -0.5)
    return values * below, below + values * density


def logistic(values):
    return 0.5 + 0.5 * jnp.tanh(0.5 * values)


def recurrent_forward(slots, gin, ghid, sin, shid, counts):
    letter_slots, rows, width = slots.shape
    hidden = ghid.shape[0]
    gates = 3 * hidden
    last_slot = letter_slots - 1

    def body(
        ahead_ref,
        behind_ref,
        gin_ref,
        ghid_ref,
        sin_ref,
        shid_ref,
        counts_ref,
        gates_ahead,
        gates_behind,
        prev_ahead,
        prev_behind,
        last_ref,
        state_ref,
    ):
        step = pl.program_id(0)

        @pl.when(step == 0)
        def _():
            state_ref[...] = jnp.zeros_like(state_ref)

        counts_in = counts_ref[...]
        work = (
            (0, ahead_ref, step, gates_ahead, prev_ahead),
            (1, behind_ref, last_slot - step, gates_behind, prev_behind),
        )
        for at, slot_ref, slot, gates_ref, prev_ref in work:
            columns = slice(at * gates, (at + 1) * gates)
            own = slice(at * hidden, (at + 1) * hidden)
            state = state_ref[:, own]
            state_low = state.astype(jnp.bfloat16)
            prev_ref[0] = state_low
            inputs = product(slot_ref[0], gin_ref[:, columns]) + sin_ref[:, columns]
            turned = product(state_low, ghid_ref[:, columns]) + shid_ref[:, columns]
            reset = logistic(inputs[:, :hidden] + turned[:, :hidden])
            update = logistic(
                inputs[:, hidden : 2 * hidden] + turned[:, hidden : 2 * hidden]
            )
            turned_new = turned[:, 2 * hidden :]
            fresh = jnp.tanh(inputs[:, 2 * hidden :] + reset * turned_new)
            gates_ref[0, :, :hidden] = reset.astype(jnp.bfloat16)
            gates_ref[0, :, hidden : 2 * hidden] = update.astype(jnp.bfloat16)
            gates_ref[0, :, 2 * hidden : 3 * hidden] = fresh.astype(jnp.bfloat16)
            gates_ref[0, :, 3 * hidden :] = turned_new.astype(jnp.bfloat16)
            moved = (1.0 - update) * fresh + update * state
            state_ref[:, own] = jnp.where(slot < counts_in, moved, state)

        @pl.when(step == last_slot)
        def _():
            last_ref[...] = state_ref[...]

    ahead = lambda i: (i, 0, 0)
    behind = lambda i: (last_slot - i, 0, 0)
    fixed = lambda i: (0, 0)
    low = jnp.bfloat16
    return pl.pallas_call(
        body,
        grid=(letter_slots,),
        in_specs=[
            pl.BlockSpec((1, rows, width), ahead),
            pl.BlockSpec((1, rows, width), behind),
            pl.BlockSpec(gin.shape, fixed),
            pl.BlockSpec(ghid.shape, fixed),
            pl.BlockSpec((1, 2 * gates), fixed),
            pl.BlockSpec((1, 2 * gates), fixed),
            pl.BlockSpec((rows, 1), fixed),
        ],
        out_specs=[
            pl.BlockSpec((1, rows, 4 * hidden), ahead),
            pl.BlockSpec((1, rows, 4 * hidden), behind),
            pl.BlockSpec((1, rows, hidden), ahead),
            pl.BlockSpec((1, rows, hidden), behind),
            pl.BlockSpec((rows, 2 * hidden), fixed),
        ],
        out_shape=[
            jax.ShapeDtypeStruct((letter_slots, rows, 4 * hidden), low),
            jax.ShapeDtypeStruct((letter_slots, rows, 4 * hidden), low),
            jax.ShapeDtypeStruct((letter_slots, rows, hidden), low),
            jax.ShapeDtypeStruct((letter_slots, rows, hidden), low),
            jax.ShapeDtypeStruct((rows, 2 * hidden), jnp.float32),
        ],
        scratch_shapes=[pltpu.VMEM((rows, 2 * hidden), jnp.float32)],
        name="recurrent_forward",
    )(slots, slots, gin, ghid, sin, shid, counts)


def recurrent_backward(saved_gates, saved_states, ghid, counts, delta):
    letter_slots, rows, _ = saved_gates[0].shape
    hidden = ghid.shape[0]
    gates = 3 * hidden
    last_slot = letter_slots - 1

    def body(
        gates_ahead,
        gates_behind,
        prev_ahead,
        prev_behind,
        ghid_ref,
        counts_ref,
        delta_ref,
        inputs_ahead,
        inputs_behind,
        turned_ahead,
        turned_behind,
        inputs_sum,
        turned_sum,
        carry_ref,
    ):
        step = pl.program_id(0)

        @pl.when(step == 0)
        def _():
            carry_ref[...] = delta_ref[...]
            inputs_sum[...] = jnp.zeros_like(inputs_sum)
            turned_sum[...] = jnp.zeros_like(turned_sum)

        counts_in = counts_ref[...]
        work = (
            (0, last_slot - step, gates_ahead, prev_ahead, inputs_ahead, turned_ahead),
            (1, step, gates_behind, prev_behind, inputs_behind, turned_behind),
        )
        for at, slot, gates_ref, prev_ref, inputs_ref, turned_ref in work:
            start = at * gates
            own = slice(at * hidden, (at + 1) * hidden)
            reset = gates_ref[0, :, :hidden].astype(jnp.float32)
            update = gates_ref[0, :, hidden : 2 * hidden].astype(jnp.float32)
            fresh = gates_ref[0, :, 2 * hidden : 3 * hidden].astype(jnp.float32)
            turned_new = gates_ref[0, :, 3 * hidden :].astype(jnp.float32)
            state = prev_ref[0].astype(jnp.float32)
            carry = carry_ref[:, own]
            active = slot < counts_in
            moved = jnp.where(active, carry, 0.0)
            delta_fresh = moved * (1.0 - update) * (1.0 - fresh * fresh)
            delta_update = moved * (state - fresh) * update * (1.0 - update)
            delta_reset = delta_fresh * turned_new * reset * (1.0 - reset)
            low_reset = delta_reset.astype(jnp.bfloat16)
            low_update = delta_update.astype(jnp.bfloat16)
            low_fresh = delta_fresh.astype(jnp.bfloat16)
            low_turned = (delta_fresh * reset).astype(jnp.bfloat16)
            inputs_ref[0, :, :hidden] = low_reset
            inputs_ref[0, :, hidden : 2 * hidden] = low_update
            inputs_ref[0, :, 2 * hidden :] = low_fresh
            turned_ref[0, :, :hidden] = low_reset
            turned_ref[0, :, hidden : 2 * hidden] = low_update
            turned_ref[0, :, 2 * hidden :] = low_turned
            through = right_product(turned_ref[0], ghid_ref[:, start : start + gates])
            carry_ref[:, own] = jnp.where(active, moved * update, carry) + through
            sums = [
                jnp.sum(part.astype(jnp.float32), axis=0, keepdims=True)
                for part in (low_reset, low_update, low_fresh, low_turned)
            ]
            for place_at, (first, second) in enumerate(
                ((sums[0], sums[0]), (sums[1], sums[1]), (sums[2], sums[3]))
            ):
                columns = slice(start + place_at * hidden, start + (place_at + 1) * hidden)
                inputs_sum[:, columns] += first
                turned_sum[:, columns] += second

    ahead = lambda i: (last_slot - i, 0, 0)
    behind = lambda i: (i, 0, 0)
    fixed = lambda i: (0, 0)
    low = jnp.bfloat16
    return pl.pallas_call(
        body,
        grid=(letter_slots,),
        in_specs=[
            pl.BlockSpec((1, rows, 4 * hidden), ahead),
            pl.BlockSpec((1, rows, 4 * hidden), behind),
            pl.BlockSpec((1, rows, hidden), ahead),
            pl.BlockSpec((1, rows, hidden), behind),
            pl.BlockSpec(ghid.shape, fixed),
            pl.BlockSpec((rows, 1), fixed),
            pl.BlockSpec((rows, 2 * hidden), fixed),
        ],
        out_specs=[
            pl.BlockSpec((1, rows, gates), ahead),
            pl.BlockSpec((1, rows, gates), behind),
            pl.BlockSpec((1, rows, gates), ahead),
            pl.BlockSpec((1, rows, gates), behind),
            pl.BlockSpec((1, 2 * gates), fixed),
            pl.BlockSpec((1, 2 * gates), fixed),
        ],
        out_shape=[
            jax.ShapeDtypeStruct((letter_slots, rows, gates), low),
            jax.ShapeDtypeStruct((letter_slots, rows, gates), low),
            jax.ShapeDtypeStruct((letter_slots, rows, gates), low),
            jax.ShapeDtypeStruct((letter_slots, rows, gates), low),
            jax.ShapeDtypeStruct((1, 2 * gates), jnp.float32),
            jax.ShapeDtypeStruct((1, 2 * gates), jnp.float32),
        ],
        scratch_shapes=[pltpu.VMEM((rows, 2 * hidden), jnp.float32)],
        name="recurrent_backward",
    )(*saved_gates, *saved_states, ghid, counts, delta)


DEPTH_SIZE = 4


def exchange(value, axis, pairs):
    return lax.ppermute(value, axis, pairs)


class Place:
    def __init__(self):
        self.rep_size = lax.axis_size("rep")
        self.shard_size = lax.axis_size("shard")
        self.depth = DEPTH_SIZE
        self.height = self.shard_size // DEPTH_SIZE
        rep_at = lax.axis_index("rep")
        shard_at = lax.axis_index("shard")
        self.shard_at = shard_at
        self.core = rep_at % 2
        self.side = (rep_at // 2) % 2
        self.row = shard_at % self.height
        self.layer = shard_at // self.height
        self.coords = jnp.stack([self.layer, self.row, self.side, self.core]).astype(jnp.int32)

    def over_core(self, value):
        return exchange(value, "rep", [(i, i ^ 1) for i in range(self.rep_size)])

    def over_side(self, value):
        return exchange(value, "rep", [(i, i ^ 2) for i in range(self.rep_size)])

    def over_far(self, value, step):
        return exchange(value, "rep", [(i, (i + 4 * step) % self.rep_size) for i in range(self.rep_size)]
        )

    def over_row(self, value, step):
        return exchange(value, "shard", [(i, i ^ step) for i in range(self.shard_size)])

    def over_layer(self, value, step):
        return exchange(value, "shard", [(i, i ^ (step * self.height)) for i in range(self.shard_size)]
        )


def put_together(place, parts, rows, half, split):
    depth = place.depth
    flat = [part for group in parts for inner in group for part in inner]
    slots = [
        (core_slot, side_slot, row_slot)
        for core_slot in range(2)
        for side_slot in range(len(parts[0]))
        for row_slot in range(len(parts[0][0]))
    ]
    height = place.height
    pieces = 2 if split else 1
    part_rows = [r // pieces for r in rows]
    starts = [sum(part_rows[:i]) for i in range(len(rows))]

    def body(coords_ref, *refs):
        ins = refs[: len(flat)]
        outs = refs[len(flat) : len(flat) + len(rows)]
        sems = refs[-1]
        layer, row, side, core = (coords_ref[i] for i in range(4))
        copies = []
        for at, (core_slot, side_slot, row_slot) in enumerate(slots):
            for layer_slot in range(depth):
                block = (layer ^ layer_slot) * height + (row ^ row_slot)
                if split:
                    block = block * 2 + (side ^ side_slot)
                column = pl.multiple_of((core ^ core_slot) * half, 128)
                for out_ref, start, count in zip(outs, starts, part_rows):
                    copies.append(
                        pltpu.make_async_copy(
                            ins[at].at[layer_slot, pl.ds(start, count), :],
                            out_ref.at[block, :, pl.ds(column, half)],
                            sems.at[len(copies)],
                        )
                    )
        for copy in copies:
            copy.start()
        for copy in copies:
            copy.wait()

    blocks = depth * height * pieces
    whole = pl.pallas_call(
        body,
        out_shape=[
            jax.ShapeDtypeStruct((blocks, count, 2 * half), flat[0].dtype) for count in part_rows
        ],
        in_specs=[pl.BlockSpec(memory_space=pltpu.SMEM)]
        + [pl.BlockSpec(memory_space=pl.ANY)] * len(flat),
        out_specs=[pl.BlockSpec(memory_space=pltpu.VMEM)] * len(rows),
        scratch_shapes=[pltpu.SemaphoreType.DMA((len(flat) * depth * len(rows),))],
        name="put_together",
    )(place.coords, *flat)
    return [w.reshape(r * place.shard_size, 2 * half) for w, r in zip(whole, rows)]


def gathered(place, shards_in, split, after=None):
    half = shards_in[0].shape[1] // 2
    pieces = []
    for shard in shards_in:
        part_rows = shard.shape[0] // 2 if split else shard.shape[0]
        top = place.side * part_rows if split else 0
        pieces.append(lax.dynamic_slice(shard, (top, place.core * half), (part_rows, half)))
    piece = pieces[0] if len(pieces) == 1 else jnp.concatenate(pieces, axis=0)
    if after is not None:
        piece = hold(piece, after)
    layers = jnp.stack([piece] + [place.over_layer(piece, step) for step in range(1, place.depth)])
    column = [layers] + [place.over_row(layers, step) for step in range(1, place.height)]
    sides = [column]
    if split:
        sides.append([place.over_side(part) for part in column])
    cores = [
        sides,
        [[place.over_core(part) for part in group] for group in sides],
    ]
    return put_together(place, cores, [shard.shape[0] for shard in shards_in], half, split), piece, layers


def hold(value, *others):
    return lax.optimization_barrier((value, *others))[0]


def pick(value, at, axis):
    return lax.dynamic_index_in_dim(value, at, axis, keepdims=False)


def widen(value):
    return value.astype(jnp.float32)


def narrow(value):
    return value.astype(jnp.bfloat16)


def core_sum(place, inputs, delta):
    half = delta.shape[1] // 2

    def half_of(at):
        return left_product(inputs, lax.dynamic_slice_in_dim(delta, at * half, half, axis=1))

    sent = half_of(1 - place.core)
    other = place.over_core(narrow(sent))
    return narrow(half_of(place.core) + widen(other))


def core_sum_of_pair(place, first, second):
    first, second = narrow(first), narrow(second)
    other = place.over_core(jnp.where(place.core == 0, second, first))
    return narrow(widen(jnp.where(place.core == 0, first, second)) + widen(other))


def summed(place, helds, split):
    half = helds[0].shape[1]
    pieces = 2 if split else 1
    parts = [h.shape[0] // place.shard_size // pieces for h in helds]
    blocks = [h.reshape(place.shard_size, pieces, p, half) for h, p in zip(helds, parts)]
    if split:
        kept = []
        for block in blocks:
            other = place.over_side(pick(block, 1 - place.side, 1))
            kept.append(narrow(widen(pick(block, place.side, 1)) + widen(other)))
    else:
        kept = [block[:, 0] for block in blocks]
    shape = (place.depth, place.height)
    kept = [k.reshape(shape + k.shape[1:]) for k in kept]

    def stacked(values):
        return values[0] if len(values) == 1 else jnp.concatenate(values, axis=-2)

    total = widen(stacked([pick(k, place.row, 1) for k in kept]))
    for step in range(1, place.height):
        sent = stacked([pick(k, place.row ^ step, 1) for k in kept])
        total = total + widen(place.over_row(sent, step))
    held = narrow(total)
    total = widen(pick(held, place.layer, 0))
    for step in range(1, place.depth):
        sent = pick(held, place.layer ^ step, 0)
        total = total + widen(place.over_layer(sent, step))
    return narrow(total), parts, split


def shared(place, pending, after=None):
    held, parts, split = pending
    pieces = 2 if split else 1
    if after is not None:
        held = hold(held, after)
    total = widen(held)
    for step in range(1, place.rep_size // 4):
        total = total + widen(place.over_far(held, step))
    held = narrow(total)
    other = place.over_side(held)
    if split:
        low_side = jnp.where(place.side == 0, held, other)
        high_side = jnp.where(place.side == 0, other, held)
        rows, start = [], 0
        for p in parts:
            rows += [low_side[start : start + p], high_side[start : start + p]]
            start += p
        held = jnp.concatenate(rows, axis=0)
    else:
        held = narrow(widen(held) + widen(other))
    other = place.over_core(held)
    first = jnp.where(place.core == 0, held, other)
    last = jnp.where(place.core == 0, other, held)
    results, start = [], 0
    for p in parts:
        own = slice(start, start + p * pieces)
        results.append(widen(jnp.concatenate([first[own], last[own]], axis=1)))
        start += p * pieces
    return results


def gathered_vectors(place, vectors, after):
    flat = [v.reshape(-1) for v in vectors]
    flat[0] = hold(flat[0], after)
    packed = jnp.concatenate(flat)[None, :]
    layers = jnp.concatenate(
        [packed] + [place.over_layer(packed, step) for step in range(1, place.depth)], axis=0
    )
    slots = jnp.stack(
        [layers] + [place.over_row(layers, step) for step in range(1, place.height)], axis=1
    ).reshape(place.shard_size, -1)
    order = jnp.arange(place.shard_size)
    slot_of = ((order // place.height) ^ place.layer) * place.height + (
        (order % place.height) ^ place.row
    )
    ordered = jnp.take(slots, slot_of, axis=0, mode="clip").astype(jnp.float32)
    whole, start = [], 0
    for v in vectors:
        width = v.size
        part = ordered[:, start : start + width]
        if v.ndim == 1:
            whole.append(part.reshape(-1))
        else:
            lead, inner = v.shape
            whole.append(
                part.reshape(place.shard_size, lead, inner).transpose(1, 0, 2).reshape(lead, -1)
            )
        start += width
    return whole


def owned_vectors(place, vectors):
    count = place.shard_size
    rows = []
    for v in vectors:
        if v.ndim == 1:
            rows.append(v.reshape(count, -1))
        else:
            lead = v.shape[0]
            rows.append(v.reshape(lead, count, -1).transpose(1, 0, 2).reshape(count, -1))
    total = jnp.concatenate(rows, axis=1)
    total = total + place.over_core(total)
    total = total + place.over_side(total)
    base = total
    for step in range(1, place.rep_size // 4):
        total = total + place.over_far(base, step)
    span = 1
    while span < place.height:
        total = total + place.over_row(total, span)
        span *= 2
    span = 1
    while span < place.depth:
        total = total + place.over_layer(total, span)
        span *= 2
    own = lax.dynamic_index_in_dim(total, place.shard_at, 0, keepdims=False)
    parts, start = [], 0
    for v in vectors:
        width = v.size // count
        part = own[start : start + width]
        parts.append(part if v.ndim == 1 else part.reshape(v.shape[0], -1))
        start += width
    return parts


def shards(
    tokens,
    letters,
    lengths,
    counts,
    cot_token,
    cot_letter,
    project_weight,
    project_bias,
    output_weight,
    output_bias,
    first_gain,
    first_shift,
    up_weight,
    up_bias,
    down_weight,
    down_bias,
    second_gain,
    second_shift,
    gates_input,
    gates_hidden,
    shift_input,
    shift_hidden,
    token_mixer,
    token_offset,
    letter_mixer,
    letter_offset,
    window_kernel,
    window_offset,
    third_gain,
    third_shift,
    fourth_gain,
    fourth_shift,
):
    place = Place()
    seq_rows, model_width = tokens.shape
    letter_slots = letters.shape[1]
    head_width = model_width // HEADS
    score_scale = float(head_width) ** (-0.5)
    row_valid = jnp.arange(seq_rows) < lengths[0]
    row_mask = row_valid.astype(jnp.float32)[:, None]
    key_valid = row_valid[None, None, :]
    letter_flat = letters.transpose(1, 0, 2).reshape(letter_slots * seq_rows, model_width)

    side_by_side = lambda w: jnp.concatenate([w[i] for i in range(w.shape[0])], axis=1)
    (full_gin, full_project), first_piece, first_layers = gathered(
        place, (side_by_side(gates_input), project_weight), True
    )
    (full_ghid,), _, second_layers = gathered(place, (side_by_side(gates_hidden),), False)
    window = side_by_side(window_kernel)
    window_half = window.shape[1] // 2
    (kernel_one,), _, third_layers = gathered(place, (window[:, :window_half],), True, first_layers)
    (full_output, full_down), _, fourth_layers = gathered(
        place, (output_weight, down_weight), False, second_layers
    )
    (full_up,), _, fifth_layers = gathered(place, (up_weight,), False, third_layers)
    (kernel_two,), _, _ = gathered(place, (window[:, window_half:],), True, fourth_layers)
    (full_tmix, full_lmix), _, _ = gathered(place, (token_mixer, letter_mixer), False, fifth_layers)
    (
        full_pbias,
        full_obias,
        gain_one,
        shift_one,
        full_ubias,
        full_dbias,
        gain_two,
        shift_two,
        full_sin,
        full_shid,
        full_toff,
        full_loff,
        full_koff,
        gain_three,
        shift_three,
        gain_four,
        shift_four,
    ) = gathered_vectors(
        place,
        (
            project_bias,
            output_bias,
            first_gain,
            first_shift,
            up_bias,
            down_bias,
            second_gain,
            second_shift,
            shift_input,
            shift_hidden,
            token_offset,
            letter_offset,
            window_offset,
            third_gain,
            third_shift,
            fourth_gain,
            fourth_shift,
        ),
        first_piece,
    )

    bias_full = jnp.concatenate(
        [full_pbias[:model_width], jnp.zeros((model_width,), jnp.float32), full_pbias[model_width:]]
    )
    mixed = (product(tokens, full_project) + bias_full).astype(jnp.bfloat16)
    queries = mixed[:, :model_width].reshape(seq_rows, HEADS, head_width)
    key_rows = mixed[:, model_width : 2 * model_width].reshape(seq_rows, HEADS, head_width)
    value_rows = mixed[:, 2 * model_width :].reshape(seq_rows, HEADS, head_width)

    def masked_scores_of(query_part, key_part):
        raw_scores = (
            jnp.einsum("qhd,khd->hqk", query_part, key_part, preferred_element_type=jnp.float32)
            * score_scale
        )
        return jnp.where(key_valid, raw_scores, -1e30)

    masked_scores = masked_scores_of(queries, key_rows)
    row_peak = jnp.max(masked_scores, axis=-1, keepdims=True)
    log_total = row_peak + jnp.log(
        jnp.sum(jnp.exp(masked_scores - row_peak), axis=-1, keepdims=True)
    )
    probabilities = jnp.exp(masked_scores - log_total)
    probs_low = probabilities.astype(jnp.bfloat16)
    context = jnp.einsum("hqk,khd->qhd", probs_low, value_rows, preferred_element_type=jnp.float32)
    context = (
        context
        .astype(jnp.bfloat16)
        .reshape(seq_rows, model_width)
    )
    attended = product(context, full_output) + full_obias
    residual_one = tokens.astype(jnp.float32) + attended
    first = normalize(residual_one, gain_one, shift_one)
    first_low = first.astype(jnp.bfloat16)
    upper = product(first_low, full_up)
    upper = upper + full_ubias
    activated, slope_upper = gelu_and_slope(upper)
    activated = activated.astype(jnp.bfloat16)
    residual_two = first + product(activated, full_down) + full_dbias
    second = normalize(residual_two, gain_two, shift_two)
    hidden_width = full_ghid.shape[0]
    gates_width = 3 * hidden_width
    counts_column = counts.reshape(-1, 1)
    gates_ahead, gates_behind, prev_ahead, prev_behind, pooled = recurrent_forward(
        letter_flat.reshape(letter_slots, seq_rows, model_width),
        full_gin,
        full_ghid,
        full_sin.reshape(1, -1),
        full_shid.reshape(1, -1),
        counts_column,
    )
    second_low = second.astype(jnp.bfloat16)
    pooled_low = pooled.astype(jnp.bfloat16)
    token_side = product(second_low, full_tmix) + full_toff
    letter_side = product(pooled_low, full_lmix) + full_loff
    joined = (jnp.concatenate([token_side, letter_side], axis=-1) * row_mask).astype(jnp.bfloat16)
    joined_width = joined.shape[1]
    taps_one = product(joined, kernel_one)
    taps_two = product(joined, kernel_two)
    rest = window_half - joined_width
    convolved = (
        jnp.pad(taps_one[:-1, :joined_width], ((1, 0), (0, 0)))
        + jnp.concatenate([taps_one[:, joined_width:], taps_two[:, :rest]], axis=1)
        + jnp.pad(taps_two[1:, rest:], ((0, 1), (0, 0)))
        + full_koff
    )
    widened, slope_conv = gelu_and_slope(convolved)
    residual_three = second + widened[:, :model_width]
    residual_four = pooled + widened[:, model_width:]
    token_out = normalize(residual_three, gain_three, shift_three) * row_mask
    letter_out = normalize(residual_four, gain_four, shift_four) * row_mask

    out_token_delta = cot_token.astype(jnp.float32) * row_mask
    out_letter_delta = cot_letter.astype(jnp.float32) * row_mask
    _, pull_three = jax.vjp(normalize, residual_three, gain_three, shift_three)
    delta_three, delta_gain_three, delta_shift_three = pull_three(out_token_delta)
    _, pull_four = jax.vjp(normalize, residual_four, gain_four, shift_four)
    delta_four, delta_gain_four, delta_shift_four = pull_four(out_letter_delta)
    delta_conv = (jnp.concatenate([delta_three, delta_four], axis=-1) * slope_conv).astype(
        jnp.bfloat16
    )
    delta_koff = column_sum(delta_conv)
    delta_taps = jnp.concatenate(
        [
            jnp.pad(delta_conv[1:], ((0, 1), (0, 0))),
            delta_conv,
            jnp.pad(delta_conv[:-1], ((1, 0), (0, 0))),
        ],
        axis=1,
    )
    taps_low, taps_high = delta_taps[:, :window_half], delta_taps[:, window_half:]
    one_sum = core_sum(place, joined, taps_low)
    two_sum = core_sum(place, joined, taps_high)
    one_pending = summed(place, (one_sum,), True)
    two_pending = summed(place, (two_sum,), True)
    delta_joined = right_product(taps_low, kernel_one) + right_product(taps_high, kernel_two)
    delta_joined = delta_joined * row_mask
    delta_tside = delta_joined[:, :model_width].astype(jnp.bfloat16)
    delta_lside = delta_joined[:, model_width:].astype(jnp.bfloat16)
    tmix_sum = core_sum(place, second_low, delta_tside)
    delta_toff = column_sum(delta_tside)
    lmix_sum = core_sum(place, pooled_low, delta_lside)
    delta_loff = column_sum(delta_lside)
    delta_second = delta_three + right_product(delta_tside, full_tmix)
    delta_pooled = delta_four + right_product(delta_lside, full_lmix)

    inputs_ahead, inputs_behind, turned_ahead, turned_behind, sin_delta, shid_delta = (
        recurrent_backward(
            (gates_ahead, gates_behind),
            (prev_ahead, prev_behind),
            full_ghid,
            counts_column,
            delta_pooled,
        )
    )
    flat_rows = lambda v: v.reshape(letter_slots * seq_rows, -1)
    inputs_ahead, inputs_behind = flat_rows(inputs_ahead), flat_rows(inputs_behind)
    gin_sum = core_sum_of_pair(
        place, left_product(letter_flat, inputs_ahead), left_product(letter_flat, inputs_behind)
    )
    ghid_sum = core_sum_of_pair(
        place,
        left_product(flat_rows(prev_ahead), flat_rows(turned_ahead)),
        left_product(flat_rows(prev_behind), flat_rows(turned_behind)),
    )
    letters_delta = right_product(inputs_ahead, full_gin[:, :gates_width]) + right_product(
        inputs_behind, full_gin[:, gates_width:]
    )
    letters_grad = (
        letters_delta.astype(jnp.bfloat16)
        .reshape(letter_slots, seq_rows, model_width)
        .transpose(1, 0, 2)
    )
    sin_delta = sin_delta.reshape(2, -1)
    shid_delta = shid_delta.reshape(2, -1)
    in_pair = lambda v: jnp.stack([v[:, :gates_width], v[:, gates_width:]])
    ghid_pending = summed(place, (ghid_sum,), False)
    gin_pending = summed(place, (gin_sum,), True)
    delta_second = hold(delta_second, letters_delta)
    _, pull_two = jax.vjp(normalize, residual_two, gain_two, shift_two)
    delta_two, delta_gain_two, delta_shift_two = pull_two(delta_second)
    delta_lowered = delta_two.astype(jnp.bfloat16)
    down_sum = core_sum(place, activated, delta_lowered)
    down_pending = summed(place, (tmix_sum, lmix_sum, down_sum), False)
    delta_dbias = column_sum(delta_lowered)
    delta_activated = right_product(delta_lowered, full_down)
    delta_upper = (delta_activated * slope_upper).astype(jnp.bfloat16)
    up_sum = core_sum(place, first_low, delta_upper)
    up_pending = summed(place, (up_sum,), False)
    delta_ubias = column_sum(delta_upper)
    delta_first = right_product(delta_upper, full_up)
    delta_first = delta_two + delta_first
    _, pull_one = jax.vjp(normalize, residual_one, gain_one, shift_one)
    delta_one, delta_gain_one, delta_shift_one = pull_one(delta_first)
    delta_attended = delta_one.astype(jnp.bfloat16)
    output_sum = core_sum(place, context, delta_attended)
    output_pending = summed(place, (output_sum,), False)
    delta_obias = column_sum(delta_attended)
    delta_context = right_product(delta_attended, full_output)
    delta_context = (
        delta_context
        .astype(jnp.bfloat16)
        .reshape(seq_rows, HEADS, head_width)
    )
    delta_values = jnp.einsum(
        "hqk,qhd->khd",
        probs_low,
        delta_context,
        preferred_element_type=jnp.float32,
    )
    delta_probs = jnp.einsum(
        "qhd,khd->hqk", delta_context, value_rows, preferred_element_type=jnp.float32
    )
    delta_scores = (
        probabilities * (delta_probs - jnp.sum(probabilities * delta_probs, axis=-1, keepdims=True))
    ).astype(jnp.bfloat16)
    delta_queries = jnp.einsum(
        "hqk,khd->qhd", delta_scores, key_rows, preferred_element_type=jnp.float32
    )
    delta_keys = jnp.einsum(
        "hqk,qhd->khd", delta_scores, queries, preferred_element_type=jnp.float32
    )
    delta_queries = delta_queries * score_scale
    delta_keys = delta_keys * score_scale
    delta_mixed = jnp.concatenate(
        [
            delta_queries.reshape(seq_rows, model_width),
            delta_keys.reshape(seq_rows, model_width),
            delta_values.reshape(seq_rows, model_width),
        ],
        axis=-1,
    ).astype(jnp.bfloat16)
    project_sum = core_sum(place, tokens, delta_mixed)
    project_pending = summed(place, (project_sum,), True)
    (ghid_grad,) = shared(place, ghid_pending, delta_context)
    (kernel_one_grad,) = shared(place, one_pending, delta_context)
    (kernel_two_grad,) = shared(place, two_pending, delta_mixed)
    (gin_grad,) = shared(place, gin_pending, delta_mixed)
    tmix_grad, lmix_grad, down_grad = shared(place, down_pending, delta_mixed)
    (up_grad,) = shared(place, up_pending, delta_mixed)
    (output_grad,) = shared(place, output_pending, delta_mixed)
    (project_grad,) = shared(place, project_pending)
    ghid_grad, gin_grad = in_pair(ghid_grad), in_pair(gin_grad)
    kernel_grad = jnp.concatenate([kernel_one_grad, kernel_two_grad], axis=1)
    delta_mixed_sum = column_sum(delta_mixed)
    delta_pbias = jnp.concatenate(
        [delta_mixed_sum[:model_width], delta_mixed_sum[2 * model_width :]]
    )
    tokens_grad = right_product(delta_mixed, full_project)
    tokens_grad = (delta_one + tokens_grad).astype(jnp.bfloat16)
    (
        pbias_grad,
        obias_grad,
        gain_one_grad,
        shift_one_grad,
        ubias_grad,
        dbias_grad,
        gain_two_grad,
        shift_two_grad,
        sin_grad,
        shid_grad,
        toff_grad,
        loff_grad,
        koff_grad,
        gain_three_grad,
        shift_three_grad,
        gain_four_grad,
        shift_four_grad,
    ) = owned_vectors(
        place,
        (
            delta_pbias,
            delta_obias,
            delta_gain_one,
            delta_shift_one,
            delta_ubias,
            delta_dbias,
            delta_gain_two,
            delta_shift_two,
            sin_delta,
            shid_delta,
            delta_toff,
            delta_loff,
            delta_koff,
            delta_gain_three,
            delta_shift_three,
            delta_gain_four,
            delta_shift_four,
        ),
    )
    taps_grad = jnp.stack(
        [kernel_grad[:, t * joined_width : (t + 1) * joined_width] for t in range(3)]
    )
    return (
        token_out.astype(jnp.bfloat16),
        letter_out.astype(jnp.bfloat16),
        tokens_grad,
        letters_grad,
        project_grad,
        pbias_grad,
        output_grad,
        obias_grad,
        gain_one_grad,
        shift_one_grad,
        up_grad,
        ubias_grad,
        down_grad,
        dbias_grad,
        gain_two_grad,
        shift_two_grad,
        gin_grad,
        ghid_grad,
        sin_grad,
        shid_grad,
        tmix_grad,
        toff_grad,
        lmix_grad,
        loff_grad,
        taps_grad,
        koff_grad,
        gain_three_grad,
        shift_three_grad,
        gain_four_grad,
        shift_four_grad,
    )


def solution(mesh):
    placed = (
        P(("rep", "shard"), None),
        P(("rep", "shard"), None, None),
        P(("rep", "shard")),
        P(("rep", "shard")),
        P(("rep", "shard"), None),
        P(("rep", "shard"), None),
        P("shard", None),
        P("shard"),
        P("shard", None),
        P("shard"),
        P("shard"),
        P("shard"),
        P("shard", None),
        P("shard"),
        P("shard", None),
        P("shard"),
        P("shard"),
        P("shard"),
        P(None, "shard", None),
        P(None, "shard", None),
        P(None, "shard"),
        P(None, "shard"),
        P("shard", None),
        P("shard"),
        P("shard", None),
        P("shard"),
        P(None, "shard", None),
        P("shard"),
        P("shard"),
        P("shard"),
        P("shard"),
        P("shard"),
    )
    return jax.shard_map(
        shards,
        mesh=mesh,
        in_specs=placed,
        out_specs=(
            P(("rep", "shard"), None),
            P(("rep", "shard"), None),
            P(("rep", "shard"), None),
            P(("rep", "shard"), None, None),
            P("shard", None),
            P("shard"),
            P("shard", None),
            P("shard"),
            P("shard"),
            P("shard"),
            P("shard", None),
            P("shard"),
            P("shard", None),
            P("shard"),
            P("shard"),
            P("shard"),
            P(None, "shard", None),
            P(None, "shard", None),
            P(None, "shard"),
            P(None, "shard"),
            P("shard", None),
            P("shard"),
            P("shard", None),
            P("shard"),
            P(None, "shard", None),
            P("shard"),
            P("shard"),
            P("shard"),
            P("shard"),
            P("shard"),
        ),
        check_vma=False,
    )
```

```python
import jax
import jax.numpy as jnp
from jax import lax
from jax.experimental import pallas as pl
from jax.experimental.pallas import tpu as pltpu
from jax.sharding import PartitionSpec as P


HEADS = 12


EPS = 1e-05

SHARD = "shard"
REP = "rep"
BOTH = (REP, SHARD)


def product(left, right):
    return jnp.dot(left, right, preferred_element_type=jnp.float32)


def left_product(left, right):
    return lax.dot_general(
        left, right, (((0,), (0,)), ((), ())), preferred_element_type=jnp.float32
    )


def right_product(left, right):
    return lax.dot_general(
        left, right, (((1,), (1,)), ((), ())), preferred_element_type=jnp.float32
    )


def column_sum(values):
    return jnp.sum(values.astype(jnp.float32), axis=0)


def normalize(values, gain, shift):
    center = jnp.mean(values, axis=-1, keepdims=True)
    centered = values - center
    spread = jnp.mean(centered * centered, axis=-1, keepdims=True)
    return centered * lax.rsqrt(spread + EPS) * gain + shift


def gelu_and_slope(values):
    below = 0.5 + 0.5 * lax.erf(values * (0.5**0.5))
    density = jnp.exp(-0.5 * values * values) * ((2.0 * jnp.pi) ** -0.5)
    return values * below, below + values * density


def logistic(values):
    return 0.5 + 0.5 * jnp.tanh(0.5 * values)


def recurrent_forward(slots, gin, ghid, sin, shid, counts):
    letter_slots, rows, width = slots.shape
    hidden = ghid.shape[0]
    gates = 3 * hidden
    last_slot = letter_slots - 1

    def body(
        ahead_ref,
        behind_ref,
        gin_ref,
        ghid_ref,
        sin_ref,
        shid_ref,
        counts_ref,
        gates_ahead,
        gates_behind,
        prev_ahead,
        prev_behind,
        last_ref,
        state_ref,
    ):
        step = pl.program_id(0)

        @pl.when(step == 0)
        def _():
            state_ref[...] = jnp.zeros_like(state_ref)

        counts_in = counts_ref[...]
        work = (
            (0, ahead_ref, step, gates_ahead, prev_ahead),
            (1, behind_ref, last_slot - step, gates_behind, prev_behind),
        )
        for at, slot_ref, slot, gates_ref, prev_ref in work:
            columns = slice(at * gates, (at + 1) * gates)
            own = slice(at * hidden, (at + 1) * hidden)
            state = state_ref[:, own]
            state_low = state.astype(jnp.bfloat16)
            prev_ref[0] = state_low
            inputs = product(slot_ref[0], gin_ref[:, columns]) + sin_ref[:, columns]
            turned = product(state_low, ghid_ref[:, columns]) + shid_ref[:, columns]
            reset = logistic(inputs[:, :hidden] + turned[:, :hidden])
            update = logistic(
                inputs[:, hidden : 2 * hidden] + turned[:, hidden : 2 * hidden]
            )
            turned_new = turned[:, 2 * hidden :]
            fresh = jnp.tanh(inputs[:, 2 * hidden :] + reset * turned_new)
            gates_ref[0, :, :hidden] = reset.astype(jnp.bfloat16)
            gates_ref[0, :, hidden : 2 * hidden] = update.astype(jnp.bfloat16)
            gates_ref[0, :, 2 * hidden : 3 * hidden] = fresh.astype(jnp.bfloat16)
            gates_ref[0, :, 3 * hidden :] = turned_new.astype(jnp.bfloat16)
            moved = (1.0 - update) * fresh + update * state
            state_ref[:, own] = jnp.where(slot < counts_in, moved, state)

        @pl.when(step == last_slot)
        def _():
            last_ref[...] = state_ref[...]

    ahead = lambda i: (i, 0, 0)
    behind = lambda i: (last_slot - i, 0, 0)
    fixed = lambda i: (0, 0)
    low = jnp.bfloat16
    return pl.pallas_call(
        body,
        grid=(letter_slots,),
        in_specs=[
            pl.BlockSpec((1, rows, width), ahead),
            pl.BlockSpec((1, rows, width), behind),
            pl.BlockSpec(gin.shape, fixed),
            pl.BlockSpec(ghid.shape, fixed),
            pl.BlockSpec((1, 2 * gates), fixed),
            pl.BlockSpec((1, 2 * gates), fixed),
            pl.BlockSpec((rows, 1), fixed),
        ],
        out_specs=[
            pl.BlockSpec((1, rows, 4 * hidden), ahead),
            pl.BlockSpec((1, rows, 4 * hidden), behind),
            pl.BlockSpec((1, rows, hidden), ahead),
            pl.BlockSpec((1, rows, hidden), behind),
            pl.BlockSpec((rows, 2 * hidden), fixed),
        ],
        out_shape=[
            jax.ShapeDtypeStruct((letter_slots, rows, 4 * hidden), low),
            jax.ShapeDtypeStruct((letter_slots, rows, 4 * hidden), low),
            jax.ShapeDtypeStruct((letter_slots, rows, hidden), low),
            jax.ShapeDtypeStruct((letter_slots, rows, hidden), low),
            jax.ShapeDtypeStruct((rows, 2 * hidden), jnp.float32),
        ],
        scratch_shapes=[pltpu.VMEM((rows, 2 * hidden), jnp.float32)],
        name="recurrent",
    )(slots, slots, gin, ghid, sin, shid, counts)


def recurrent_backward(saved_gates, saved_states, ghid, counts, delta):
    letter_slots, rows, _ = saved_gates[0].shape
    hidden = ghid.shape[0]
    gates = 3 * hidden
    last_slot = letter_slots - 1

    def body(
        gates_ahead,
        gates_behind,
        prev_ahead,
        prev_behind,
        ghid_ref,
        counts_ref,
        delta_ref,
        inputs_ahead,
        inputs_behind,
        turned_ahead,
        turned_behind,
        inputs_sum,
        turned_sum,
        carry_ref,
    ):
        step = pl.program_id(0)

        @pl.when(step == 0)
        def _():
            carry_ref[...] = delta_ref[...]
            inputs_sum[...] = jnp.zeros_like(inputs_sum)
            turned_sum[...] = jnp.zeros_like(turned_sum)

        counts_in = counts_ref[...]
        work = (
            (0, last_slot - step, gates_ahead, prev_ahead, inputs_ahead, turned_ahead),
            (1, step, gates_behind, prev_behind, inputs_behind, turned_behind),
        )
        for at, slot, gates_ref, prev_ref, inputs_ref, turned_ref in work:
            start = at * gates
            own = slice(at * hidden, (at + 1) * hidden)
            reset = gates_ref[0, :, :hidden].astype(jnp.float32)
            update = gates_ref[0, :, hidden : 2 * hidden].astype(jnp.float32)
            fresh = gates_ref[0, :, 2 * hidden : 3 * hidden].astype(jnp.float32)
            turned_new = gates_ref[0, :, 3 * hidden :].astype(jnp.float32)
            state = prev_ref[0].astype(jnp.float32)
            carry = carry_ref[:, own]
            active = slot < counts_in
            moved = jnp.where(active, carry, 0.0)
            delta_fresh = moved * (1.0 - update) * (1.0 - fresh * fresh)
            delta_update = moved * (state - fresh) * update * (1.0 - update)
            delta_reset = delta_fresh * turned_new * reset * (1.0 - reset)
            low_reset = delta_reset.astype(jnp.bfloat16)
            low_update = delta_update.astype(jnp.bfloat16)
            low_fresh = delta_fresh.astype(jnp.bfloat16)
            low_turned = (delta_fresh * reset).astype(jnp.bfloat16)
            inputs_ref[0, :, :hidden] = low_reset
            inputs_ref[0, :, hidden : 2 * hidden] = low_update
            inputs_ref[0, :, 2 * hidden :] = low_fresh
            turned_ref[0, :, :hidden] = low_reset
            turned_ref[0, :, hidden : 2 * hidden] = low_update
            turned_ref[0, :, 2 * hidden :] = low_turned
            through = right_product(turned_ref[0], ghid_ref[:, start : start + gates])
            carry_ref[:, own] = jnp.where(active, moved * update, carry) + through
            sums = [
                jnp.sum(part.astype(jnp.float32), axis=0, keepdims=True)
                for part in (low_reset, low_update, low_fresh, low_turned)
            ]
            for place_at, (first, second) in enumerate(
                ((sums[0], sums[0]), (sums[1], sums[1]), (sums[2], sums[3]))
            ):
                columns = slice(start + place_at * hidden, start + (place_at + 1) * hidden)
                inputs_sum[:, columns] += first
                turned_sum[:, columns] += second

    ahead = lambda i: (last_slot - i, 0, 0)
    behind = lambda i: (i, 0, 0)
    fixed = lambda i: (0, 0)
    low = jnp.bfloat16
    return pl.pallas_call(
        body,
        grid=(letter_slots,),
        in_specs=[
            pl.BlockSpec((1, rows, 4 * hidden), ahead),
            pl.BlockSpec((1, rows, 4 * hidden), behind),
            pl.BlockSpec((1, rows, hidden), ahead),
            pl.BlockSpec((1, rows, hidden), behind),
            pl.BlockSpec(ghid.shape, fixed),
            pl.BlockSpec((rows, 1), fixed),
            pl.BlockSpec((rows, 2 * hidden), fixed),
        ],
        out_specs=[
            pl.BlockSpec((1, rows, gates), ahead),
            pl.BlockSpec((1, rows, gates), behind),
            pl.BlockSpec((1, rows, gates), ahead),
            pl.BlockSpec((1, rows, gates), behind),
            pl.BlockSpec((1, 2 * gates), fixed),
            pl.BlockSpec((1, 2 * gates), fixed),
        ],
        out_shape=[
            jax.ShapeDtypeStruct((letter_slots, rows, gates), low),
            jax.ShapeDtypeStruct((letter_slots, rows, gates), low),
            jax.ShapeDtypeStruct((letter_slots, rows, gates), low),
            jax.ShapeDtypeStruct((letter_slots, rows, gates), low),
            jax.ShapeDtypeStruct((1, 2 * gates), jnp.float32),
            jax.ShapeDtypeStruct((1, 2 * gates), jnp.float32),
        ],
        scratch_shapes=[pltpu.VMEM((rows, 2 * hidden), jnp.float32)],
        name="recurrent_back",
    )(*saved_gates, *saved_states, ghid, counts, delta)


DEPTH_SIZE = 4


def exchange(value, axis, pairs):
    return lax.ppermute(value, axis, pairs)


class Place:
    def __init__(self):
        self.rep_size = lax.axis_size(REP)
        self.shard_size = lax.axis_size(SHARD)
        self.depth = DEPTH_SIZE
        self.height = self.shard_size // DEPTH_SIZE
        rep_at = lax.axis_index(REP)
        shard_at = lax.axis_index(SHARD)
        self.shard_at = shard_at
        self.core = rep_at % 2
        self.side = (rep_at // 2) % 2
        self.row = shard_at % self.height
        self.layer = shard_at // self.height
        self.coords = jnp.stack([self.layer, self.row, self.side, self.core]).astype(jnp.int32)

    def over_core(self, value):
        return exchange(value, REP, [(i, i ^ 1) for i in range(self.rep_size)])

    def over_side(self, value):
        return exchange(value, REP, [(i, i ^ 2) for i in range(self.rep_size)])

    def over_far(self, value, step):
        return exchange(value, REP, [(i, (i + 4 * step) % self.rep_size) for i in range(self.rep_size)]
        )

    def over_row(self, value, step):
        return exchange(value, SHARD, [(i, i ^ step) for i in range(self.shard_size)])

    def over_layer(self, value, step):
        return exchange(value, SHARD, [(i, i ^ (step * self.height)) for i in range(self.shard_size)]
        )


def put_together(place, parts, rows, half, split):
    depth = place.depth
    flat = [part for group in parts for inner in group for part in inner]
    slots = [
        (core_slot, side_slot, row_slot)
        for core_slot in range(2)
        for side_slot in range(len(parts[0]))
        for row_slot in range(len(parts[0][0]))
    ]
    height = place.height
    pieces = 2 if split else 1
    part_rows = [r // pieces for r in rows]
    starts = [sum(part_rows[:i]) for i in range(len(rows))]

    def body(coords_ref, *refs):
        ins = refs[: len(flat)]
        outs = refs[len(flat) : len(flat) + len(rows)]
        sems = refs[-1]
        layer, row, side, core = (coords_ref[i] for i in range(4))
        copies = []
        for at, (core_slot, side_slot, row_slot) in enumerate(slots):
            for layer_slot in range(depth):
                block = (layer ^ layer_slot) * height + (row ^ row_slot)
                if split:
                    block = block * 2 + (side ^ side_slot)
                column = pl.multiple_of((core ^ core_slot) * half, 128)
                for out_ref, start, count in zip(outs, starts, part_rows):
                    copies.append(
                        pltpu.make_async_copy(
                            ins[at].at[layer_slot, pl.ds(start, count), :],
                            out_ref.at[block, :, pl.ds(column, half)],
                            sems.at[len(copies)],
                        )
                    )
        for copy in copies:
            copy.start()
        for copy in copies:
            copy.wait()

    blocks = depth * height * pieces
    whole = pl.pallas_call(
        body,
        out_shape=[
            jax.ShapeDtypeStruct((blocks, count, 2 * half), flat[0].dtype) for count in part_rows
        ],
        in_specs=[pl.BlockSpec(memory_space=pltpu.SMEM)]
        + [pl.BlockSpec(memory_space=pl.ANY)] * len(flat),
        out_specs=[pl.BlockSpec(memory_space=pltpu.VMEM)] * len(rows),
        scratch_shapes=[pltpu.SemaphoreType.DMA((len(flat) * depth * len(rows),))],
        name="put_together",
    )(place.coords, *flat)
    return [w.reshape(r * place.shard_size, 2 * half) for w, r in zip(whole, rows)]


def gathered(place, shards_in, split):
    half = shards_in[0].shape[1] // 2
    pieces = []
    for shard in shards_in:
        part_rows = shard.shape[0] // 2 if split else shard.shape[0]
        top = place.side * part_rows if split else 0
        pieces.append(lax.dynamic_slice(shard, (top, place.core * half), (part_rows, half)))
    piece = pieces[0] if len(pieces) == 1 else jnp.concatenate(pieces, axis=0)
    layers = jnp.stack([piece] + [place.over_layer(piece, step) for step in range(1, place.depth)])
    column = [layers] + [place.over_row(layers, step) for step in range(1, place.height)]
    sides = [column]
    if split:
        sides.append([place.over_side(part) for part in column])
    cores = [
        sides,
        [[place.over_core(part) for part in group] for group in sides],
    ]
    whole = put_together(place, cores, [shard.shape[0] for shard in shards_in], half, split)
    return whole, piece


def hold(value, *others):
    return lax.optimization_barrier((value, *others))[0]


def pick(value, at, axis):
    return lax.dynamic_index_in_dim(value, at, axis, keepdims=False)


def widen(value):
    return value.astype(jnp.float32)


def narrow(value):
    return value.astype(jnp.bfloat16)


def core_sum(place, inputs, delta):
    half = delta.shape[1] // 2

    def half_of(at):
        return left_product(inputs, lax.dynamic_slice_in_dim(delta, at * half, half, axis=1))

    sent = half_of(1 - place.core)
    other = place.over_core(narrow(sent))
    return narrow(half_of(place.core) + widen(other))


def core_sum_of_pair(place, first, second):
    first, second = narrow(first), narrow(second)
    other = place.over_core(jnp.where(place.core == 0, second, first))
    return narrow(widen(jnp.where(place.core == 0, first, second)) + widen(other))


def summed(place, helds, split):
    half = helds[0].shape[1]
    pieces = 2 if split else 1
    parts = [h.shape[0] // place.shard_size // pieces for h in helds]
    blocks = [h.reshape(place.shard_size, pieces, p, half) for h, p in zip(helds, parts)]
    if split:
        kept = []
        for block in blocks:
            other = place.over_side(pick(block, 1 - place.side, 1))
            kept.append(narrow(widen(pick(block, place.side, 1)) + widen(other)))
    else:
        kept = [block[:, 0] for block in blocks]
    shape = (place.depth, place.height)
    kept = [k.reshape(shape + k.shape[1:]) for k in kept]

    def stacked(values):
        return values[0] if len(values) == 1 else jnp.concatenate(values, axis=-2)

    total = widen(stacked([pick(k, place.row, 1) for k in kept]))
    for step in range(1, place.height):
        sent = stacked([pick(k, place.row ^ step, 1) for k in kept])
        total = total + widen(place.over_row(sent, step))
    held = narrow(total)
    total = widen(pick(held, place.layer, 0))
    for step in range(1, place.depth):
        sent = pick(held, place.layer ^ step, 0)
        total = total + widen(place.over_layer(sent, step))
    return narrow(total), parts, split


def shared(place, pending, after=None):
    held, parts, split = pending
    pieces = 2 if split else 1
    if after is not None:
        held = hold(held, after)
    total = widen(held)
    for step in range(1, place.rep_size // 4):
        total = total + widen(place.over_far(held, step))
    held = narrow(total)
    other = place.over_side(held)
    if split:
        low_side = jnp.where(place.side == 0, held, other)
        high_side = jnp.where(place.side == 0, other, held)
        rows, start = [], 0
        for p in parts:
            rows += [low_side[start : start + p], high_side[start : start + p]]
            start += p
        held = jnp.concatenate(rows, axis=0)
    else:
        held = narrow(widen(held) + widen(other))
    other = place.over_core(held)
    first = jnp.where(place.core == 0, held, other)
    last = jnp.where(place.core == 0, other, held)
    results, start = [], 0
    for p in parts:
        own = slice(start, start + p * pieces)
        results.append(widen(jnp.concatenate([first[own], last[own]], axis=1)))
        start += p * pieces
    return results


def gathered_vectors(place, vectors, after):
    flat = [v.reshape(-1) for v in vectors]
    flat[0] = hold(flat[0], after)
    packed = jnp.concatenate(flat)[None, :]
    layers = jnp.concatenate(
        [packed] + [place.over_layer(packed, step) for step in range(1, place.depth)], axis=0
    )
    slots = jnp.stack(
        [layers] + [place.over_row(layers, step) for step in range(1, place.height)], axis=1
    ).reshape(place.shard_size, -1)
    order = jnp.arange(place.shard_size)
    slot_of = ((order // place.height) ^ place.layer) * place.height + (
        (order % place.height) ^ place.row
    )
    ordered = jnp.take(slots, slot_of, axis=0, mode="clip").astype(jnp.float32)
    whole, start = [], 0
    for v in vectors:
        width = v.size
        part = ordered[:, start : start + width]
        if v.ndim == 1:
            whole.append(part.reshape(-1))
        else:
            lead, inner = v.shape
            whole.append(
                part.reshape(place.shard_size, lead, inner).transpose(1, 0, 2).reshape(lead, -1)
            )
        start += width
    return whole


def owned_vectors(place, vectors):
    count = place.shard_size
    rows = []
    for v in vectors:
        if v.ndim == 1:
            rows.append(v.reshape(count, -1))
        else:
            lead = v.shape[0]
            rows.append(v.reshape(lead, count, -1).transpose(1, 0, 2).reshape(count, -1))
    total = jnp.concatenate(rows, axis=1)
    total = total + place.over_core(total)
    total = total + place.over_side(total)
    base = total
    for step in range(1, place.rep_size // 4):
        total = total + place.over_far(base, step)
    span = 1
    while span < place.height:
        total = total + place.over_row(total, span)
        span *= 2
    span = 1
    while span < place.depth:
        total = total + place.over_layer(total, span)
        span *= 2
    own = lax.dynamic_index_in_dim(total, place.shard_at, 0, keepdims=False)
    parts, start = [], 0
    for v in vectors:
        width = v.size // count
        part = own[start : start + width]
        parts.append(part if v.ndim == 1 else part.reshape(v.shape[0], -1))
        start += width
    return parts


def shards(
    tokens,
    letters,
    lengths,
    counts,
    cot_token,
    cot_letter,
    project_weight,
    project_bias,
    output_weight,
    output_bias,
    first_gain,
    first_shift,
    up_weight,
    up_bias,
    down_weight,
    down_bias,
    second_gain,
    second_shift,
    gates_input,
    gates_hidden,
    shift_input,
    shift_hidden,
    token_mixer,
    token_offset,
    letter_mixer,
    letter_offset,
    window_kernel,
    window_offset,
    third_gain,
    third_shift,
    fourth_gain,
    fourth_shift,
):
    place = Place()
    seq_rows, model_width = tokens.shape
    letter_slots = letters.shape[1]
    head_width = model_width // HEADS
    score_scale = float(head_width) ** (-0.5)
    row_valid = jnp.arange(seq_rows) < lengths[0]
    row_mask = row_valid.astype(jnp.float32)[:, None]
    key_valid = row_valid[None, None, :]
    letter_flat = letters.transpose(1, 0, 2).reshape(letter_slots * seq_rows, model_width)

    side_by_side = lambda w: jnp.concatenate([w[i] for i in range(w.shape[0])], axis=1)
    (full_gin, full_project), first_piece = gathered(
        place, (side_by_side(gates_input), project_weight), True
    )
    (full_ghid,), _ = gathered(place, (side_by_side(gates_hidden),), False)
    window = side_by_side(window_kernel)
    window_half = window.shape[1] // 2
    (kernel_one,), _ = gathered(place, (window[:, :window_half],), True)
    (full_output, full_down), _ = gathered(place, (output_weight, down_weight), False)
    (full_up,), _ = gathered(place, (up_weight,), False)
    (kernel_two,), _ = gathered(place, (window[:, window_half:],), True)
    (full_tmix, full_lmix), _ = gathered(place, (token_mixer, letter_mixer), False)
    (
        full_pbias,
        full_obias,
        gain_one,
        shift_one,
        full_ubias,
        full_dbias,
        gain_two,
        shift_two,
        full_sin,
        full_shid,
        full_toff,
        full_loff,
        full_koff,
        gain_three,
        shift_three,
        gain_four,
        shift_four,
    ) = gathered_vectors(
        place,
        (
            project_bias,
            output_bias,
            first_gain,
            first_shift,
            up_bias,
            down_bias,
            second_gain,
            second_shift,
            shift_input,
            shift_hidden,
            token_offset,
            letter_offset,
            window_offset,
            third_gain,
            third_shift,
            fourth_gain,
            fourth_shift,
        ),
        first_piece,
    )

    bias_full = jnp.concatenate(
        [full_pbias[:model_width], jnp.zeros((model_width,), jnp.float32), full_pbias[model_width:]]
    )
    mixed = (product(tokens, full_project) + bias_full).astype(jnp.bfloat16)
    queries = mixed[:, :model_width].reshape(seq_rows, HEADS, head_width)
    key_rows = mixed[:, model_width : 2 * model_width].reshape(seq_rows, HEADS, head_width)
    value_rows = mixed[:, 2 * model_width :].reshape(seq_rows, HEADS, head_width)

    def masked_scores_of(query_part, key_part):
        raw_scores = (
            jnp.einsum("qhd,khd->hqk", query_part, key_part, preferred_element_type=jnp.float32)
            * score_scale
        )
        return jnp.where(key_valid, raw_scores, -1e30)

    masked_scores = masked_scores_of(queries, key_rows)
    row_peak = jnp.max(masked_scores, axis=-1, keepdims=True)
    log_total = row_peak + jnp.log(
        jnp.sum(jnp.exp(masked_scores - row_peak), axis=-1, keepdims=True)
    )
    probabilities = jnp.exp(masked_scores - log_total)
    probs_low = probabilities.astype(jnp.bfloat16)
    context = jnp.einsum("hqk,khd->qhd", probs_low, value_rows, preferred_element_type=jnp.float32)
    context = (
        context
        .astype(jnp.bfloat16)
        .reshape(seq_rows, model_width)
    )
    attended = product(context, full_output) + full_obias
    residual_one = tokens.astype(jnp.float32) + attended
    first = normalize(residual_one, gain_one, shift_one)
    first_low = first.astype(jnp.bfloat16)
    upper = product(first_low, full_up)
    upper = upper + full_ubias
    activated, slope_upper = gelu_and_slope(upper)
    activated = activated.astype(jnp.bfloat16)
    residual_two = first + product(activated, full_down) + full_dbias
    second = normalize(residual_two, gain_two, shift_two)
    hidden_width = full_ghid.shape[0]
    gates_width = 3 * hidden_width
    counts_column = counts.reshape(-1, 1)
    gates_ahead, gates_behind, prev_ahead, prev_behind, pooled = recurrent_forward(
        letter_flat.reshape(letter_slots, seq_rows, model_width),
        full_gin,
        full_ghid,
        full_sin.reshape(1, -1),
        full_shid.reshape(1, -1),
        counts_column,
    )
    second_low = second.astype(jnp.bfloat16)
    pooled_low = pooled.astype(jnp.bfloat16)
    token_side = product(second_low, full_tmix) + full_toff
    letter_side = product(pooled_low, full_lmix) + full_loff
    joined = (jnp.concatenate([token_side, letter_side], axis=-1) * row_mask).astype(jnp.bfloat16)
    joined_width = joined.shape[1]
    taps_one = product(joined, kernel_one)
    taps_two = product(joined, kernel_two)
    rest = window_half - joined_width
    convolved = (
        jnp.pad(taps_one[:-1, :joined_width], ((1, 0), (0, 0)))
        + jnp.concatenate([taps_one[:, joined_width:], taps_two[:, :rest]], axis=1)
        + jnp.pad(taps_two[1:, rest:], ((0, 1), (0, 0)))
        + full_koff
    )
    widened, slope_conv = gelu_and_slope(convolved)
    residual_three = second + widened[:, :model_width]
    residual_four = pooled + widened[:, model_width:]
    token_out = normalize(residual_three, gain_three, shift_three) * row_mask
    letter_out = normalize(residual_four, gain_four, shift_four) * row_mask

    out_token_delta = cot_token.astype(jnp.float32) * row_mask
    out_letter_delta = cot_letter.astype(jnp.float32) * row_mask
    _, pull_three = jax.vjp(normalize, residual_three, gain_three, shift_three)
    delta_three, delta_gain_three, delta_shift_three = pull_three(out_token_delta)
    _, pull_four = jax.vjp(normalize, residual_four, gain_four, shift_four)
    delta_four, delta_gain_four, delta_shift_four = pull_four(out_letter_delta)
    delta_conv = (jnp.concatenate([delta_three, delta_four], axis=-1) * slope_conv).astype(
        jnp.bfloat16
    )
    delta_koff = column_sum(delta_conv)
    delta_taps = jnp.concatenate(
        [
            jnp.pad(delta_conv[1:], ((0, 1), (0, 0))),
            delta_conv,
            jnp.pad(delta_conv[:-1], ((1, 0), (0, 0))),
        ],
        axis=1,
    )
    taps_low, taps_high = delta_taps[:, :window_half], delta_taps[:, window_half:]
    one_sum = core_sum(place, joined, taps_low)
    two_sum = core_sum(place, joined, taps_high)
    one_pending = summed(place, (one_sum,), True)
    two_pending = summed(place, (two_sum,), True)
    delta_joined = right_product(taps_low, kernel_one) + right_product(taps_high, kernel_two)
    delta_joined = delta_joined * row_mask
    delta_tside = delta_joined[:, :model_width].astype(jnp.bfloat16)
    delta_lside = delta_joined[:, model_width:].astype(jnp.bfloat16)
    tmix_sum = core_sum(place, second_low, delta_tside)
    delta_toff = column_sum(delta_tside)
    lmix_sum = core_sum(place, pooled_low, delta_lside)
    delta_loff = column_sum(delta_lside)
    delta_second = delta_three + right_product(delta_tside, full_tmix)
    delta_pooled = delta_four + right_product(delta_lside, full_lmix)

    inputs_ahead, inputs_behind, turned_ahead, turned_behind, sin_delta, shid_delta = (
        recurrent_backward(
            (gates_ahead, gates_behind),
            (prev_ahead, prev_behind),
            full_ghid,
            counts_column,
            delta_pooled,
        )
    )
    flat_rows = lambda v: v.reshape(letter_slots * seq_rows, -1)
    inputs_ahead, inputs_behind = flat_rows(inputs_ahead), flat_rows(inputs_behind)
    gin_sum = core_sum_of_pair(
        place, left_product(letter_flat, inputs_ahead), left_product(letter_flat, inputs_behind)
    )
    ghid_sum = core_sum_of_pair(
        place,
        left_product(flat_rows(prev_ahead), flat_rows(turned_ahead)),
        left_product(flat_rows(prev_behind), flat_rows(turned_behind)),
    )
    letters_delta = right_product(inputs_ahead, full_gin[:, :gates_width]) + right_product(
        inputs_behind, full_gin[:, gates_width:]
    )
    letters_grad = (
        letters_delta.astype(jnp.bfloat16)
        .reshape(letter_slots, seq_rows, model_width)
        .transpose(1, 0, 2)
    )
    sin_delta = sin_delta.reshape(2, -1)
    shid_delta = shid_delta.reshape(2, -1)
    in_pair = lambda v: jnp.stack([v[:, :gates_width], v[:, gates_width:]])
    ghid_pending = summed(place, (ghid_sum,), False)
    gin_pending = summed(place, (gin_sum,), True)
    delta_second = hold(delta_second, letters_delta)
    _, pull_two = jax.vjp(normalize, residual_two, gain_two, shift_two)
    delta_two, delta_gain_two, delta_shift_two = pull_two(delta_second)
    delta_lowered = delta_two.astype(jnp.bfloat16)
    down_sum = core_sum(place, activated, delta_lowered)
    down_pending = summed(place, (tmix_sum, lmix_sum, down_sum), False)
    delta_dbias = column_sum(delta_lowered)
    delta_activated = right_product(delta_lowered, full_down)
    delta_upper = (delta_activated * slope_upper).astype(jnp.bfloat16)
    up_sum = core_sum(place, first_low, delta_upper)
    up_pending = summed(place, (up_sum,), False)
    delta_ubias = column_sum(delta_upper)
    delta_first = right_product(delta_upper, full_up)
    delta_first = delta_two + delta_first
    _, pull_one = jax.vjp(normalize, residual_one, gain_one, shift_one)
    delta_one, delta_gain_one, delta_shift_one = pull_one(delta_first)
    delta_attended = delta_one.astype(jnp.bfloat16)
    output_sum = core_sum(place, context, delta_attended)
    output_pending = summed(place, (output_sum,), False)
    delta_obias = column_sum(delta_attended)
    delta_context = right_product(delta_attended, full_output)
    delta_context = (
        delta_context
        .astype(jnp.bfloat16)
        .reshape(seq_rows, HEADS, head_width)
    )
    delta_values = jnp.einsum(
        "hqk,qhd->khd",
        probs_low,
        delta_context,
        preferred_element_type=jnp.float32,
    )
    delta_probs = jnp.einsum(
        "qhd,khd->hqk", delta_context, value_rows, preferred_element_type=jnp.float32
    )
    delta_scores = (
        probabilities * (delta_probs - jnp.sum(probabilities * delta_probs, axis=-1, keepdims=True))
    ).astype(jnp.bfloat16)
    delta_queries = jnp.einsum(
        "hqk,khd->qhd", delta_scores, key_rows, preferred_element_type=jnp.float32
    )
    delta_keys = jnp.einsum(
        "hqk,qhd->khd", delta_scores, queries, preferred_element_type=jnp.float32
    )
    delta_queries = delta_queries * score_scale
    delta_keys = delta_keys * score_scale
    delta_mixed = jnp.concatenate(
        [
            delta_queries.reshape(seq_rows, model_width),
            delta_keys.reshape(seq_rows, model_width),
            delta_values.reshape(seq_rows, model_width),
        ],
        axis=-1,
    ).astype(jnp.bfloat16)
    project_sum = core_sum(place, tokens, delta_mixed)
    project_pending = summed(place, (project_sum,), True)
    (ghid_grad,) = shared(place, ghid_pending, delta_context)
    (kernel_one_grad,) = shared(place, one_pending, delta_context)
    (kernel_two_grad,) = shared(place, two_pending, delta_context)
    (gin_grad,) = shared(place, gin_pending, delta_mixed)
    tmix_grad, lmix_grad, down_grad = shared(place, down_pending, delta_mixed)
    (up_grad,) = shared(place, up_pending, delta_mixed)
    (output_grad,) = shared(place, output_pending, delta_mixed)
    (project_grad,) = shared(place, project_pending)
    ghid_grad, gin_grad = in_pair(ghid_grad), in_pair(gin_grad)
    kernel_grad = jnp.concatenate([kernel_one_grad, kernel_two_grad], axis=1)
    delta_mixed_sum = column_sum(delta_mixed)
    delta_pbias = jnp.concatenate(
        [delta_mixed_sum[:model_width], delta_mixed_sum[2 * model_width :]]
    )
    tokens_grad = right_product(delta_mixed, full_project)
    tokens_grad = (delta_one + tokens_grad).astype(jnp.bfloat16)
    (
        pbias_grad,
        obias_grad,
        gain_one_grad,
        shift_one_grad,
        ubias_grad,
        dbias_grad,
        gain_two_grad,
        shift_two_grad,
        sin_grad,
        shid_grad,
        toff_grad,
        loff_grad,
        koff_grad,
        gain_three_grad,
        shift_three_grad,
        gain_four_grad,
        shift_four_grad,
    ) = owned_vectors(
        place,
        (
            delta_pbias,
            delta_obias,
            delta_gain_one,
            delta_shift_one,
            delta_ubias,
            delta_dbias,
            delta_gain_two,
            delta_shift_two,
            sin_delta,
            shid_delta,
            delta_toff,
            delta_loff,
            delta_koff,
            delta_gain_three,
            delta_shift_three,
            delta_gain_four,
            delta_shift_four,
        ),
    )
    taps_grad = jnp.stack(
        [kernel_grad[:, t * joined_width : (t + 1) * joined_width] for t in range(3)]
    )
    return (
        token_out.astype(jnp.bfloat16),
        letter_out.astype(jnp.bfloat16),
        tokens_grad,
        letters_grad,
        project_grad,
        pbias_grad,
        output_grad,
        obias_grad,
        gain_one_grad,
        shift_one_grad,
        up_grad,
        ubias_grad,
        down_grad,
        dbias_grad,
        gain_two_grad,
        shift_two_grad,
        gin_grad,
        ghid_grad,
        sin_grad,
        shid_grad,
        tmix_grad,
        toff_grad,
        lmix_grad,
        loff_grad,
        taps_grad,
        koff_grad,
        gain_three_grad,
        shift_three_grad,
        gain_four_grad,
        shift_four_grad,
    )


def solution(mesh):
    placed = (
        P(BOTH, None),
        P(BOTH, None, None),
        P(BOTH),
        P(BOTH),
        P(BOTH, None),
        P(BOTH, None),
        P(SHARD, None),
        P(SHARD),
        P(SHARD, None),
        P(SHARD),
        P(SHARD),
        P(SHARD),
        P(SHARD, None),
        P(SHARD),
        P(SHARD, None),
        P(SHARD),
        P(SHARD),
        P(SHARD),
        P(None, SHARD, None),
        P(None, SHARD, None),
        P(None, SHARD),
        P(None, SHARD),
        P(SHARD, None),
        P(SHARD),
        P(SHARD, None),
        P(SHARD),
        P(None, SHARD, None),
        P(SHARD),
        P(SHARD),
        P(SHARD),
        P(SHARD),
        P(SHARD),
    )
    return jax.shard_map(
        shards,
        mesh=mesh,
        in_specs=placed,
        out_specs=(
            P(BOTH, None),
            P(BOTH, None),
            P(BOTH, None),
            P(BOTH, None, None),
            P(SHARD, None),
            P(SHARD),
            P(SHARD, None),
            P(SHARD),
            P(SHARD),
            P(SHARD),
            P(SHARD, None),
            P(SHARD),
            P(SHARD, None),
            P(SHARD),
            P(SHARD),
            P(SHARD),
            P(None, SHARD, None),
            P(None, SHARD, None),
            P(None, SHARD),
            P(None, SHARD),
            P(SHARD, None),
            P(SHARD),
            P(SHARD, None),
            P(SHARD),
            P(None, SHARD, None),
            P(SHARD),
            P(SHARD),
            P(SHARD),
            P(SHARD),
            P(SHARD),
        ),
        check_vma=False,
    )
```

```python
import jax
import jax.numpy as jnp
from jax import lax
from jax.experimental import pallas as pl
from jax.experimental.pallas import tpu as pltpu
from jax.sharding import PartitionSpec as P


HEADS = 12


EPS = 1e-05

SHARD = "shard"
REP = "rep"
BOTH = (REP, SHARD)


def product(left, right):
    return jnp.dot(left, right, preferred_element_type=jnp.float32)


def left_product(left, right):
    return lax.dot_general(
        left, right, (((0,), (0,)), ((), ())), preferred_element_type=jnp.float32
    )


def right_product(left, right):
    return lax.dot_general(
        left, right, (((1,), (1,)), ((), ())), preferred_element_type=jnp.float32
    )


def column_sum(values):
    return jnp.sum(values.astype(jnp.float32), axis=0)


def normalize(values, gain, shift):
    center = jnp.mean(values, axis=-1, keepdims=True)
    centered = values - center
    spread = jnp.mean(centered * centered, axis=-1, keepdims=True)
    return centered * lax.rsqrt(spread + EPS) * gain + shift


def gelu_and_slope(values):
    below = 0.5 + 0.5 * lax.erf(values * (0.5**0.5))
    density = jnp.exp(-0.5 * values * values) * ((2.0 * jnp.pi) ** -0.5)
    return values * below, below + values * density


def logistic(values):
    return 0.5 + 0.5 * jnp.tanh(0.5 * values)


def recurrent_forward(slots, gin, ghid, sin, shid, counts):
    letter_slots, rows, width = slots.shape
    hidden = ghid.shape[0]
    gates = 3 * hidden
    last_slot = letter_slots - 1

    def body(
        ahead_ref,
        behind_ref,
        gin_ref,
        ghid_ref,
        sin_ref,
        shid_ref,
        counts_ref,
        gates_ahead,
        gates_behind,
        prev_ahead,
        prev_behind,
        last_ref,
        state_ref,
    ):
        step = pl.program_id(0)

        @pl.when(step == 0)
        def _():
            state_ref[...] = jnp.zeros_like(state_ref)

        counts_in = counts_ref[...]
        work = (
            (0, ahead_ref, step, gates_ahead, prev_ahead),
            (1, behind_ref, last_slot - step, gates_behind, prev_behind),
        )
        for at, slot_ref, slot, gates_ref, prev_ref in work:
            columns = slice(at * gates, (at + 1) * gates)
            own = slice(at * hidden, (at + 1) * hidden)
            state = state_ref[:, own]
            state_low = state.astype(jnp.bfloat16)
            prev_ref[0] = state_low
            inputs = product(slot_ref[0], gin_ref[:, columns]) + sin_ref[:, columns]
            turned = product(state_low, ghid_ref[:, columns]) + shid_ref[:, columns]
            reset = logistic(inputs[:, :hidden] + turned[:, :hidden])
            update = logistic(
                inputs[:, hidden : 2 * hidden] + turned[:, hidden : 2 * hidden]
            )
            turned_new = turned[:, 2 * hidden :]
            fresh = jnp.tanh(inputs[:, 2 * hidden :] + reset * turned_new)
            gates_ref[0, :, :hidden] = reset.astype(jnp.bfloat16)
            gates_ref[0, :, hidden : 2 * hidden] = update.astype(jnp.bfloat16)
            gates_ref[0, :, 2 * hidden : 3 * hidden] = fresh.astype(jnp.bfloat16)
            gates_ref[0, :, 3 * hidden :] = turned_new.astype(jnp.bfloat16)
            moved = (1.0 - update) * fresh + update * state
            state_ref[:, own] = jnp.where(slot < counts_in, moved, state)

        @pl.when(step == last_slot)
        def _():
            last_ref[...] = state_ref[...]

    ahead = lambda i: (i, 0, 0)
    behind = lambda i: (last_slot - i, 0, 0)
    fixed = lambda i: (0, 0)
    low = jnp.bfloat16
    return pl.pallas_call(
        body,
        grid=(letter_slots,),
        in_specs=[
            pl.BlockSpec((1, rows, width), ahead),
            pl.BlockSpec((1, rows, width), behind),
            pl.BlockSpec(gin.shape, fixed),
            pl.BlockSpec(ghid.shape, fixed),
            pl.BlockSpec((1, 2 * gates), fixed),
            pl.BlockSpec((1, 2 * gates), fixed),
            pl.BlockSpec((rows, 1), fixed),
        ],
        out_specs=[
            pl.BlockSpec((1, rows, 4 * hidden), ahead),
            pl.BlockSpec((1, rows, 4 * hidden), behind),
            pl.BlockSpec((1, rows, hidden), ahead),
            pl.BlockSpec((1, rows, hidden), behind),
            pl.BlockSpec((rows, 2 * hidden), fixed),
        ],
        out_shape=[
            jax.ShapeDtypeStruct((letter_slots, rows, 4 * hidden), low),
            jax.ShapeDtypeStruct((letter_slots, rows, 4 * hidden), low),
            jax.ShapeDtypeStruct((letter_slots, rows, hidden), low),
            jax.ShapeDtypeStruct((letter_slots, rows, hidden), low),
            jax.ShapeDtypeStruct((rows, 2 * hidden), jnp.float32),
        ],
        scratch_shapes=[pltpu.VMEM((rows, 2 * hidden), jnp.float32)],
        name="recurrent",
    )(slots, slots, gin, ghid, sin, shid, counts)


def recurrent_backward(saved_gates, saved_states, ghid, counts, delta):
    letter_slots, rows, _ = saved_gates[0].shape
    hidden = ghid.shape[0]
    gates = 3 * hidden
    last_slot = letter_slots - 1

    def body(
        gates_ahead,
        gates_behind,
        prev_ahead,
        prev_behind,
        ghid_ref,
        counts_ref,
        delta_ref,
        inputs_ahead,
        inputs_behind,
        turned_ahead,
        turned_behind,
        inputs_sum,
        turned_sum,
        carry_ref,
    ):
        step = pl.program_id(0)

        @pl.when(step == 0)
        def _():
            carry_ref[...] = delta_ref[...]
            inputs_sum[...] = jnp.zeros_like(inputs_sum)
            turned_sum[...] = jnp.zeros_like(turned_sum)

        counts_in = counts_ref[...]
        work = (
            (0, last_slot - step, gates_ahead, prev_ahead, inputs_ahead, turned_ahead),
            (1, step, gates_behind, prev_behind, inputs_behind, turned_behind),
        )
        for at, slot, gates_ref, prev_ref, inputs_ref, turned_ref in work:
            start = at * gates
            own = slice(at * hidden, (at + 1) * hidden)
            reset = gates_ref[0, :, :hidden].astype(jnp.float32)
            update = gates_ref[0, :, hidden : 2 * hidden].astype(jnp.float32)
            fresh = gates_ref[0, :, 2 * hidden : 3 * hidden].astype(jnp.float32)
            turned_new = gates_ref[0, :, 3 * hidden :].astype(jnp.float32)
            state = prev_ref[0].astype(jnp.float32)
            carry = carry_ref[:, own]
            active = slot < counts_in
            moved = jnp.where(active, carry, 0.0)
            delta_fresh = moved * (1.0 - update) * (1.0 - fresh * fresh)
            delta_update = moved * (state - fresh) * update * (1.0 - update)
            delta_reset = delta_fresh * turned_new * reset * (1.0 - reset)
            low_reset = delta_reset.astype(jnp.bfloat16)
            low_update = delta_update.astype(jnp.bfloat16)
            low_fresh = delta_fresh.astype(jnp.bfloat16)
            low_turned = (delta_fresh * reset).astype(jnp.bfloat16)
            inputs_ref[0, :, :hidden] = low_reset
            inputs_ref[0, :, hidden : 2 * hidden] = low_update
            inputs_ref[0, :, 2 * hidden :] = low_fresh
            turned_ref[0, :, :hidden] = low_reset
            turned_ref[0, :, hidden : 2 * hidden] = low_update
            turned_ref[0, :, 2 * hidden :] = low_turned
            through = right_product(turned_ref[0], ghid_ref[:, start : start + gates])
            carry_ref[:, own] = jnp.where(active, moved * update, carry) + through
            sums = [
                jnp.sum(part.astype(jnp.float32), axis=0, keepdims=True)
                for part in (low_reset, low_update, low_fresh, low_turned)
            ]
            for place_at, (first, second) in enumerate(
                ((sums[0], sums[0]), (sums[1], sums[1]), (sums[2], sums[3]))
            ):
                columns = slice(start + place_at * hidden, start + (place_at + 1) * hidden)
                inputs_sum[:, columns] += first
                turned_sum[:, columns] += second

    ahead = lambda i: (last_slot - i, 0, 0)
    behind = lambda i: (i, 0, 0)
    fixed = lambda i: (0, 0)
    low = jnp.bfloat16
    return pl.pallas_call(
        body,
        grid=(letter_slots,),
        in_specs=[
            pl.BlockSpec((1, rows, 4 * hidden), ahead),
            pl.BlockSpec((1, rows, 4 * hidden), behind),
            pl.BlockSpec((1, rows, hidden), ahead),
            pl.BlockSpec((1, rows, hidden), behind),
            pl.BlockSpec(ghid.shape, fixed),
            pl.BlockSpec((rows, 1), fixed),
            pl.BlockSpec((rows, 2 * hidden), fixed),
        ],
        out_specs=[
            pl.BlockSpec((1, rows, gates), ahead),
            pl.BlockSpec((1, rows, gates), behind),
            pl.BlockSpec((1, rows, gates), ahead),
            pl.BlockSpec((1, rows, gates), behind),
            pl.BlockSpec((1, 2 * gates), fixed),
            pl.BlockSpec((1, 2 * gates), fixed),
        ],
        out_shape=[
            jax.ShapeDtypeStruct((letter_slots, rows, gates), low),
            jax.ShapeDtypeStruct((letter_slots, rows, gates), low),
            jax.ShapeDtypeStruct((letter_slots, rows, gates), low),
            jax.ShapeDtypeStruct((letter_slots, rows, gates), low),
            jax.ShapeDtypeStruct((1, 2 * gates), jnp.float32),
            jax.ShapeDtypeStruct((1, 2 * gates), jnp.float32),
        ],
        scratch_shapes=[pltpu.VMEM((rows, 2 * hidden), jnp.float32)],
        name="recurrent_back",
    )(*saved_gates, *saved_states, ghid, counts, delta)


DEPTH_SIZE = 4


def exchange(value, axis, pairs):
    return lax.ppermute(value, axis, pairs)


class Place:
    def __init__(self):
        self.rep_size = lax.axis_size(REP)
        self.shard_size = lax.axis_size(SHARD)
        self.depth = DEPTH_SIZE
        self.height = self.shard_size // DEPTH_SIZE
        rep_at = lax.axis_index(REP)
        shard_at = lax.axis_index(SHARD)
        self.shard_at = shard_at
        self.core = rep_at % 2
        self.side = (rep_at // 2) % 2
        self.row = shard_at % self.height
        self.layer = shard_at // self.height
        self.coords = jnp.stack([self.layer, self.row, self.side, self.core]).astype(jnp.int32)

    def over_core(self, value):
        return exchange(value, REP, [(i, i ^ 1) for i in range(self.rep_size)])

    def over_side(self, value):
        return exchange(value, REP, [(i, i ^ 2) for i in range(self.rep_size)])

    def over_far(self, value, step):
        return exchange(value, REP, [(i, (i + 4 * step) % self.rep_size) for i in range(self.rep_size)]
        )

    def over_row(self, value, step):
        return exchange(value, SHARD, [(i, i ^ step) for i in range(self.shard_size)])

    def over_layer(self, value, step):
        return exchange(value, SHARD, [(i, i ^ (step * self.height)) for i in range(self.shard_size)]
        )


def put_together(place, parts, rows, half, split):
    depth = place.depth
    flat = [part for group in parts for inner in group for part in inner]
    slots = [
        (core_slot, side_slot, row_slot)
        for core_slot in range(2)
        for side_slot in range(len(parts[0]))
        for row_slot in range(len(parts[0][0]))
    ]
    height = place.height
    pieces = 2 if split else 1
    part_rows = [r // pieces for r in rows]
    starts = [sum(part_rows[:i]) for i in range(len(rows))]

    def body(coords_ref, *refs):
        ins = refs[: len(flat)]
        outs = refs[len(flat) : len(flat) + len(rows)]
        sems = refs[-1]
        layer, row, side, core = (coords_ref[i] for i in range(4))
        copies = []
        for at, (core_slot, side_slot, row_slot) in enumerate(slots):
            for layer_slot in range(depth):
                block = (layer ^ layer_slot) * height + (row ^ row_slot)
                if split:
                    block = block * 2 + (side ^ side_slot)
                column = pl.multiple_of((core ^ core_slot) * half, 128)
                for out_ref, start, count in zip(outs, starts, part_rows):
                    copies.append(
                        pltpu.make_async_copy(
                            ins[at].at[layer_slot, pl.ds(start, count), :],
                            out_ref.at[block, :, pl.ds(column, half)],
                            sems.at[len(copies)],
                        )
                    )
        for copy in copies:
            copy.start()
        for copy in copies:
            copy.wait()

    blocks = depth * height * pieces
    whole = pl.pallas_call(
        body,
        out_shape=[
            jax.ShapeDtypeStruct((blocks, count, 2 * half), flat[0].dtype) for count in part_rows
        ],
        in_specs=[pl.BlockSpec(memory_space=pltpu.SMEM)]
        + [pl.BlockSpec(memory_space=pl.ANY)] * len(flat),
        out_specs=[pl.BlockSpec(memory_space=pltpu.VMEM)] * len(rows),
        scratch_shapes=[pltpu.SemaphoreType.DMA((len(flat) * depth * len(rows),))],
        name="put_together",
    )(place.coords, *flat)
    return [w.reshape(r * place.shard_size, 2 * half) for w, r in zip(whole, rows)]


def gathered(place, shards_in, split):
    half = shards_in[0].shape[1] // 2
    pieces = []
    for shard in shards_in:
        part_rows = shard.shape[0] // 2 if split else shard.shape[0]
        top = place.side * part_rows if split else 0
        pieces.append(lax.dynamic_slice(shard, (top, place.core * half), (part_rows, half)))
    piece = pieces[0] if len(pieces) == 1 else jnp.concatenate(pieces, axis=0)
    layers = jnp.stack([piece] + [place.over_layer(piece, step) for step in range(1, place.depth)])
    column = [layers] + [place.over_row(layers, step) for step in range(1, place.height)]
    sides = [column]
    if split:
        sides.append([place.over_side(part) for part in column])
    cores = [
        sides,
        [[place.over_core(part) for part in group] for group in sides],
    ]
    whole = put_together(place, cores, [shard.shape[0] for shard in shards_in], half, split)
    return whole, piece


def hold(value, *others):
    return lax.optimization_barrier((value, *others))[0]


def pick(value, at, axis):
    return lax.dynamic_index_in_dim(value, at, axis, keepdims=False)


def widen(value):
    return value.astype(jnp.float32)


def narrow(value):
    return value.astype(jnp.bfloat16)


def core_sum(place, inputs, delta):
    half = delta.shape[1] // 2

    def half_of(at):
        return left_product(inputs, lax.dynamic_slice_in_dim(delta, at * half, half, axis=1))

    sent = half_of(1 - place.core)
    other = place.over_core(narrow(sent))
    return narrow(half_of(place.core) + widen(other))


def core_sum_of_pair(place, first, second):
    first, second = narrow(first), narrow(second)
    other = place.over_core(jnp.where(place.core == 0, second, first))
    return narrow(widen(jnp.where(place.core == 0, first, second)) + widen(other))


def summed(place, helds, split):
    half = helds[0].shape[1]
    pieces = 2 if split else 1
    parts = [h.shape[0] // place.shard_size // pieces for h in helds]
    blocks = [h.reshape(place.shard_size, pieces, p, half) for h, p in zip(helds, parts)]
    if split:
        kept = []
        for block in blocks:
            other = place.over_side(pick(block, 1 - place.side, 1))
            kept.append(narrow(widen(pick(block, place.side, 1)) + widen(other)))
    else:
        kept = [block[:, 0] for block in blocks]
    shape = (place.depth, place.height)
    kept = [k.reshape(shape + k.shape[1:]) for k in kept]

    def stacked(values):
        return values[0] if len(values) == 1 else jnp.concatenate(values, axis=-2)

    total = widen(stacked([pick(k, place.row, 1) for k in kept]))
    for step in range(1, place.height):
        sent = stacked([pick(k, place.row ^ step, 1) for k in kept])
        total = total + widen(place.over_row(sent, step))
    held = narrow(total)
    total = widen(pick(held, place.layer, 0))
    for step in range(1, place.depth):
        sent = pick(held, place.layer ^ step, 0)
        total = total + widen(place.over_layer(sent, step))
    return narrow(total), parts, split


def shared(place, pending, after=None):
    held, parts, split = pending
    pieces = 2 if split else 1
    if after is not None:
        held = hold(held, after)
    total = widen(held)
    for step in range(1, place.rep_size // 4):
        total = total + widen(place.over_far(held, step))
    held = narrow(total)
    other = place.over_side(held)
    if split:
        low_side = jnp.where(place.side == 0, held, other)
        high_side = jnp.where(place.side == 0, other, held)
        rows, start = [], 0
        for p in parts:
            rows += [low_side[start : start + p], high_side[start : start + p]]
            start += p
        held = jnp.concatenate(rows, axis=0)
    else:
        held = narrow(widen(held) + widen(other))
    other = place.over_core(held)
    first = jnp.where(place.core == 0, held, other)
    last = jnp.where(place.core == 0, other, held)
    results, start = [], 0
    for p in parts:
        own = slice(start, start + p * pieces)
        results.append(widen(jnp.concatenate([first[own], last[own]], axis=1)))
        start += p * pieces
    return results


def gathered_vectors(place, vectors, after):
    flat = [v.reshape(-1) for v in vectors]
    flat[0] = hold(flat[0], after)
    packed = jnp.concatenate(flat)[None, :]
    layers = jnp.concatenate(
        [packed] + [place.over_layer(packed, step) for step in range(1, place.depth)], axis=0
    )
    slots = jnp.stack(
        [layers] + [place.over_row(layers, step) for step in range(1, place.height)], axis=1
    ).reshape(place.shard_size, -1)
    order = jnp.arange(place.shard_size)
    slot_of = ((order // place.height) ^ place.layer) * place.height + (
        (order % place.height) ^ place.row
    )
    ordered = jnp.take(slots, slot_of, axis=0, mode="clip").astype(jnp.float32)
    whole, start = [], 0
    for v in vectors:
        width = v.size
        part = ordered[:, start : start + width]
        if v.ndim == 1:
            whole.append(part.reshape(-1))
        else:
            lead, inner = v.shape
            whole.append(
                part.reshape(place.shard_size, lead, inner).transpose(1, 0, 2).reshape(lead, -1)
            )
        start += width
    return whole


def owned_vectors(place, vectors):
    count = place.shard_size
    rows = []
    for v in vectors:
        if v.ndim == 1:
            rows.append(v.reshape(count, -1))
        else:
            lead = v.shape[0]
            rows.append(v.reshape(lead, count, -1).transpose(1, 0, 2).reshape(count, -1))
    total = jnp.concatenate(rows, axis=1)
    total = total + place.over_core(total)
    total = total + place.over_side(total)
    base = total
    for step in range(1, place.rep_size // 4):
        total = total + place.over_far(base, step)
    span = 1
    while span < place.height:
        total = total + place.over_row(total, span)
        span *= 2
    span = 1
    while span < place.depth:
        total = total + place.over_layer(total, span)
        span *= 2
    own = lax.dynamic_index_in_dim(total, place.shard_at, 0, keepdims=False)
    parts, start = [], 0
    for v in vectors:
        width = v.size // count
        part = own[start : start + width]
        parts.append(part if v.ndim == 1 else part.reshape(v.shape[0], -1))
        start += width
    return parts


def shards(
    tokens,
    letters,
    lengths,
    counts,
    cot_token,
    cot_letter,
    project_weight,
    project_bias,
    output_weight,
    output_bias,
    first_gain,
    first_shift,
    up_weight,
    up_bias,
    down_weight,
    down_bias,
    second_gain,
    second_shift,
    gates_input,
    gates_hidden,
    shift_input,
    shift_hidden,
    token_mixer,
    token_offset,
    letter_mixer,
    letter_offset,
    window_kernel,
    window_offset,
    third_gain,
    third_shift,
    fourth_gain,
    fourth_shift,
):
    place = Place()
    seq_rows, model_width = tokens.shape
    letter_slots = letters.shape[1]
    head_width = model_width // HEADS
    score_scale = float(head_width) ** (-0.5)
    row_valid = jnp.arange(seq_rows) < lengths[0]
    row_mask = row_valid.astype(jnp.float32)[:, None]
    key_valid = row_valid[None, None, :]
    letter_flat = letters.transpose(1, 0, 2).reshape(letter_slots * seq_rows, model_width)

    side_by_side = lambda w: jnp.concatenate([w[i] for i in range(w.shape[0])], axis=1)
    (full_gin, full_project), first_piece = gathered(
        place, (side_by_side(gates_input), project_weight), True
    )
    (full_ghid,), _ = gathered(place, (side_by_side(gates_hidden),), False)
    window = side_by_side(window_kernel)
    window_half = window.shape[1] // 2
    (kernel_one,), _ = gathered(place, (window[:, :window_half],), True)
    (full_output, full_down), _ = gathered(place, (output_weight, down_weight), False)
    (full_up,), _ = gathered(place, (up_weight,), False)
    (kernel_two,), _ = gathered(place, (window[:, window_half:],), True)
    (full_tmix, full_lmix), _ = gathered(place, (token_mixer, letter_mixer), False)
    (
        full_pbias,
        full_obias,
        gain_one,
        shift_one,
        full_ubias,
        full_dbias,
        gain_two,
        shift_two,
        full_sin,
        full_shid,
        full_toff,
        full_loff,
        full_koff,
        gain_three,
        shift_three,
        gain_four,
        shift_four,
    ) = gathered_vectors(
        place,
        (
            project_bias,
            output_bias,
            first_gain,
            first_shift,
            up_bias,
            down_bias,
            second_gain,
            second_shift,
            shift_input,
            shift_hidden,
            token_offset,
            letter_offset,
            window_offset,
            third_gain,
            third_shift,
            fourth_gain,
            fourth_shift,
        ),
        first_piece,
    )

    bias_full = jnp.concatenate(
        [full_pbias[:model_width], jnp.zeros((model_width,), jnp.float32), full_pbias[model_width:]]
    )
    mixed = (product(tokens, full_project) + bias_full).astype(jnp.bfloat16)
    queries = mixed[:, :model_width].reshape(seq_rows, HEADS, head_width)
    key_rows = mixed[:, model_width : 2 * model_width].reshape(seq_rows, HEADS, head_width)
    value_rows = mixed[:, 2 * model_width :].reshape(seq_rows, HEADS, head_width)

    def masked_scores_of(query_part, key_part):
        raw_scores = (
            jnp.einsum("qhd,khd->hqk", query_part, key_part, preferred_element_type=jnp.float32)
            * score_scale
        )
        return jnp.where(key_valid, raw_scores, -1e30)

    masked_scores = masked_scores_of(queries, key_rows)
    row_peak = jnp.max(masked_scores, axis=-1, keepdims=True)
    log_total = row_peak + jnp.log(
        jnp.sum(jnp.exp(masked_scores - row_peak), axis=-1, keepdims=True)
    )
    probabilities = jnp.exp(masked_scores - log_total)
    probs_low = probabilities.astype(jnp.bfloat16)
    context = jnp.einsum("hqk,khd->qhd", probs_low, value_rows, preferred_element_type=jnp.float32)
    context = (
        context
        .astype(jnp.bfloat16)
        .reshape(seq_rows, model_width)
    )
    attended = product(context, full_output) + full_obias
    residual_one = tokens.astype(jnp.float32) + attended
    first = normalize(residual_one, gain_one, shift_one)
    first_low = first.astype(jnp.bfloat16)
    upper = product(first_low, full_up)
    upper = upper + full_ubias
    activated, slope_upper = gelu_and_slope(upper)
    activated = activated.astype(jnp.bfloat16)
    residual_two = first + product(activated, full_down) + full_dbias
    second = normalize(residual_two, gain_two, shift_two)
    hidden_width = full_ghid.shape[0]
    gates_width = 3 * hidden_width
    counts_column = counts.reshape(-1, 1)
    gates_ahead, gates_behind, prev_ahead, prev_behind, pooled = recurrent_forward(
        letter_flat.reshape(letter_slots, seq_rows, model_width),
        full_gin,
        full_ghid,
        full_sin.reshape(1, -1),
        full_shid.reshape(1, -1),
        counts_column,
    )
    second_low = second.astype(jnp.bfloat16)
    pooled_low = pooled.astype(jnp.bfloat16)
    token_side = product(second_low, full_tmix) + full_toff
    letter_side = product(pooled_low, full_lmix) + full_loff
    joined = (jnp.concatenate([token_side, letter_side], axis=-1) * row_mask).astype(jnp.bfloat16)
    joined_width = joined.shape[1]
    taps_one = product(joined, kernel_one)
    taps_two = product(joined, kernel_two)
    rest = window_half - joined_width
    convolved = (
        jnp.pad(taps_one[:-1, :joined_width], ((1, 0), (0, 0)))
        + jnp.concatenate([taps_one[:, joined_width:], taps_two[:, :rest]], axis=1)
        + jnp.pad(taps_two[1:, rest:], ((0, 1), (0, 0)))
        + full_koff
    )
    widened, slope_conv = gelu_and_slope(convolved)
    residual_three = second + widened[:, :model_width]
    residual_four = pooled + widened[:, model_width:]
    token_out = normalize(residual_three, gain_three, shift_three) * row_mask
    letter_out = normalize(residual_four, gain_four, shift_four) * row_mask

    out_token_delta = cot_token.astype(jnp.float32) * row_mask
    out_letter_delta = cot_letter.astype(jnp.float32) * row_mask
    _, pull_three = jax.vjp(normalize, residual_three, gain_three, shift_three)
    delta_three, delta_gain_three, delta_shift_three = pull_three(out_token_delta)
    _, pull_four = jax.vjp(normalize, residual_four, gain_four, shift_four)
    delta_four, delta_gain_four, delta_shift_four = pull_four(out_letter_delta)
    delta_conv = (jnp.concatenate([delta_three, delta_four], axis=-1) * slope_conv).astype(
        jnp.bfloat16
    )
    delta_koff = column_sum(delta_conv)
    delta_taps = jnp.concatenate(
        [
            jnp.pad(delta_conv[1:], ((0, 1), (0, 0))),
            delta_conv,
            jnp.pad(delta_conv[:-1], ((1, 0), (0, 0))),
        ],
        axis=1,
    )
    taps_low, taps_high = delta_taps[:, :window_half], delta_taps[:, window_half:]
    one_sum = core_sum(place, joined, taps_low)
    two_sum = core_sum(place, joined, taps_high)
    one_pending = summed(place, (one_sum,), True)
    two_pending = summed(place, (two_sum,), True)
    delta_joined = right_product(taps_low, kernel_one) + right_product(taps_high, kernel_two)
    delta_joined = delta_joined * row_mask
    delta_tside = delta_joined[:, :model_width].astype(jnp.bfloat16)
    delta_lside = delta_joined[:, model_width:].astype(jnp.bfloat16)
    tmix_sum = core_sum(place, second_low, delta_tside)
    delta_toff = column_sum(delta_tside)
    lmix_sum = core_sum(place, pooled_low, delta_lside)
    delta_loff = column_sum(delta_lside)
    mixer_pending = summed(place, (tmix_sum, lmix_sum), False)
    delta_second = delta_three + right_product(delta_tside, full_tmix)
    delta_pooled = delta_four + right_product(delta_lside, full_lmix)

    inputs_ahead, inputs_behind, turned_ahead, turned_behind, sin_delta, shid_delta = (
        recurrent_backward(
            (gates_ahead, gates_behind),
            (prev_ahead, prev_behind),
            full_ghid,
            counts_column,
            delta_pooled,
        )
    )
    flat_rows = lambda v: v.reshape(letter_slots * seq_rows, -1)
    inputs_ahead, inputs_behind = flat_rows(inputs_ahead), flat_rows(inputs_behind)
    gin_sum = core_sum_of_pair(
        place, left_product(letter_flat, inputs_ahead), left_product(letter_flat, inputs_behind)
    )
    ghid_sum = core_sum_of_pair(
        place,
        left_product(flat_rows(prev_ahead), flat_rows(turned_ahead)),
        left_product(flat_rows(prev_behind), flat_rows(turned_behind)),
    )
    letters_delta = right_product(inputs_ahead, full_gin[:, :gates_width]) + right_product(
        inputs_behind, full_gin[:, gates_width:]
    )
    letters_grad = (
        letters_delta.astype(jnp.bfloat16)
        .reshape(letter_slots, seq_rows, model_width)
        .transpose(1, 0, 2)
    )
    sin_delta = sin_delta.reshape(2, -1)
    shid_delta = shid_delta.reshape(2, -1)
    in_pair = lambda v: jnp.stack([v[:, :gates_width], v[:, gates_width:]])
    ghid_pending = summed(place, (ghid_sum,), False)
    gin_pending = summed(place, (gin_sum,), True)
    delta_second = hold(delta_second, letters_delta)
    _, pull_two = jax.vjp(normalize, residual_two, gain_two, shift_two)
    delta_two, delta_gain_two, delta_shift_two = pull_two(delta_second)
    delta_lowered = delta_two.astype(jnp.bfloat16)
    down_sum = core_sum(place, activated, delta_lowered)
    down_pending = summed(place, (down_sum,), True)
    delta_dbias = column_sum(delta_lowered)
    delta_activated = right_product(delta_lowered, full_down)
    delta_upper = (delta_activated * slope_upper).astype(jnp.bfloat16)
    up_sum = core_sum(place, first_low, delta_upper)
    up_pending = summed(place, (up_sum,), False)
    delta_ubias = column_sum(delta_upper)
    delta_first = right_product(delta_upper, full_up)
    delta_first = delta_two + delta_first
    _, pull_one = jax.vjp(normalize, residual_one, gain_one, shift_one)
    delta_one, delta_gain_one, delta_shift_one = pull_one(delta_first)
    delta_attended = delta_one.astype(jnp.bfloat16)
    output_sum = core_sum(place, context, delta_attended)
    output_pending = summed(place, (output_sum,), False)
    delta_obias = column_sum(delta_attended)
    delta_context = right_product(delta_attended, full_output)
    delta_context = (
        delta_context
        .astype(jnp.bfloat16)
        .reshape(seq_rows, HEADS, head_width)
    )
    delta_values = jnp.einsum(
        "hqk,qhd->khd",
        probs_low,
        delta_context,
        preferred_element_type=jnp.float32,
    )
    delta_probs = jnp.einsum(
        "qhd,khd->hqk", delta_context, value_rows, preferred_element_type=jnp.float32
    )
    delta_scores = (
        probabilities * (delta_probs - jnp.sum(probabilities * delta_probs, axis=-1, keepdims=True))
    ).astype(jnp.bfloat16)
    delta_queries = jnp.einsum(
        "hqk,khd->qhd", delta_scores, key_rows, preferred_element_type=jnp.float32
    )
    delta_keys = jnp.einsum(
        "hqk,qhd->khd", delta_scores, queries, preferred_element_type=jnp.float32
    )
    delta_queries = delta_queries * score_scale
    delta_keys = delta_keys * score_scale
    delta_mixed = jnp.concatenate(
        [
            delta_queries.reshape(seq_rows, model_width),
            delta_keys.reshape(seq_rows, model_width),
            delta_values.reshape(seq_rows, model_width),
        ],
        axis=-1,
    ).astype(jnp.bfloat16)
    project_sum = core_sum(place, tokens, delta_mixed)
    project_pending = summed(place, (project_sum,), True)
    (ghid_grad,) = shared(place, ghid_pending, delta_context)
    (kernel_one_grad,) = shared(place, one_pending, delta_context)
    (kernel_two_grad,) = shared(place, two_pending, delta_context)
    (gin_grad,) = shared(place, gin_pending, delta_mixed)
    tmix_grad, lmix_grad = shared(place, mixer_pending, delta_context)
    (down_grad,) = shared(place, down_pending, delta_mixed)
    (up_grad,) = shared(place, up_pending, delta_mixed)
    (output_grad,) = shared(place, output_pending, delta_mixed)
    (project_grad,) = shared(place, project_pending)
    ghid_grad, gin_grad = in_pair(ghid_grad), in_pair(gin_grad)
    kernel_grad = jnp.concatenate([kernel_one_grad, kernel_two_grad], axis=1)
    delta_mixed_sum = column_sum(delta_mixed)
    delta_pbias = jnp.concatenate(
        [delta_mixed_sum[:model_width], delta_mixed_sum[2 * model_width :]]
    )
    tokens_grad = right_product(delta_mixed, full_project)
    tokens_grad = (delta_one + tokens_grad).astype(jnp.bfloat16)
    (
        pbias_grad,
        obias_grad,
        gain_one_grad,
        shift_one_grad,
        ubias_grad,
        dbias_grad,
        gain_two_grad,
        shift_two_grad,
        sin_grad,
        shid_grad,
        toff_grad,
        loff_grad,
        koff_grad,
        gain_three_grad,
        shift_three_grad,
        gain_four_grad,
        shift_four_grad,
    ) = owned_vectors(
        place,
        (
            delta_pbias,
            delta_obias,
            delta_gain_one,
            delta_shift_one,
            delta_ubias,
            delta_dbias,
            delta_gain_two,
            delta_shift_two,
            sin_delta,
            shid_delta,
            delta_toff,
            delta_loff,
            delta_koff,
            delta_gain_three,
            delta_shift_three,
            delta_gain_four,
            delta_shift_four,
        ),
    )
    taps_grad = jnp.stack(
        [kernel_grad[:, t * joined_width : (t + 1) * joined_width] for t in range(3)]
    )
    return (
        token_out.astype(jnp.bfloat16),
        letter_out.astype(jnp.bfloat16),
        tokens_grad,
        letters_grad,
        project_grad,
        pbias_grad,
        output_grad,
        obias_grad,
        gain_one_grad,
        shift_one_grad,
        up_grad,
        ubias_grad,
        down_grad,
        dbias_grad,
        gain_two_grad,
        shift_two_grad,
        gin_grad,
        ghid_grad,
        sin_grad,
        shid_grad,
        tmix_grad,
        toff_grad,
        lmix_grad,
        loff_grad,
        taps_grad,
        koff_grad,
        gain_three_grad,
        shift_three_grad,
        gain_four_grad,
        shift_four_grad,
    )


def solution(mesh):
    placed = (
        P(BOTH, None),
        P(BOTH, None, None),
        P(BOTH),
        P(BOTH),
        P(BOTH, None),
        P(BOTH, None),
        P(SHARD, None),
        P(SHARD),
        P(SHARD, None),
        P(SHARD),
        P(SHARD),
        P(SHARD),
        P(SHARD, None),
        P(SHARD),
        P(SHARD, None),
        P(SHARD),
        P(SHARD),
        P(SHARD),
        P(None, SHARD, None),
        P(None, SHARD, None),
        P(None, SHARD),
        P(None, SHARD),
        P(SHARD, None),
        P(SHARD),
        P(SHARD, None),
        P(SHARD),
        P(None, SHARD, None),
        P(SHARD),
        P(SHARD),
        P(SHARD),
        P(SHARD),
        P(SHARD),
    )
    return jax.shard_map(
        shards,
        mesh=mesh,
        in_specs=placed,
        out_specs=(
            P(BOTH, None),
            P(BOTH, None),
            P(BOTH, None),
            P(BOTH, None, None),
            P(SHARD, None),
            P(SHARD),
            P(SHARD, None),
            P(SHARD),
            P(SHARD),
            P(SHARD),
            P(SHARD, None),
            P(SHARD),
            P(SHARD, None),
            P(SHARD),
            P(SHARD),
            P(SHARD),
            P(None, SHARD, None),
            P(None, SHARD, None),
            P(None, SHARD),
            P(None, SHARD),
            P(SHARD, None),
            P(SHARD),
            P(SHARD, None),
            P(SHARD),
            P(None, SHARD, None),
            P(SHARD),
            P(SHARD),
            P(SHARD),
            P(SHARD),
            P(SHARD),
        ),
        check_vma=False,
    )
```
